128 devices in a mesh: gx: 8 (over x_hi, z), gy: 16 (over x_lo, y, core).
Axes of the slice: x: 4 (x_hi: 2, x_lo: 2; x = x_hi * 2 + x_lo), y: 4, z: 4, core: 2. Of those that a mesh axis runs over, the one named last changes fastest.
Arguments:
- positions: bfloat16 [64, 128, 3, 128], P('gx', 'gy'), may hold values from 0 to 1
- features: bfloat16 [64, 128, 256, 128], P('gx', 'gy'), may hold values from -6 to 6
- lever: float32 [64, 128, 3, 128], P('gx', 'gy'), may hold values from -4 to 4
- partner: int32 [64, 128, 6], P('gx', 'gy'), may hold values from 0 to 8, as said below
- body_slot: int32 [64, 128, 128], P('gx', 'gy'), may hold values from 0 to 127
- owner_dir: int32 [64, 128, 128], P('gx', 'gy'), may hold values from 0 to 8, as said below
- body_pose: float32 [8, 16, 7, 128], P('gx', 'gy'), as said below
- body_motion: float32 [8, 16, 6, 128], P('gx', 'gy'), may hold values from -5 to 5
- body_inverse: float32 [8, 16, 4, 128], P('gx', 'gy'), may hold values from 0.1 to 1
- weight_u: bfloat16 [512, 256], replicated, may hold values from -0.375 to 0.375
- weight_v: bfloat16 [128, 256], replicated, may hold values from -0.375 to 0.375
- radial_rate: float32 [4], replicated, may hold values from 0.5 to 4
Outputs:
- moved: float32 [64, 128, 3, 128], P('gx', 'gy')
- body_next: float32 [8, 16, 13, 128], P('gx', 'gy')
The draws below stay inside these ranges and needn't reach their ends.
Inputs may be any that keep to these rules, and one draw needn't show every extreme that they name: `partner`: each tile's 6 codes are distinct; code 3 (a + 1) + (b + 1) names the tile a tiles along the first and b along the second dimension, a, b in -1, 0, 1. `owner_dir`: code 3 (a + 1) + (b + 1) names the domain a, b domains away; a is -1 only in a domain's first row of 8 tiles and 1 only in its last, b likewise for its 8 columns. `body_pose`: rows 3 to 6 are unit quaternions with a positive first entry.
All inputs are finite; a program needn't handle non-finite values.
Results may differ from the reference program's by a relative error of at most 0.0023.
Values may be sent and summed in bfloat16 or wider, within the bound.
A program may use at most 128 MiB of HBM per device.

```python
import math
import jax
import jax.numpy as jnp
from jax import lax

F = 256
H = 128
K = 4
NB = 6
TILE = 128
BOD = 128
TX = 8
TY = 8
NXT = 64
NYT = 128
N_GX = 8
N_GY = 16


def draw_partner(key, part):
    scores = jax.random.randint(key, (NXT, NYT, 9), 0, 1048576) * 16 + jnp.arange(9, dtype=jnp.int32)
    order = jnp.argsort(scores, axis=-1)
    return order[:, :, :NB].astype(jnp.int32)


def draw_owner_dir(key, part):
    key_a, key_b = jax.random.split(key)
    coin_x = jax.random.randint(key_a, (NXT, NYT, TILE), 0, 4)
    coin_y = jax.random.randint(key_b, (NXT, NYT, TILE), 0, 4)
    local_x = (jnp.arange(NXT, dtype=jnp.int32) % TX)[:, None, None]
    local_y = (jnp.arange(NYT, dtype=jnp.int32) % TY)[None, :, None]
    step_x = jnp.where((local_x == 0) & (coin_x == 1), -1, jnp.where((local_x == TX - 1) & (coin_x == 2), 1, 0))
    step_y = jnp.where((local_y == 0) & (coin_y == 1), -1, jnp.where((local_y == TY - 1) & (coin_y == 2), 1, 0))
    return ((step_x + 1) * 3 + step_y + 1).astype(jnp.int32)


def draw_body_pose(key, part):
    key_c, key_w, key_v = jax.random.split(key, 3)
    centre = 1.5 * jax.random.normal(key_c, (N_GX, N_GY, 3, BOD))
    leading = jax.random.uniform(key_w, (N_GX, N_GY, 1, BOD), minval=0.5, maxval=1.0)
    others = 0.5 * jax.random.normal(key_v, (N_GX, N_GY, 3, BOD))
    quat = jnp.concatenate([leading, others], axis=2)
    quat = quat / jnp.sqrt(jnp.sum(quat * quat, axis=2, keepdims=True))
    return jnp.concatenate([centre, quat], axis=2).astype(jnp.float32)


def place_ends(values, key, smallest, high):
    dims = values.shape
    spot = [jax.random.randint(jax.random.fold_in(key, axis), (), 0, dims[axis]) for axis in range(len(dims))]
    values = values.at[tuple(spot)].set(smallest)
    longest = dims.index(max(dims))
    spot[longest] = (spot[longest] + 1) % dims[longest]
    return values.at[tuple(spot)].set(high)


def levels(own_key, extent, shards, low, top_value):
    def one(position, shards_of):
        steps = jax.random.uniform(jax.random.fold_in(jax.random.fold_in(own_key, 6), position), (shards_of,), jnp.float32, low / len(shards), top_value / len(shards))
        return jnp.repeat(jnp.exp(steps), extent[position] // shards_of).reshape((-1,) + (1,) * (len(extent) - position - 1))

    level = one(*shards[0])
    for cut in shards[1:]:
        level = level * one(*cut)
    return level


def normal_values(stream_key, dims, deviation, most, cuts=(), kind=jnp.bfloat16):
    level = levels(stream_key, dims, cuts, -0.22, 0.18) if cuts else 1.0
    values = jax.random.normal(stream_key, dims, jnp.float32) * deviation * level
    return jnp.minimum(jnp.maximum(values, -most), most).astype(kind)


def setup_inputs(seed: int = 0) -> dict:
    arg_keys = jax.random.split(jax.random.key(seed), 13)
    positions = jnp.clip(1.0 * jax.random.uniform(arg_keys[0], (NXT, NYT, 3, TILE), jnp.float32) ** levels(arg_keys[0], (NXT, NYT, 3, TILE), ((0, 8), (1, 16)), -0.2, 0.2), 0.0, 1.0).astype(jnp.bfloat16)
    features = normal_values(arg_keys[1], (NXT, NYT, F, TILE), 1.0, 6.0, ((0, 8), (1, 16)))
    lever = normal_values(arg_keys[2], (NXT, NYT, 3, TILE), 1.0, 4.0, ((0, 8), (1, 16)), jnp.float32)
    partner = draw_partner(jax.random.fold_in(arg_keys[12], 71), 0)
    body_slot = place_ends(jax.random.randint(arg_keys[4], (NXT, NYT, TILE), 0, BOD), jax.random.fold_in(arg_keys[4], 1), 0, BOD - 1).astype(jnp.int32)
    owner_dir = draw_owner_dir(jax.random.fold_in(arg_keys[12], 71), 0)
    body_pose = draw_body_pose(jax.random.fold_in(arg_keys[12], 71), 0)
    body_motion = normal_values(arg_keys[7], (N_GX, N_GY, 6, BOD), 1.0, 5.0, ((0, 8), (1, 16)), jnp.float32)
    body_inverse = jnp.clip(jnp.exp(math.log(1.0) - 2.3025851 * jax.random.uniform(arg_keys[8], (N_GX, N_GY, 4, BOD), jnp.float32) ** levels(arg_keys[8], (N_GX, N_GY, 4, BOD), ((0, 8), (1, 16)), -0.2, 0.2)), 0.1, 1.0)
    weight_u = normal_values(arg_keys[9], (K * H, F), F ** -0.5, 0.375)
    weight_v = normal_values(arg_keys[10], (H, F), F ** -0.5, 0.375)
    radial_rate = jnp.clip(jnp.exp(jax.random.uniform(arg_keys[11], (K,), jnp.float32, math.log(0.5), math.log(4.0))), 0.5, 4.0)
    return dict(positions=positions, features=features, lever=lever, partner=partner, body_slot=body_slot, owner_dir=owner_dir, body_pose=body_pose, body_motion=body_motion, body_inverse=body_inverse, weight_u=weight_u, weight_v=weight_v, radial_rate=radial_rate)


STEP_DT = 0.25
CUT_SQUARE = 4.0

def rotation(quat):
    qw, qa, qb, qc = (quat[0], quat[1], quat[2], quat[3])
    first = jnp.stack([1 - 2 * (qb * qb + qc * qc), 2 * (qa * qb - qw * qc), 2 * (qa * qc + qw * qb)])
    second = jnp.stack([2 * (qa * qb + qw * qc), 1 - 2 * (qa * qa + qc * qc), 2 * (qb * qc - qw * qa)])
    third = jnp.stack([2 * (qa * qc - qw * qb), 2 * (qb * qc + qw * qa), 1 - 2 * (qa * qa + qb * qb)])
    return jnp.stack([first, second, third])

def integrate(pose, motion, inverse, totals):
    centre = pose[0:3]
    quat = pose[3:7]
    new_vel = motion[0:3] + STEP_DT * inverse[0] * totals[0:3]
    new_centre = centre + STEP_DT * new_vel
    new_ang = motion[3:6] + STEP_DT * totals[3:6]
    rot_old = rotation(quat)
    body_frame = lax.optimization_barrier(jnp.sum(rot_old * new_ang[:, None], axis=0)) * inverse[1:4]
    omega = lax.optimization_barrier(jnp.sum(rot_old * body_frame[None, :], axis=1))
    scalar = -lax.optimization_barrier(jnp.sum(omega * quat[1:4], axis=0))
    vector = quat[0] * omega + jnp.cross(omega, quat[1:4], axis=0)
    stepped = quat + 0.5 * STEP_DT * jnp.concatenate([scalar[None], vector], axis=0)
    new_quat = stepped / jnp.sqrt(lax.optimization_barrier(jnp.sum(stepped * stepped, axis=0)))
    rot_new = rotation(new_quat)
    relative = lax.optimization_barrier(jnp.sum(rot_new[:, None, :] * rot_old[None, :, :], axis=2))
    next_state = jnp.concatenate([new_centre, new_quat, new_vel, new_ang], axis=0)
    packed = jnp.concatenate([STEP_DT * new_vel, relative.reshape((9,) + relative.shape[2:])], axis=0)
    return (next_state, packed)

def tile_forces(u_row, p_row, v_part, p_part, offset, radial_rate):
    differ = p_row[:, :, :, None] - p_part[:, :, None, :] - offset[:, :, None, None]
    radius_sq = lax.optimization_barrier(jnp.sum(differ * differ, axis=1))
    envelope = jnp.square(jnp.maximum(1.0 - radius_sq / CUT_SQUARE, 0.0))
    scores = jnp.einsum('mkha,mhb->mkab', u_row.astype(jnp.float32), v_part.astype(jnp.float32))
    radial = jnp.exp(-radial_rate[None, :, None, None] * radius_sq[:, None])
    couple = envelope * lax.optimization_barrier(jnp.sum(radial * scores, axis=1)) / v_part.shape[1]
    weight_sum = lax.optimization_barrier(jnp.sum(couple, axis=2))
    pulled = jnp.einsum('mab,mcb->mca', couple, p_part, precision=lax.Precision.HIGHEST)
    return (p_row - offset[:, :, None]) * weight_sum[:, None, :] - pulled

def reference(positions, features, lever, partner, body_slot, owner_dir, body_pose, body_motion, body_inverse, weight_u, weight_v, radial_rate):
    weight_uf = weight_u.astype(jnp.float32)
    weight_vf = weight_v.astype(jnp.float32)

    def project_row(feat_row):
        return jnp.einsum('hf,yfb->yhb', weight_vf, feat_row.astype(jnp.float32)).astype(jnp.bfloat16)
    proj_v = lax.map(project_row, features)
    flat_v = proj_v.reshape(NXT * NYT, H, TILE)
    flat_pos = positions.astype(jnp.float32).reshape(NXT * NYT, 3, TILE)
    col_index = jnp.arange(NYT, dtype=jnp.int32)

    def row_forces(inputs):
        row_index, feat_row, pos_row, codes = inputs
        u_row = jnp.einsum('gf,yfb->ygb', weight_uf, feat_row.astype(jnp.float32)).astype(jnp.bfloat16)
        u_row = u_row.reshape(NYT, K, H, TILE)
        p_row = pos_row.astype(jnp.float32)
        total = jnp.zeros((NYT, 3, TILE), jnp.float32)
        for which in range(NB):
            code = codes[:, which]
            off_x = code // 3 - 1
            off_y = code % 3 - 1
            global_index = (row_index + off_x) % NXT * NYT + (col_index + off_y) % NYT
            v_part = flat_v[global_index]
            p_part = flat_pos[global_index]
            offset = jnp.stack([off_x, off_y, jnp.zeros_like(off_x)], axis=1).astype(jnp.float32)
            total = total + tile_forces(u_row, p_row, v_part, p_part, offset, radial_rate)
        return total
    forces = lax.map(row_forces, (jnp.arange(NXT, dtype=jnp.int32), features, positions, partner))
    torque = jnp.cross(lever, forces, axis=2)
    terms = jnp.concatenate([forces, torque], axis=2)
    grid_x = jnp.arange(NXT, dtype=jnp.int32)[:, None, None]
    grid_y = jnp.arange(NYT, dtype=jnp.int32)[None, :, None]
    owner_x = (grid_x // TX + owner_dir // 3 - 1) % N_GX
    owner_y = (grid_y // TY + owner_dir % 3 - 1) % N_GY
    body_ids = (owner_x * N_GY + owner_y) * BOD + body_slot
    flat_terms = jnp.moveaxis(terms, 2, 3).reshape(-1, 6)
    sums = jax.ops.segment_sum(flat_terms, body_ids.reshape(-1), num_segments=N_GX * N_GY * BOD)
    sums = sums.reshape(N_GX, N_GY, BOD, 6)
    next_state, packed = integrate(jnp.moveaxis(body_pose, 2, 0), jnp.moveaxis(body_motion, 2, 0), jnp.moveaxis(body_inverse, 2, 0), jnp.moveaxis(sums, 3, 0))
    body_next = jnp.moveaxis(next_state, 0, 2)
    table = jnp.moveaxis(packed, 0, -1).reshape(-1, 12)
    looked = jnp.moveaxis(table[body_ids], 3, 2)
    rotated = jnp.stack([lax.optimization_barrier(jnp.sum(looked[:, :, 3 + 3 * row:6 + 3 * row] * lever, axis=2)) for row in range(3)], axis=2)
    moved = positions.astype(jnp.float32) + looked[:, :, 0:3] + rotated - lever
    return (moved, body_next)
```

```python
import jax
import jax.numpy as jnp
from jax import lax
from jax.experimental import pallas as pl
from jax.experimental.pallas import tpu as pltpu
from jax.sharding import PartitionSpec as P

STEP_DT = 0.25
LOG2E = 1.4426950408889634
MESH = pl.DeviceIdType.MESH
F32 = jnp.float32
BF16 = jnp.bfloat16
INNER_FIRST = 14
CODES = [c for c in range(9) if c != 4]
MIX = "DUUDUUDUUDUUDUU"


def mm(a, b):
    return jnp.dot(a, b, preferred_element_type=F32)


def mm_nt(a, b):
    return lax.dot_general(a, b, (((1,), (1,)), ((), ())), preferred_element_type=F32)


def split3(value):
    high = value.astype(BF16).astype(F32)
    rest = value - high
    mid = rest.astype(BF16).astype(F32)
    return high, mid, rest - mid


def inner_pair(q):
    i = 1 + q // 3
    j = 1 + 2 * (q % 3)
    return i, j, i, j + 1


def rim_pair(q):
    in_rows = q < 8
    c = q - 8
    i = jnp.where(in_rows, 7 * (q // 4), 1 + 2 * (c % 3))
    j = jnp.where(in_rows, 2 * (q % 4), 7 * (c // 3))
    return i, j, jnp.where(in_rows, i, i + 1), jnp.where(in_rows, j + 1, j)


def row_pair(q):
    i = 7 * (q // 4)
    j = 2 * (q % 4)
    return i, j, i, j + 1


def col_pair(q):
    i = 1 + 2 * (q % 3)
    j = 7 * (q // 3)
    return i, j, i + 1, j


def any_pair(p):
    rim = rim_pair(jnp.clip(p - INNER_FIRST, 0, 13))
    inner = inner_pair(jnp.clip(jnp.where(p < INNER_FIRST, p, p - 14), 0, 17))
    is_rim = (p >= INNER_FIRST) & (p < INNER_FIRST + 14)
    return tuple(jnp.where(is_rim, r, n) for r, n in zip(rim, inner))


def rotation_rows(qw, qa, qb, qc):
    return [
        [1 - 2 * (qb * qb + qc * qc), 2 * (qa * qb - qw * qc), 2 * (qa * qc + qw * qb)],
        [2 * (qa * qb + qw * qc), 1 - 2 * (qa * qa + qc * qc), 2 * (qb * qc - qw * qa)],
        [2 * (qa * qc - qw * qb), 2 * (qb * qc + qw * qa), 1 - 2 * (qa * qa + qb * qb)],
    ]


def kernel(
    codes,
    rates,
    positions,
    features,
    lever_in,
    slot_in,
    owner_in,
    pose_in,
    motion_in,
    inverse_in,
    wu_in,
    wv_in,
    moved,
    body_next,
    pos,
    feat,
    lever,
    slot,
    owner,
    pose,
    motion,
    inverse,
    wu,
    wv,
    vt,
    qf,
    qm,
    rp,
    u,
    oh,
    raw,
    terms,
    acc,
    part_out,
    part_in,
    table,
    table_f32,
    pos_row,
    pos_col,
    pos_corner,
    v_row,
    v_col,
    v_corner,
    s_even,
    s_odd,
    in_sem,
    pos_send,
    pos_recv,
    v_send,
    v_recv,
    part_send,
    part_recv,
    table_send,
    table_recv,
):
    gx, gy = lax.axis_index("gx"), lax.axis_index("gy")
    nx, ny = lax.axis_size("gx"), lax.axis_size("gy")

    def neighbour(code):
        a, b = code // 3 - 1, code % 3 - 1
        return (lax.rem(gx + a + nx, nx), lax.rem(gy + b + ny, ny))

    loads = []

    def load(src, dst):
        copy = pltpu.make_async_copy(src, dst, in_sem.at[len(loads)])
        copy.start()
        loads.append(copy)
        return copy

    got_pos = load(positions, pos)
    got_wv = load(wv_in, wv)
    rim_loads = [
        load(features.at[0], feat.at[0]),
        load(features.at[7], feat.at[7]),
        load(features.at[1:7, 0], feat.at[1:7, 0]),
        load(features.at[1:7, 7], feat.at[1:7, 7]),
    ]
    small_loads = [
        load(slot_in, slot),
        load(owner_in, owner),
        load(lever_in, lever),
        load(pose_in, pose),
        load(motion_in, motion),
        load(inverse_in, inverse),
        load(wu_in, wu),
    ]
    inner_loads = [load(features.at[i, 1:7], feat.at[i, 1:7]) for i in range(1, 7)]

    barrier = pltpu.get_barrier_semaphore()
    for code in CODES:
        pl.semaphore_signal(barrier, inc=1, device_id=neighbour(code), device_id_type=MESH)

    rate_scale = [rates[k] * (-LOG2E) for k in range(4)]
    lead = rate_scale[0]
    ratio = [None] + [rate_scale[k] / lead for k in range(1, 4)]
    four_lead = -4.0 * lead
    final_scale = 1.0 / (2048.0 * lead * lead)
    row8 = lax.broadcasted_iota(jnp.int32, (8, 128), 0)
    zero8 = jnp.zeros((8, 128), F32)

    raw[...] = jnp.zeros_like(raw)
    acc[...] = jnp.zeros_like(acc)
    table_f32[...] = jnp.zeros_like(table_f32)

    def clear(t, carry):
        qf[t] = jnp.zeros((128, 128), BF16)
        return carry

    lax.fori_loop(0, 100, clear, 0)

    got_pos.wait()
    pl.semaphore_wait(barrier, 8)

    def pos_src(a, b):
        if b == 0:
            return pos.at[0 if a < 0 else 7]
        if a == 0:
            return pos.at[:, 0 if b < 0 else 7]
        return pos.at[0 if a < 0 else 7, 0 if b < 0 else 7]

    def v_src(a, b):
        if b == 0:
            return vt.at[pl.ds(11 if a < 0 else 81, 8)]
        if a == 0:
            return None
        return vt.at[(10 if a < 0 else 80) + (1 if b < 0 else 8)]

    def landing(a, b, row_ref, col_ref, corner_ref):
        if b == 0:
            return row_ref.at[1 if a < 0 else 0]
        if a == 0:
            return col_ref.at[1 if b < 0 else 0]
        return corner_ref.at[(2 if a < 0 else 0) + (1 if b < 0 else 0)]

    pos_copies, v_copies = [], []
    for n, code in enumerate(CODES):
        a, b = code // 3 - 1, code % 3 - 1
        pos_copies.append(
            pltpu.make_async_remote_copy(
                src_ref=pos_src(a, b),
                dst_ref=landing(a, b, pos_row, pos_col, pos_corner),
                send_sem=pos_send.at[n],
                recv_sem=pos_recv.at[n],
                device_id=neighbour(code),
                device_id_type=MESH,
            )
        )
    for copy in pos_copies:
        copy.start()

    def pair_features(pair):
        ia, ja, ib, jb = pair
        return jnp.concatenate([feat[ia, ja], feat[ib, jb]], axis=1)

    def project_v(pair):
        ia, ja, ib, jb = pair
        v = mm(wv[...], pair_features(pair)).astype(BF16)
        vt[(ia + 1) * 10 + ja + 1] = v[:, 0:128].T
        vt[(ib + 1) * 10 + jb + 1] = v[:, 128:256].T

    def project_u(pair):
        ia, ja, ib, jb = pair
        both = mm(wu[...], pair_features(pair)).astype(BF16)
        u[ia * 8 + ja] = both[:, 0:128]
        u[ib * 8 + jb] = both[:, 128:256]

    got_wv.wait()
    for copy in rim_loads:
        copy.wait()

    def rim_rows_v(q, carry):
        project_v(row_pair(2 * q))
        project_v(row_pair(2 * q + 1))
        return carry

    def rim_cols_v(q, carry):
        for extra in range(3):
            pair = col_pair(3 * q + extra)
            ia, ja, ib, jb = pair
            project_v(pair)
        return carry

    lax.fori_loop(0, 4, rim_rows_v, 0)
    lax.fori_loop(0, 2, rim_cols_v, 0)

    vt4 = vt.reshape(10, 10, 128, 128)
    for n, code in enumerate(CODES):
        a, b = code // 3 - 1, code % 3 - 1
        src = vt4.at[1:9, 1 if b < 0 else 8] if a == 0 else v_src(a, b)
        v_copies.append(
            pltpu.make_async_remote_copy(
                src_ref=src,
                dst_ref=landing(a, b, v_row, v_col, v_corner),
                send_sem=v_send.at[n],
                recv_sem=v_recv.at[n],
                device_id=neighbour(code),
                device_id_type=MESH,
            )
        )
    for n in sorted(range(8), key=lambda n: (CODES[n] // 3 == 1, CODES[n])):
        v_copies[n].start()

    def partner_tables(index, x3, gi, gj):
        qx, qy, qz = x3[0:1], x3[1:2], x3[2:3]
        ax, ay = qx + gi, qy + gj
        b_high, b_mid, b_low = split3(lead * (ax * ax + ay * ay + qz * qz))
        g0 = jnp.where(row8 < 3, qx, jnp.where(row8 < 6, qy, qz))
        g1 = jnp.where(row8 == 0, qz, jnp.where(row8 < 4, gi, jnp.where(row8 < 7, gj, 0.0)))
        g2 = jnp.where(
            row8 == 0,
            b_high,
            jnp.where(
                row8 == 1,
                b_mid,
                jnp.where(row8 == 2, b_low, jnp.where(row8 < 6, 1.0, 0.0)),
            ),
        )
        stack = jnp.concatenate([g0, g1, g2, zero8], axis=0)
        qf[index, :, 0:32] = stack.T.astype(BF16)
        m0 = jnp.where(
            row8 == 0,
            qx,
            jnp.where(
                row8 == 1,
                qy,
                jnp.where(
                    row8 == 2,
                    qz,
                    jnp.where(
                        row8 == 3,
                        1.0,
                        jnp.where(row8 == 4, gi, jnp.where(row8 == 5, gj, 0.0)),
                    ),
                ),
            ),
        )
        qm[index] = jnp.concatenate([m0, zero8], axis=0).astype(BF16)

    def place(i):
        return i.astype(F32) - 3.5 if not isinstance(i, int) else float(i) - 3.5

    def pick3(first, parts):
        return jnp.where(row8 == first, parts[0], jnp.where(row8 == first + 1, parts[1], parts[2]))

    def own_tables(i, j):
        x3 = pos[i, j].astype(F32)
        gi, gj = place(i), place(j)
        partner_tables((i + 1) * 10 + j + 1, x3, gi, gj)
        ax, ay, az = x3[0:1] + gi, x3[1:2] + gj, x3[2:3]
        xs = split3(-2.0 * lead * ax)
        ys = split3(-2.0 * lead * ay)
        zs = split3(-2.0 * lead * az)
        sq = split3(lead * (ax * ax + ay * ay + az * az))
        g0 = jnp.where(
            row8 < 3,
            pick3(0, xs),
            jnp.where(row8 < 6, pick3(3, ys), jnp.where(row8 == 6, zs[0], zs[1])),
        )
        g1 = jnp.where(
            row8 == 0,
            zs[2],
            jnp.where(row8 < 4, pick3(1, xs), jnp.where(row8 < 7, pick3(4, ys), 0.0)),
        )
        g2 = jnp.where(row8 < 3, 1.0, jnp.where(row8 < 6, pick3(3, sq), 0.0))
        rp[i * 8 + j] = jnp.concatenate([g0, g1, g2, zero8], axis=0).astype(BF16)

    slots = lax.broadcasted_iota(jnp.int32, (128, 128), 0)

    def onehot(i, j):
        here = slot[i, pl.ds(j, 1), :]
        oh[i * 8 + j] = jnp.where(slots == here, 1.0, 0.0).astype(BF16)

    for copy in small_loads:
        copy.wait()

    def prepare(q, carry):
        i = q // 2
        for step in range(4):
            j = 4 * (q % 2) + step
            own_tables(i, j)
            onehot(i, j)
        return carry

    lax.fori_loop(0, 16, prepare, 0)
    for copy in inner_loads:
        copy.wait()

    def inner_v(q, carry):
        project_v(inner_pair(2 * q))
        project_v(inner_pair(2 * q + 1))
        return carry

    lax.fori_loop(0, 9, inner_v, 0)

    def all_u(q, carry):
        for step in range(2):
            p = 2 * q + step
            i, j = p // 4, 2 * (p % 4)
            project_u((i, j, i, j + 1))
        return carry

    lax.fori_loop(0, 16, all_u, 0)

    def partners(i, j):
        found = []
        for n in range(6):
            c = codes[i, j, n]
            found.append(i * 10 + j + c + 7 * ((c * 11) >> 5))
        return found

    zeros96 = jnp.zeros((96, 128), BF16)
    zeros128 = jnp.zeros((128, 128), BF16)

    def scores(p, s):
        ia, ja, ib, jb = any_pair(p)
        pa, pb = partners(ia, ja), partners(ib, jb)
        for x, (t, found) in enumerate(((ia * 8 + ja, pa), (ib * 8 + jb, pb))):
            rows = jnp.concatenate([vt[n] for n in found], axis=0)
            for half in range(2):
                first = u[t, 256 * half : 256 * half + 128, :]
                second = u[t, 256 * half + 128 : 256 * half + 256, :]
                s[2 * x + half] = mm(rows, jnp.concatenate([first, second], axis=1))
                yield
        rows = jnp.concatenate(
            [jnp.concatenate([qf[n], qf[m]], axis=1) for n, m in zip(pa, pb)], axis=0
        )
        right = jnp.concatenate(
            [
                jnp.concatenate([rp[ia * 8 + ja], zeros96, zeros128], axis=0),
                jnp.concatenate([zeros128, rp[ib * 8 + jb], zeros96], axis=0),
            ],
            axis=1,
        )
        s[4] = mm(rows, right)
        yield

    def couples(p, s):
        ia, ja, ib, jb = any_pair(p)
        pa, pb = partners(ia, ja), partners(ib, jb)
        for x, (t, found) in enumerate(((ia * 8 + ja, pa), (ib * 8 + jb, pb))):
            total = None
            for two in range(3):
                couple = []
                for n in (2 * two, 2 * two + 1):
                    rows = slice(n * 128, (n + 1) * 128)
                    t0 = s[4, rows, x * 128 : (x + 1) * 128]
                    mixed = None
                    for k in range(4):
                        score = s[2 * x + k // 2, rows, (k % 2) * 128 : (k % 2 + 1) * 128]
                        term = jnp.exp2(t0 if k == 0 else t0 * ratio[k]) * score
                        mixed = term if mixed is None else mixed + term
                    inside = jnp.maximum(t0 + four_lead, 0.0)
                    couple.append((mixed * (inside * inside)).astype(BF16))
                    yield
                left = jnp.concatenate([qm[found[2 * two]], qm[found[2 * two + 1]]], axis=1)
                got = mm(left, jnp.concatenate(couple, axis=0))
                total = got if total is None else total + got
            raw[pl.ds(pl.multiple_of(t * 8, 8), 8), :] = total[0:8]

    def run(steps):
        for _ in steps:
            pass

    def mixed_run(first, second):
        for which in MIX:
            next(first if which == "D" else second)
        run(first)
        run(second)

    def finish_halo():
        for copy in pos_copies:
            copy.wait_recv()
        for copy in v_copies:
            copy.wait_recv()

        def rows(q, carry):
            side, j = q // 8, q % 8
            index = 90 * side + j + 1
            vt[index] = v_row[side, j]
            partner_tables(index, pos_row[side, j].astype(F32), 9 * side.astype(F32) - 4.5, place(j))
            return carry

        def cols(q, carry):
            side, i = q // 8, q % 8
            index = (i + 1) * 10 + 9 * side
            vt[index] = v_col[side, i]
            partner_tables(index, pos_col[side, i].astype(F32), place(i), 9 * side.astype(F32) - 4.5)
            return carry

        def corners(q, carry):
            si, sj = q // 2, q % 2
            index = 90 * si + 9 * sj
            vt[index] = v_corner[q]
            partner_tables(
                index,
                pos_corner[q].astype(F32),
                9 * si.astype(F32) - 4.5,
                9 * sj.astype(F32) - 4.5,
            )
            return carry

        lax.fori_loop(0, 16, rows, 0)
        lax.fori_loop(0, 16, cols, 0)
        lax.fori_loop(0, 4, corners, 0)

    def force_terms():
        def row(i, carry):
            def strided(c):
                return raw[pl.ds(64 * i + c, 8, stride=8), :]

            weight = strided(3)
            ground = lax.broadcasted_iota(jnp.int32, (8, 128), 0).astype(F32) - 3.5
            px = pos[i, :, 0, :].astype(F32) + place(i)
            py = pos[i, :, 1, :].astype(F32) + ground
            pz = pos[i, :, 2, :].astype(F32)
            lx, ly, lz = lever[i, :, 0, :], lever[i, :, 1, :], lever[i, :, 2, :]
            fx = (px * weight - (strided(0) + strided(4))) * final_scale
            fy = (py * weight - (strided(1) + strided(5))) * final_scale
            fz = (pz * weight - strided(2)) * final_scale
            rows = [fx, fy, fz, ly * fz - lz * fy, lz * fx - lx * fz, lx * fy - ly * fx]
            for c, value in enumerate(rows + [jnp.zeros_like(fx)] * 2):
                terms[pl.ds(64 * i + c, 8, stride=8), :] = value
            return carry

        lax.fori_loop(0, 8, row, 0)

    def two_parts(t):
        value = terms[pl.ds(pl.multiple_of(t * 8, 8), 8), :]
        high = value.astype(BF16).astype(F32)
        return jnp.concatenate([high, value - high], axis=0)

    def pair_onehot(ta, tb):
        return jnp.concatenate([oh[ta], oh[tb]], axis=1)

    def masked_sums(pair, start, count):
        ia, ja, ib, jb = pair
        ta, tb = ia * 8 + ja, ib * 8 + jb
        value = jnp.concatenate([two_parts(ta), two_parts(tb)], axis=1)
        whose = jnp.concatenate([owner[ia, pl.ds(ja, 1), :], owner[ib, pl.ds(jb, 1), :]], axis=1)
        left = [jnp.where(whose == start + c, value, 0.0).astype(BF16) for c in range(count)]
        got = mm_nt(jnp.concatenate(left, axis=0), pair_onehot(ta, tb))
        where = pl.ds(pl.multiple_of(start * 16, 16), count * 16)
        acc[where, :] = acc[where, :] + got

    part_copies = []
    for n, code in enumerate(CODES):
        part_copies.append(
            pltpu.make_async_remote_copy(
                src_ref=part_out.at[code],
                dst_ref=part_in.at[code],
                send_sem=part_send.at[n],
                recv_sem=part_recv.at[n],
                device_id=neighbour(code),
                device_id_type=MESH,
            )
        )

    def send_parts():
        force_terms()

        def rows(q, carry):
            masked_sums(row_pair(q), 3 * (q // 4), 6)
            return carry

        def cols(q, carry):
            masked_sums(col_pair(q), 3 + q // 3, 2)
            return carry

        lax.fori_loop(0, 8, rows, 0)
        lax.fori_loop(0, 6, cols, 0)
        for code in CODES:
            part_out[code] = acc[16 * code : 16 * code + 8, :] + acc[16 * code + 8 : 16 * code + 16, :]
        for copy in part_copies:
            copy.start()

    run(scores(0, s_even))

    def two_pairs(q, carry):
        pl.when(q == INNER_FIRST // 2 - 1)(finish_halo)
        pl.when(q == INNER_FIRST // 2 + 7)(send_parts)
        mixed_run(scores(2 * q + 1, s_odd), couples(2 * q, s_even))
        mixed_run(scores(2 * q + 2, s_even), couples(2 * q + 1, s_odd))
        return carry

    lax.fori_loop(0, 15, two_pairs, 0)
    mixed_run(scores(31, s_odd), couples(30, s_even))
    run(couples(31, s_odd))

    force_terms()

    def inner_sums(q, total):
        for step in range(2):
            ia, ja, ib, jb = inner_pair(2 * q + step)
            ta, tb = ia * 8 + ja, ib * 8 + jb
            value = jnp.concatenate([two_parts(ta), two_parts(tb)], axis=1).astype(BF16)
            total = total + mm_nt(value, pair_onehot(ta, tb))
        return total

    own = lax.fori_loop(0, 9, inner_sums, acc[64:80, :])
    total = own[0:8] + own[8:16]
    for copy in part_copies:
        copy.wait_recv()
    for code in CODES:
        total = total + part_in[code]

    state = pose[0, 0]
    moving = motion[0, 0]
    inv = inverse[0, 0]
    centre = [state[c : c + 1] for c in range(3)]
    quat = [state[c : c + 1] for c in range(3, 7)]
    vel = [moving[c : c + 1] + STEP_DT * inv[0:1] * total[c : c + 1] for c in range(3)]
    ang = [moving[c : c + 1] + STEP_DT * total[c : c + 1] for c in range(3, 6)]
    shift = [STEP_DT * v for v in vel]
    rot = rotation_rows(*quat)
    frame = [
        (rot[0][c] * ang[0] + rot[1][c] * ang[1] + rot[2][c] * ang[2]) * inv[c + 1 : c + 2]
        for c in range(3)
    ]
    omega = [rot[r][0] * frame[0] + rot[r][1] * frame[1] + rot[r][2] * frame[2] for r in range(3)]
    qw, qv = quat[0], quat[1:4]
    change = [
        -(omega[0] * qv[0] + omega[1] * qv[1] + omega[2] * qv[2]),
        qw * omega[0] + (omega[1] * qv[2] - omega[2] * qv[1]),
        qw * omega[1] + (omega[2] * qv[0] - omega[0] * qv[2]),
        qw * omega[2] + (omega[0] * qv[1] - omega[1] * qv[0]),
    ]
    stepped = [q + 0.5 * STEP_DT * d for q, d in zip(quat, change)]
    norm = jnp.sqrt(sum(s * s for s in stepped[1:]) + stepped[0] * stepped[0])
    turned = [s / norm for s in stepped]
    rot_new = rotation_rows(*turned)
    for c in range(3):
        table_f32[c : c + 1, :] = shift[c]
        for r in range(3):
            entry = sum(rot_new[r][k] * rot[c][k] for k in range(3))
            table_f32[8 * (c + 1) + r : 8 * (c + 1) + r + 1, :] = entry
    whole = table_f32[...]
    high = whole.astype(BF16)
    table[256:288, :] = high
    table[288:320, :] = (whole - high.astype(F32)).astype(BF16)
    table_copies = []
    for n, code in enumerate(CODES):
        table_copies.append(
            pltpu.make_async_remote_copy(
                src_ref=table.at[pl.ds(256, 64)],
                dst_ref=table.at[pl.ds((8 - code) * 64, 64)],
                send_sem=table_send.at[n],
                recv_sem=table_recv.at[n],
                device_id=neighbour(code),
                device_id_type=MESH,
            )
        )
    for copy in table_copies:
        copy.start()
    next_rows = [c + s for c, s in zip(centre, shift)] + turned + vel + ang
    for c, value in enumerate(next_rows):
        body_next[0, 0, c : c + 1, :] = value

    def put(i, j, picked):
        x3 = pos[i, j].astype(F32)
        l3 = lever[i, j]
        moved[i, j] = (
            x3
            + picked[0:3]
            + picked[8:11] * l3[0:1]
            + picked[16:19] * l3[1:2]
            + picked[24:27] * l3[2:3]
            - l3
        )

    def move_pair(pair, start, count):
        ia, ja, ib, jb = pair
        ta, tb = ia * 8 + ja, ib * 8 + jb
        if count == 1:
            rows = table[256:320, :]
        else:
            rows = table[pl.ds(pl.multiple_of(start * 64, 64), count * 64), :]
        got = mm(rows, pair_onehot(ta, tb))
        whose = None
        if count > 1:
            whose = jnp.concatenate([owner[ia, pl.ds(ja, 1), :], owner[ib, pl.ds(jb, 1), :]], axis=1)
        picked = None
        for c in range(count):
            one = got[64 * c : 64 * c + 32] + got[64 * c + 32 : 64 * c + 64]
            picked = one if picked is None else jnp.where(whose == start + c, one, picked)
        put(ia, ja, picked[:, 0:128])
        put(ib, jb, picked[:, 128:256])

    def move_inner(q, carry):
        move_pair(inner_pair(2 * q), 4, 1)
        move_pair(inner_pair(2 * q + 1), 4, 1)
        return carry

    lax.fori_loop(0, 9, move_inner, 0)
    for copy in table_copies:
        copy.wait_recv()

    def move_rows(q, carry):
        move_pair(row_pair(q), 3 * (q // 4), 6)
        return carry

    def move_cols(q, carry):
        move_pair(col_pair(2 * q), 3 + (2 * q) // 3, 2)
        move_pair(col_pair(2 * q + 1), 3 + (2 * q + 1) // 3, 2)
        return carry

    lax.fori_loop(0, 8, move_rows, 0)
    lax.fori_loop(0, 3, move_cols, 0)
    for copy in pos_copies + v_copies + part_copies + table_copies:
        copy.wait_send()


def local(
    positions,
    features,
    lever,
    partner,
    body_slot,
    owner_dir,
    body_pose,
    body_motion,
    body_inverse,
    weight_u,
    weight_v,
    radial_rate,
):
    hbm = pl.BlockSpec(memory_space=pl.ANY)
    smem = pl.BlockSpec(memory_space=pltpu.SMEM)
    vmem = pl.BlockSpec(memory_space=pltpu.VMEM)
    dma = pltpu.SemaphoreType.DMA
    like = lambda x: pltpu.VMEM(x.shape, x.dtype)
    return pl.pallas_call(
        kernel,
        out_shape=(
            jax.ShapeDtypeStruct((8, 8, 3, 128), F32),
            jax.ShapeDtypeStruct((1, 1, 13, 128), F32),
        ),
        in_specs=[smem, smem] + [hbm] * 10,
        out_specs=(vmem, vmem),
        scratch_shapes=[
            like(positions),
            like(features),
            like(lever),
            like(body_slot),
            like(owner_dir),
            like(body_pose),
            like(body_motion),
            like(body_inverse),
            like(weight_u),
            like(weight_v),
            pltpu.VMEM((100, 128, 128), BF16),
            pltpu.VMEM((100, 128, 128), BF16),
            pltpu.VMEM((100, 16, 128), BF16),
            pltpu.VMEM((64, 32, 128), BF16),
            pltpu.VMEM((64, 512, 128), BF16),
            pltpu.VMEM((64, 128, 128), BF16),
            pltpu.VMEM((512, 128), F32),
            pltpu.VMEM((512, 128), F32),
            pltpu.VMEM((144, 128), F32),
            pltpu.VMEM((9, 8, 128), F32),
            pltpu.VMEM((9, 8, 128), F32),
            pltpu.VMEM((576, 128), BF16),
            pltpu.VMEM((32, 128), F32),
            pltpu.VMEM((2, 8, 3, 128), BF16),
            pltpu.VMEM((2, 8, 3, 128), BF16),
            pltpu.VMEM((4, 3, 128), BF16),
            pltpu.VMEM((2, 8, 128, 128), BF16),
            pltpu.VMEM((2, 8, 128, 128), BF16),
            pltpu.VMEM((4, 128, 128), BF16),
            pltpu.VMEM((5, 768, 256), F32),
            pltpu.VMEM((5, 768, 256), F32),
            dma((24,)),
            dma((8,)),
            dma((8,)),
            dma((8,)),
            dma((8,)),
            dma((8,)),
            dma((8,)),
            dma((8,)),
            dma((8,)),
        ],
        compiler_params=pltpu.CompilerParams(
            collective_id=0, has_side_effects=True, vmem_limit_bytes=60 * 1024 * 1024
        ),
        name="step",
    )(
        partner,
        radial_rate,
        positions,
        features,
        lever,
        body_slot,
        owner_dir,
        body_pose,
        body_motion,
        body_inverse,
        weight_u,
        weight_v,
    )


def solution(mesh):
    tiles = P("gx", "gy", None, None)
    flat = P("gx", "gy", None)
    return jax.shard_map(
        local,
        mesh=mesh,
        in_specs=(tiles, tiles, tiles, flat, flat, flat, tiles, tiles, tiles, P(), P(), P()),
        out_specs=(tiles, tiles),
        check_vma=False,
    )
```

```python
import jax
import jax.numpy as jnp
from jax import lax
from jax.experimental import pallas as pl
from jax.experimental.pallas import tpu as pltpu
from jax.sharding import PartitionSpec as P

STEP_DT = 0.25
LOG2E = 1.4426950408889634
MESH = pl.DeviceIdType.MESH
F32 = jnp.float32
BF16 = jnp.bfloat16
INNER_FIRST = 14
CODES = [c for c in range(9) if c != 4]
MIX = "DUUDUUDUUDUUDUU"


def mm(a, b):
    return jnp.dot(a, b, preferred_element_type=F32)


def mm_nt(a, b):
    return lax.dot_general(a, b, (((1,), (1,)), ((), ())), preferred_element_type=F32)


def split3(value):
    high = value.astype(BF16).astype(F32)
    rest = value - high
    mid = rest.astype(BF16).astype(F32)
    return high, mid, rest - mid


def inner_pair(q):
    i = 1 + q // 3
    j = 1 + 2 * (q % 3)
    return i, j, i, j + 1


def rim_pair(q):
    in_rows = q < 8
    c = q - 8
    i = jnp.where(in_rows, 7 * (q // 4), 1 + 2 * (c % 3))
    j = jnp.where(in_rows, 2 * (q % 4), 7 * (c // 3))
    return i, j, jnp.where(in_rows, i, i + 1), jnp.where(in_rows, j + 1, j)


def row_pair(q):
    i = 7 * (q // 4)
    j = 2 * (q % 4)
    return i, j, i, j + 1


def col_pair(q):
    i = 1 + 2 * (q % 3)
    j = 7 * (q // 3)
    return i, j, i + 1, j


def any_pair(p):
    rim = rim_pair(jnp.clip(p - INNER_FIRST, 0, 13))
    inner = inner_pair(jnp.clip(jnp.where(p < INNER_FIRST, p, p - 14), 0, 17))
    is_rim = (p >= INNER_FIRST) & (p < INNER_FIRST + 14)
    return tuple(jnp.where(is_rim, r, n) for r, n in zip(rim, inner))


def rotation_rows(qw, qa, qb, qc):
    return [
        [1 - 2 * (qb * qb + qc * qc), 2 * (qa * qb - qw * qc), 2 * (qa * qc + qw * qb)],
        [2 * (qa * qb + qw * qc), 1 - 2 * (qa * qa + qc * qc), 2 * (qb * qc - qw * qa)],
        [2 * (qa * qc - qw * qb), 2 * (qb * qc + qw * qa), 1 - 2 * (qa * qa + qb * qb)],
    ]


def kernel(
    codes,
    rates,
    positions,
    features,
    lever_in,
    slot_in,
    owner_in,
    pose_in,
    motion_in,
    inverse_in,
    wu_in,
    wv_in,
    moved,
    body_next,
    pos,
    feat,
    lever,
    slot,
    owner,
    pose,
    motion,
    inverse,
    wu,
    wv,
    vt,
    qf,
    qm,
    rp,
    u,
    oh,
    raw,
    terms,
    picked,
    acc,
    part_out,
    part_in,
    table,
    table_f32,
    pos32,
    stage_q,
    stage_r,
    stage_m,
    pos_row,
    pos_col,
    pos_corner,
    v_row,
    v_col,
    v_corner,
    s_even,
    s_odd,
    in_sem,
    pos_send,
    pos_recv,
    v_send,
    v_recv,
    part_send,
    part_recv,
    table_send,
    table_recv,
):
    gx, gy = lax.axis_index("gx"), lax.axis_index("gy")
    nx, ny = lax.axis_size("gx"), lax.axis_size("gy")

    def neighbour(code):
        a, b = code // 3 - 1, code % 3 - 1
        return (lax.rem(gx + a + nx, nx), lax.rem(gy + b + ny, ny))

    loads = []

    def load(src, dst):
        copy = pltpu.make_async_copy(src, dst, in_sem.at[len(loads)])
        copy.start()
        loads.append(copy)
        return copy

    got_pos = load(positions, pos)
    got_wv = load(wv_in, wv)
    rim_loads = [
        load(features.at[0], feat.at[0]),
        load(features.at[7], feat.at[7]),
        load(features.at[1:7, 0], feat.at[1:7, 0]),
        load(features.at[1:7, 7], feat.at[1:7, 7]),
    ]
    small_loads = [
        load(slot_in, slot),
        load(owner_in, owner),
        load(lever_in, lever),
        load(pose_in, pose),
        load(motion_in, motion),
        load(inverse_in, inverse),
        load(wu_in, wu),
    ]
    inner_loads = [load(features.at[i, 1:7], feat.at[i, 1:7]) for i in range(1, 7)]

    barrier = pltpu.get_barrier_semaphore()
    for code in CODES:
        pl.semaphore_signal(barrier, inc=1, device_id=neighbour(code), device_id_type=MESH)

    rate_scale = [rates[k] * (-LOG2E) for k in range(4)]
    lead = rate_scale[0]
    ratio = [None] + [rate_scale[k] / lead for k in range(1, 4)]
    four_lead = -4.0 * lead
    final_scale = 1.0 / (2048.0 * lead * lead)
    raw[...] = jnp.zeros_like(raw)
    acc[...] = jnp.zeros_like(acc)
    stage_q[...] = jnp.zeros_like(stage_q)
    stage_r[...] = jnp.zeros_like(stage_r)
    stage_m[...] = jnp.zeros_like(stage_m)
    table_f32[...] = jnp.zeros_like(table_f32)

    got_pos.wait()
    pos32[...] = pos[...].astype(F32)
    pl.semaphore_wait(barrier, 8)

    def v_src(a, b):
        if b == 0:
            return vt.at[pl.ds(11 if a < 0 else 81, 8)]
        if a == 0:
            return None
        return vt.at[(10 if a < 0 else 80) + (1 if b < 0 else 8)]

    def landing(a, b, row_ref, col_ref, corner_ref):
        if b == 0:
            return row_ref.at[1 if a < 0 else 0]
        if a == 0:
            return col_ref.at[1 if b < 0 else 0]
        return corner_ref.at[(2 if a < 0 else 0) + (1 if b < 0 else 0)]

    pos_copies, v_copies = [], []

    def send_pos(src, dst, code):
        n = len(pos_copies)
        copy = pltpu.make_async_remote_copy(
            src_ref=src,
            dst_ref=dst,
            send_sem=pos_send.at[n],
            recv_sem=pos_recv.at[n],
            device_id=neighbour(code),
            device_id_type=MESH,
        )
        copy.start()
        pos_copies.append(copy)

    for code in CODES:
        a, b = code // 3 - 1, code % 3 - 1
        i, j = (0 if a < 0 else 7), (0 if b < 0 else 7)
        if b == 0:
            send_pos(pos32.at[i], pos_row.at[1 if a < 0 else 0], code)
        elif a == 0:
            for c in range(3):
                send_pos(pos32.at[:, c, j], pos_col.at[1 if b < 0 else 0, c], code)
        else:
            k = (2 if a < 0 else 0) + (1 if b < 0 else 0)
            send_pos(pos32.at[i, :, j], pos_corner.at[:, k], code)

    lane = lax.broadcasted_iota(jnp.int32, (128, 128), 1)
    own_lanes = [jnp.where(lane // 32 == m, 1.0, 0.0).astype(BF16) for m in range(4)]
    zero8 = jnp.zeros((8, 128), F32)
    one8 = jnp.ones((8, 128), F32)
    steps8 = lax.broadcasted_iota(jnp.int32, (8, 128), 0).astype(F32) - 3.5

    def place(i):
        return jnp.full((8, 128), i.astype(F32) - 3.5)

    def put_rows(ref, stride, values):
        for r, value in enumerate(values):
            ref[pl.ds(r, 8, stride=stride), :] = value

    def partner_tables(q, gi, gj, indices):
        ax, ay = q[0] + gi, q[1] + gj
        square = split3(lead * (ax * ax + ay * ay + q[2] * q[2]))
        values = [q[0]] * 3 + [q[1]] * 3 + [q[2]] * 3 + [gi] * 3 + [gj] * 3
        put_rows(stage_q, 32, values + list(square) + [one8] * 3)
        put_rows(stage_m, 8, [q[0], q[1], q[2], one8, gi, gj])
        for half in range((len(indices) + 3) // 4):
            turned = stage_q[128 * half : 128 * half + 128, :].T.astype(BF16)
            for m, index in enumerate(indices[4 * half : 4 * half + 4]):
                qf[index] = turned * own_lanes[m]
        for m, index in enumerate(indices):
            rows = stage_m[8 * m : 8 * m + 8, :]
            qm[index] = jnp.concatenate([rows, zero8], axis=0).astype(BF16)

    slots = lax.broadcasted_iota(jnp.int32, (128, 128), 0)
    for copy in small_loads:
        copy.wait()

    def prepare(i, carry):
        q = [pos32[i, c] for c in range(3)]
        gi = place(i)
        partner_tables(q, gi, steps8, [(i + 1) * 10 + 1 + m for m in range(8)])
        ax, ay, az = q[0] + gi, q[1] + steps8, q[2]
        xs = list(split3(-2.0 * lead * ax))
        ys = list(split3(-2.0 * lead * ay))
        zs = list(split3(-2.0 * lead * az))
        sq = list(split3(lead * (ax * ax + ay * ay + az * az)))
        put_rows(stage_r, 32, xs + ys + zs + xs + ys + [one8] * 3 + sq)
        for m in range(8):
            rp[i * 8 + m] = stage_r[32 * m : 32 * m + 32, :].astype(BF16)
            here = slot[i, m : m + 1, :]
            oh[i * 8 + m] = jnp.where(slots == here, 1.0, 0.0).astype(BF16)
        return carry

    lax.fori_loop(0, 8, prepare, 0)

    def project(pair, want_v, want_u):
        ia, ja, ib, jb = pair
        both = jnp.concatenate([feat[ia, ja], feat[ib, jb]], axis=1)
        if want_v:
            v = mm(wv[...], both).astype(BF16)
            vt[(ia + 1) * 10 + ja + 1] = v[:, 0:128].T
            vt[(ib + 1) * 10 + jb + 1] = v[:, 128:256].T
        if want_u:
            all_u = mm(wu[...], both).astype(BF16)
            u[ia * 8 + ja] = all_u[:, 0:128]
            u[ib * 8 + jb] = all_u[:, 128:256]

    got_wv.wait()
    for copy in rim_loads:
        copy.wait()

    def rim_v(q, carry):
        project(rim_pair(2 * q), True, False)
        project(rim_pair(2 * q + 1), True, False)
        return carry

    lax.fori_loop(0, 7, rim_v, 0)

    vt4 = vt.reshape(10, 10, 128, 128)
    for n, code in enumerate(CODES):
        a, b = code // 3 - 1, code % 3 - 1
        src = vt4.at[1:9, 1 if b < 0 else 8] if a == 0 else v_src(a, b)
        v_copies.append(
            pltpu.make_async_remote_copy(
                src_ref=src,
                dst_ref=landing(a, b, v_row, v_col, v_corner),
                send_sem=v_send.at[n],
                recv_sem=v_recv.at[n],
                device_id=neighbour(code),
                device_id_type=MESH,
            )
        )
    for n in sorted(range(8), key=lambda n: (CODES[n] // 3 == 1, CODES[n])):
        v_copies[n].start()

    for copy in inner_loads:
        copy.wait()

    def inner_rows(q, carry):
        for step in range(3):
            project(inner_pair(3 * q + step), True, True)
        return carry

    def rim_u(q, carry):
        project(rim_pair(2 * q), False, True)
        project(rim_pair(2 * q + 1), False, True)
        return carry

    lax.fori_loop(0, 6, inner_rows, 0)
    lax.fori_loop(0, 7, rim_u, 0)

    def where_is(p):
        ia, ja, ib, jb = any_pair(p)
        found = [ia * 8 + ja, ib * 8 + jb]
        for i, j in ((ia, ja), (ib, jb)):
            for n in range(6):
                c = codes[n, i, j]
                found.append(i * 10 + j + c + 7 * ((c * 11) >> 5))
        return tuple(found)

    zeros128 = jnp.zeros((128, 128), BF16)

    def scores(at, s):
        for x in range(2):
            rows = jnp.concatenate([vt[n] for n in at[2 + 6 * x : 8 + 6 * x]], axis=0)
            for half in range(2):
                first = u[at[x], 256 * half : 256 * half + 128, :]
                second = u[at[x], 256 * half + 128 : 256 * half + 256, :]
                s[2 * x + half] = mm(rows, jnp.concatenate([first, second], axis=1))
                yield
        rows = jnp.concatenate(
            [jnp.concatenate([qf[n], qf[m]], axis=1) for n, m in zip(at[2:8], at[8:14])], axis=0
        )
        right = jnp.concatenate(
            [
                jnp.concatenate([rp[at[0]]] * 4 + [zeros128], axis=0),
                jnp.concatenate([zeros128] + [rp[at[1]]] * 4, axis=0),
            ],
            axis=1,
        )
        s[4] = mm(rows, right)
        yield

    def couples(at, s):
        for x in range(2):
            t, found = at[x], at[2 + 6 * x : 8 + 6 * x]
            total = None
            for two in range(3):
                couple = []
                for n in (2 * two, 2 * two + 1):
                    rows = slice(n * 128, (n + 1) * 128)
                    t0 = s[4, rows, x * 128 : (x + 1) * 128]
                    mixed = None
                    for k in range(4):
                        score = s[2 * x + k // 2, rows, (k % 2) * 128 : (k % 2 + 1) * 128]
                        term = jnp.exp2(t0 if k == 0 else t0 * ratio[k]) * score
                        mixed = term if mixed is None else mixed + term
                    inside = jnp.maximum(t0 + four_lead, 0.0)
                    couple.append((mixed * (inside * inside)).astype(BF16))
                    yield
                left = jnp.concatenate([qm[found[2 * two]], qm[found[2 * two + 1]]], axis=1)
                got = mm(left, jnp.concatenate(couple, axis=0))
                total = got if total is None else total + got
            raw[pl.ds(pl.multiple_of(t * 8, 8), 8), :] = total[0:8]

    def run(steps):
        for _ in steps:
            pass

    def mixed_run(first, second):
        for which in MIX:
            next(first if which == "D" else second)
        run(first)
        run(second)

    def finish_halo():
        for copy in pos_copies:
            copy.wait_recv()
        for copy in v_copies:
            copy.wait_recv()

        def rows(side, carry):
            edge = place(9 * side - 1)
            at = [90 * side + 1 + m for m in range(8)]
            for m in range(8):
                vt[at[m]] = v_row[side, m]
            partner_tables([pos_row[side, c] for c in range(3)], edge, steps8, at)
            return carry

        def cols(side, carry):
            edge = place(9 * side - 1)
            at = [(m + 1) * 10 + 9 * side for m in range(8)]
            for m in range(8):
                vt[at[m]] = v_col[side, m]
            partner_tables([pos_col[side, c] for c in range(3)], steps8, edge, at)
            return carry

        lax.fori_loop(0, 2, rows, 0)
        lax.fori_loop(0, 2, cols, 0)
        k = lax.broadcasted_iota(jnp.int32, (8, 128), 0)
        gi = jnp.where(k < 2, -4.5, 4.5)
        gj = jnp.where(k % 2 == 0, -4.5, 4.5)
        at = [0, 9, 90, 99]
        for m in range(4):
            vt[at[m]] = v_corner[m]
        partner_tables([pos_corner[c] for c in range(3)], gi, gj, at)

    def force_terms():
        def row(i, carry):
            def strided(c):
                return raw[pl.ds(64 * i + c, 8, stride=8), :]

            weight = strided(3)
            px, py, pz = pos32[i, 0] + place(i), pos32[i, 1] + steps8, pos32[i, 2]
            lx, ly, lz = lever[i, 0], lever[i, 1], lever[i, 2]
            fx = (px * weight - (strided(0) + strided(4))) * final_scale
            fy = (py * weight - (strided(1) + strided(5))) * final_scale
            fz = (pz * weight - strided(2)) * final_scale
            rows = [fx, fy, fz, ly * fz - lz * fy, lz * fx - lx * fz, lx * fy - ly * fx]
            put = rows + [zero8] * 2
            for c, value in enumerate(put):
                high = value.astype(BF16).astype(F32)
                terms[pl.ds(128 * i + c, 8, stride=16), :] = high
                terms[pl.ds(128 * i + 8 + c, 8, stride=16), :] = value - high
            return carry

        lax.fori_loop(0, 8, row, 0)

    def part_terms(t):
        return terms[pl.ds(pl.multiple_of(t * 16, 16), 16), :]

    def masked_sums(places, start, count):
        left, right = [], []
        for i, j in places:
            t = i * 8 + j
            value = part_terms(t)
            whose = owner[i, pl.ds(j, 1), :]
            masks = [jnp.where(whose == start + c, value, 0.0) for c in range(count)]
            left.append(jnp.concatenate(masks, axis=0).astype(BF16))
            right.append(oh[t])
        got = mm_nt(jnp.concatenate(left, axis=1), jnp.concatenate(right, axis=1))
        where = pl.ds(pl.multiple_of(start * 16, 16), count * 16)
        acc[where, :] = acc[where, :] + got

    part_copies = []
    for n, code in enumerate(CODES):
        part_copies.append(
            pltpu.make_async_remote_copy(
                src_ref=part_out.at[code],
                dst_ref=part_in.at[code],
                send_sem=part_send.at[n],
                recv_sem=part_recv.at[n],
                device_id=neighbour(code),
                device_id_type=MESH,
            )
        )

    def send_parts():
        force_terms()

        def rows(side, carry):
            masked_sums([(7 * side, m) for m in range(8)], 3 * side, 6)
            return carry

        def cols(side, carry):
            masked_sums([(m, 7 * side) for m in range(1, 7)], 3 + side, 2)
            return carry

        lax.fori_loop(0, 2, rows, 0)
        lax.fori_loop(0, 2, cols, 0)
        for code in CODES:
            part_out[code] = acc[16 * code : 16 * code + 8, :] + acc[16 * code + 8 : 16 * code + 16, :]
        for copy in part_copies:
            copy.start()

    first = where_is(jnp.int32(0))
    run(scores(first, s_even))

    def two_pairs(q, carry):
        now, after = carry[:14], carry[14:]
        pl.when(q == INNER_FIRST // 2 - 1)(finish_halo)
        pl.when(q == INNER_FIRST // 2 + 7)(send_parts)
        later = where_is(2 * q + 2)
        last = where_is(2 * q + 3)
        mixed_run(scores(after, s_odd), couples(now, s_even))
        mixed_run(scores(later, s_even), couples(after, s_odd))
        return later + last

    carry = lax.fori_loop(0, 15, two_pairs, first + where_is(jnp.int32(1)))
    now, after = carry[:14], carry[14:]
    mixed_run(scores(after, s_odd), couples(now, s_even))
    run(couples(after, s_odd))

    force_terms()

    def inner_sums(q, total):
        left, right = [], []
        for i in (2 * q + 1, 2 * q + 2):
            for j in range(1, 7):
                left.append(part_terms(i * 8 + j).astype(BF16))
                right.append(oh[i * 8 + j])
        return total + mm_nt(jnp.concatenate(left, axis=1), jnp.concatenate(right, axis=1))

    own = lax.fori_loop(0, 3, inner_sums, acc[64:80, :])
    total = own[0:8] + own[8:16]
    for copy in part_copies:
        copy.wait_recv()
    for code in CODES:
        total = total + part_in[code]

    inv = inverse[0, 0]
    centre = [pose[0, c] for c in range(3)]
    quat = [pose[0, c] for c in range(3, 7)]
    vel = [motion[0, c] + STEP_DT * inv[0:1] * total[c : c + 1] for c in range(3)]
    ang = [motion[0, c] + STEP_DT * total[c : c + 1] for c in range(3, 6)]
    shift = [STEP_DT * v for v in vel]
    rot = rotation_rows(*quat)
    frame = [
        (rot[0][c] * ang[0] + rot[1][c] * ang[1] + rot[2][c] * ang[2]) * inv[c + 1 : c + 2]
        for c in range(3)
    ]
    omega = [rot[r][0] * frame[0] + rot[r][1] * frame[1] + rot[r][2] * frame[2] for r in range(3)]
    qw, qv = quat[0], quat[1:4]
    change = [
        -(omega[0] * qv[0] + omega[1] * qv[1] + omega[2] * qv[2]),
        qw * omega[0] + (omega[1] * qv[2] - omega[2] * qv[1]),
        qw * omega[1] + (omega[2] * qv[0] - omega[0] * qv[2]),
        qw * omega[2] + (omega[0] * qv[1] - omega[1] * qv[0]),
    ]
    stepped = [q + 0.5 * STEP_DT * d for q, d in zip(quat, change)]
    norm = jnp.sqrt(sum(s * s for s in stepped[1:]) + stepped[0] * stepped[0])
    turned = [s / norm for s in stepped]
    rot_new = rotation_rows(*turned)
    for c in range(3):
        table_f32[c : c + 1, :] = shift[c]
        for r in range(3):
            entry = sum(rot_new[r][k] * rot[c][k] for k in range(3))
            table_f32[3 * (c + 1) + r : 3 * (c + 1) + r + 1, :] = entry
    whole = table_f32[...]
    high = whole.astype(BF16)
    table[128:144, :] = high
    table[144:160, :] = (whole - high.astype(F32)).astype(BF16)
    table_copies = []
    for n, code in enumerate(CODES):
        table_copies.append(
            pltpu.make_async_remote_copy(
                src_ref=table.at[pl.ds(128, 32)],
                dst_ref=table.at[pl.ds((8 - code) * 32, 32)],
                send_sem=table_send.at[n],
                recv_sem=table_recv.at[n],
                device_id=neighbour(code),
                device_id_type=MESH,
            )
        )
    for copy in table_copies:
        copy.start()
    next_rows = [c + s for c, s in zip(centre, shift)] + turned + vel + ang
    for c, value in enumerate(next_rows):
        body_next[0, c] = value

    def look_up(places, start, count):
        if count == 1:
            rows = table[128:160, :]
        else:
            rows = table[pl.ds(pl.multiple_of(start * 32, 32), count * 32), :]
        tiles = [i * 8 + j for i, j in places]
        got = mm(rows, jnp.concatenate([oh[t] for t in tiles], axis=1))
        for n, (i, j) in enumerate(places):
            lanes = slice(128 * n, 128 * n + 128)
            found = None
            for c in range(count):
                one = got[32 * c : 32 * c + 16, lanes] + got[32 * c + 16 : 32 * c + 32, lanes]
                if c:
                    whose = owner[i, pl.ds(j, 1), :]
                    found = jnp.where(whose == start + c, one, found)
                else:
                    found = one
            picked[pl.ds(pl.multiple_of(tiles[n] * 16, 16), 16), :] = found

    def look_inner(i, carry):
        look_up([(i, j) for j in range(1, 7)], 4, 1)
        return carry

    lax.fori_loop(1, 7, look_inner, 0)
    for copy in table_copies:
        copy.wait_recv()

    def look_rows(q, carry):
        i, start = 7 * (q // 2), 3 * (q // 2)
        look_up([(i, 4 * (q % 2) + m) for m in range(4)], start, 6)
        return carry

    def look_cols(side, carry):
        look_up([(i, 7 * side) for i in range(1, 7)], 3 + side, 2)
        return carry

    lax.fori_loop(0, 4, look_rows, 0)
    lax.fori_loop(0, 2, look_cols, 0)

    def move(i, carry):
        def strided(c):
            return picked[pl.ds(128 * i + c, 8, stride=16), :]

        levers = [lever[i, c] for c in range(3)]
        for r in range(3):
            value = pos32[i, r] + strided(r)
            for c in range(3):
                value = value + strided(3 + 3 * c + r) * levers[c]
            moved[i, r] = value - levers[r]
        return carry

    lax.fori_loop(0, 8, move, 0)
    for copy in pos_copies + v_copies + part_copies + table_copies:
        copy.wait_send()


def local(
    positions,
    features,
    lever,
    partner,
    body_slot,
    owner_dir,
    body_pose,
    body_motion,
    body_inverse,
    weight_u,
    weight_v,
    radial_rate,
):
    hbm = pl.BlockSpec(memory_space=pl.ANY)
    smem = pl.BlockSpec(memory_space=pltpu.SMEM)
    vmem = pl.BlockSpec(memory_space=pltpu.VMEM)
    dma = pltpu.SemaphoreType.DMA
    like = lambda x: pltpu.VMEM(x.shape, x.dtype)
    inside = lambda x: jnp.transpose(x, (0, 2, 1, 3))
    positions, lever = inside(positions), inside(lever)
    body_pose, body_motion = inside(body_pose), inside(body_motion)
    partner = jnp.transpose(partner, (2, 0, 1))
    moved, body_next = pl.pallas_call(
        kernel,
        out_shape=(
            jax.ShapeDtypeStruct((8, 3, 8, 128), F32),
            jax.ShapeDtypeStruct((1, 13, 1, 128), F32),
        ),
        in_specs=[smem, smem] + [hbm] * 10,
        out_specs=(vmem, vmem),
        scratch_shapes=[
            like(positions),
            like(features),
            like(lever),
            like(body_slot),
            like(owner_dir),
            like(body_pose),
            like(body_motion),
            like(body_inverse),
            like(weight_u),
            like(weight_v),
            pltpu.VMEM((100, 128, 128), BF16),
            pltpu.VMEM((100, 128, 128), BF16),
            pltpu.VMEM((100, 16, 128), BF16),
            pltpu.VMEM((64, 32, 128), BF16),
            pltpu.VMEM((64, 512, 128), BF16),
            pltpu.VMEM((64, 128, 128), BF16),
            pltpu.VMEM((512, 128), F32),
            pltpu.VMEM((1024, 128), F32),
            pltpu.VMEM((1024, 128), F32),
            pltpu.VMEM((144, 128), F32),
            pltpu.VMEM((9, 8, 128), F32),
            pltpu.VMEM((9, 8, 128), F32),
            pltpu.VMEM((288, 128), BF16),
            pltpu.VMEM((16, 128), F32),
            pltpu.VMEM((8, 3, 8, 128), F32),
            pltpu.VMEM((256, 128), F32),
            pltpu.VMEM((256, 128), F32),
            pltpu.VMEM((64, 128), F32),
            pltpu.VMEM((2, 3, 8, 128), F32),
            pltpu.VMEM((2, 3, 8, 128), F32),
            pltpu.VMEM((3, 8, 128), F32),
            pltpu.VMEM((2, 8, 128, 128), BF16),
            pltpu.VMEM((2, 8, 128, 128), BF16),
            pltpu.VMEM((4, 128, 128), BF16),
            pltpu.VMEM((5, 768, 256), F32),
            pltpu.VMEM((5, 768, 256), F32),
            dma((24,)),
            dma((12,)),
            dma((12,)),
            dma((8,)),
            dma((8,)),
            dma((8,)),
            dma((8,)),
            dma((8,)),
            dma((8,)),
        ],
        compiler_params=pltpu.CompilerParams(
            collective_id=0, has_side_effects=True, vmem_limit_bytes=60 * 1024 * 1024
        ),
        name="step",
    )(
        partner,
        radial_rate,
        positions,
        features,
        lever,
        body_slot,
        owner_dir,
        body_pose,
        body_motion,
        body_inverse,
        weight_u,
        weight_v,
    )
    return inside(moved), inside(body_next)


def solution(mesh):
    tiles = P("gx", "gy", None, None)
    flat = P("gx", "gy", None)
    return jax.shard_map(
        local,
        mesh=mesh,
        in_specs=(tiles, tiles, tiles, flat, flat, flat, tiles, tiles, tiles, P(), P(), P()),
        out_specs=(tiles, tiles),
        check_vma=False,
    )
```

```python
import jax
import jax.numpy as jnp
from jax import lax
from jax.experimental import pallas as pl
from jax.experimental.pallas import tpu as pltpu
from jax.sharding import PartitionSpec as P

STEP_DT = 0.25
LOG2E = 1.4426950408889634
MESH = pl.DeviceIdType.MESH
F32 = jnp.float32
BF16 = jnp.bfloat16
INNER_FIRST = 14
CODES = [c for c in range(9) if c != 4]
MIX = "DUUDUUDUUDUUDUU"
DOTS = (0, 1, 4, 2, 3)


def mm(a, b):
    return jnp.dot(a, b, preferred_element_type=F32)


def mm_nt(a, b):
    return lax.dot_general(a, b, (((1,), (1,)), ((), ())), preferred_element_type=F32)


def split3(value):
    high = value.astype(BF16).astype(F32)
    rest = value - high
    mid = rest.astype(BF16).astype(F32)
    return high, mid, rest - mid


def inner_pair(q):
    i = 1 + q // 3
    j = 1 + 2 * (q % 3)
    return i, j, i, j + 1


def rim_pair(q):
    in_rows = q < 8
    c = q - 8
    i = jnp.where(in_rows, 7 * (q // 4), 1 + 2 * (c % 3))
    j = jnp.where(in_rows, 2 * (q % 4), 7 * (c // 3))
    return i, j, jnp.where(in_rows, i, i + 1), jnp.where(in_rows, j + 1, j)


def row_pair(q):
    i = 7 * (q // 4)
    j = 2 * (q % 4)
    return i, j, i, j + 1


def col_pair(q):
    i = 1 + 2 * (q % 3)
    j = 7 * (q // 3)
    return i, j, i + 1, j


def any_pair(p):
    rim = rim_pair(jnp.clip(p - INNER_FIRST, 0, 13))
    inner = inner_pair(jnp.clip(jnp.where(p < INNER_FIRST, p, p - 14), 0, 17))
    is_rim = (p >= INNER_FIRST) & (p < INNER_FIRST + 14)
    return tuple(jnp.where(is_rim, r, n) for r, n in zip(rim, inner))


def rotation_rows(qw, qa, qb, qc):
    return [
        [1 - 2 * (qb * qb + qc * qc), 2 * (qa * qb - qw * qc), 2 * (qa * qc + qw * qb)],
        [2 * (qa * qb + qw * qc), 1 - 2 * (qa * qa + qc * qc), 2 * (qb * qc - qw * qa)],
        [2 * (qa * qc - qw * qb), 2 * (qb * qc + qw * qa), 1 - 2 * (qa * qa + qb * qb)],
    ]


def kernel(
    codes,
    rates,
    positions,
    features,
    lever_in,
    slot_in,
    owner_in,
    pose_in,
    motion_in,
    inverse_in,
    wu_in,
    wv_in,
    moved,
    body_next,
    pos,
    feat,
    lever,
    slot,
    owner,
    pose,
    motion,
    inverse,
    wu,
    wv,
    vt,
    qf,
    qm,
    rp,
    u,
    oh,
    raw,
    terms,
    picked,
    acc,
    part_out,
    part_in,
    table,
    table_f32,
    pos32,
    stage_q,
    stage_r,
    stage_m,
    pos_row,
    pos_col,
    pos_corner,
    v_row,
    v_col,
    v_corner,
    s_even,
    s_odd,
    in_sem,
    pos_send,
    pos_recv,
    v_send,
    v_recv,
    part_send,
    part_recv,
    table_send,
    table_recv,
):
    gx, gy = lax.axis_index("gx"), lax.axis_index("gy")
    nx, ny = lax.axis_size("gx"), lax.axis_size("gy")

    def neighbour(code):
        a, b = code // 3 - 1, code % 3 - 1
        return (lax.rem(gx + a + nx, nx), lax.rem(gy + b + ny, ny))

    loads = []

    def load(src, dst):
        copy = pltpu.make_async_copy(src, dst, in_sem.at[len(loads)])
        copy.start()
        loads.append(copy)
        return copy

    got_pos = load(positions, pos)
    got_wv = load(wv_in, wv)
    rim_loads = [
        load(features.at[0], feat.at[0]),
        load(features.at[7], feat.at[7]),
        load(features.at[1:7, 0], feat.at[1:7, 0]),
        load(features.at[1:7, 7], feat.at[1:7, 7]),
    ]
    small_loads = [
        load(slot_in, slot),
        load(owner_in, owner),
        load(lever_in, lever),
        load(pose_in, pose),
        load(motion_in, motion),
        load(inverse_in, inverse),
        load(wu_in, wu),
    ]
    inner_loads = [load(features.at[i, 1:7], feat.at[i, 1:7]) for i in range(1, 7)]

    barrier = pltpu.get_barrier_semaphore()
    for code in CODES:
        pl.semaphore_signal(barrier, inc=1, device_id=neighbour(code), device_id_type=MESH)

    rate_scale = [rates[k] * (-LOG2E) for k in range(4)]
    lead = rate_scale[0]
    ratio = [None] + [rate_scale[k] / lead for k in range(1, 4)]
    four_lead = -4.0 * lead
    final_scale = 1.0 / (2048.0 * lead * lead)
    raw[...] = jnp.zeros_like(raw)
    acc[...] = jnp.zeros_like(acc)
    stage_q[...] = jnp.zeros_like(stage_q)
    stage_r[...] = jnp.zeros_like(stage_r)
    stage_m[...] = jnp.zeros_like(stage_m)
    table_f32[...] = jnp.zeros_like(table_f32)

    got_pos.wait()
    pos32[...] = pos[...].astype(F32)

    def v_src(a, b):
        if b == 0:
            return vt.at[pl.ds(11 if a < 0 else 81, 8)]
        if a == 0:
            return None
        return vt.at[(10 if a < 0 else 80) + (1 if b < 0 else 8)]

    def landing(a, b, row_ref, col_ref, corner_ref):
        if b == 0:
            return row_ref.at[1 if a < 0 else 0]
        if a == 0:
            return col_ref.at[1 if b < 0 else 0]
        return corner_ref.at[(2 if a < 0 else 0) + (1 if b < 0 else 0)]

    lane = lax.broadcasted_iota(jnp.int32, (128, 128), 1)
    own_lanes = [jnp.where(lane // 32 == m, 1.0, 0.0).astype(BF16) for m in range(4)]
    zero8 = jnp.zeros((8, 128), F32)
    one8 = jnp.ones((8, 128), F32)
    steps8 = lax.broadcasted_iota(jnp.int32, (8, 128), 0).astype(F32) - 3.5

    def place(i):
        return jnp.full((8, 128), i.astype(F32) - 3.5)

    def put_rows(ref, stride, values):
        for r, value in enumerate(values):
            ref[pl.ds(r, 8, stride=stride), :] = value

    def partner_tables(q, gi, gj, indices):
        ax, ay = q[0] + gi, q[1] + gj
        square = split3(lead * (ax * ax + ay * ay + q[2] * q[2]))
        values = [q[0]] * 3 + [q[1]] * 3 + [q[2]] * 3 + [gi] * 3 + [gj] * 3
        put_rows(stage_q, 32, values + list(square) + [one8] * 3)
        put_rows(stage_m, 8, [q[0], q[1], q[2], one8, gi, gj])
        for half in range((len(indices) + 3) // 4):
            turned = stage_q[128 * half : 128 * half + 128, :].T.astype(BF16)
            for m, index in enumerate(indices[4 * half : 4 * half + 4]):
                qf[index] = turned * own_lanes[m]
        for m, index in enumerate(indices):
            rows = stage_m[8 * m : 8 * m + 8, :]
            qm[index] = jnp.concatenate([rows, zero8], axis=0).astype(BF16)

    slots = lax.broadcasted_iota(jnp.int32, (128, 128), 0)
    for copy in small_loads:
        copy.wait()

    def prepare(i, carry):
        q = [pos32[i, c] for c in range(3)]
        gi = place(i)
        partner_tables(q, gi, steps8, [(i + 1) * 10 + 1 + m for m in range(8)])
        ax, ay, az = q[0] + gi, q[1] + steps8, q[2]
        xs = list(split3(-2.0 * lead * ax))
        ys = list(split3(-2.0 * lead * ay))
        zs = list(split3(-2.0 * lead * az))
        sq = list(split3(lead * (ax * ax + ay * ay + az * az)))
        put_rows(stage_r, 32, xs + ys + zs + xs + ys + [one8] * 3 + sq)
        for m in range(8):
            rp[i * 8 + m] = stage_r[32 * m : 32 * m + 32, :].astype(BF16)
            here = slot[i, m : m + 1, :]
            oh[i * 8 + m] = jnp.where(slots == here, 1.0, 0.0).astype(BF16)
        return carry

    lax.fori_loop(0, 8, prepare, 0)

    def project(pair, want_v, want_u):
        ia, ja, ib, jb = pair
        both = jnp.concatenate([feat[ia, ja], feat[ib, jb]], axis=1)
        if want_v:
            v = mm(wv[...], both).astype(BF16)
            vt[(ia + 1) * 10 + ja + 1] = v[:, 0:128].T
            vt[(ib + 1) * 10 + jb + 1] = v[:, 128:256].T
        if want_u:
            all_u = mm(wu[...], both).astype(BF16)
            u[ia * 8 + ja] = all_u[:, 0:128]
            u[ib * 8 + jb] = all_u[:, 128:256]

    got_wv.wait()
    for copy in rim_loads:
        copy.wait()

    def rim_v(q, carry):
        project(rim_pair(2 * q), True, False)
        project(rim_pair(2 * q + 1), True, False)
        return carry

    lax.fori_loop(0, 7, rim_v, 0)

    pl.semaphore_wait(barrier, 8)
    pos_copies, v_copies = [], []

    def send_pos(src, dst, code):
        n = len(pos_copies)
        copy = pltpu.make_async_remote_copy(
            src_ref=src,
            dst_ref=dst,
            send_sem=pos_send.at[n],
            recv_sem=pos_recv.at[n],
            device_id=neighbour(code),
            device_id_type=MESH,
        )
        copy.start()
        pos_copies.append(copy)

    for code in CODES:
        a, b = code // 3 - 1, code % 3 - 1
        i, j = (0 if a < 0 else 7), (0 if b < 0 else 7)
        if b == 0:
            send_pos(pos32.at[i], pos_row.at[1 if a < 0 else 0], code)
        elif a == 0:
            for c in range(3):
                send_pos(pos32.at[:, c, j], pos_col.at[1 if b < 0 else 0, c], code)
        else:
            k = (2 if a < 0 else 0) + (1 if b < 0 else 0)
            send_pos(pos32.at[i, :, j], pos_corner.at[:, k], code)

    vt4 = vt.reshape(10, 10, 128, 128)
    for n, code in enumerate(CODES):
        a, b = code // 3 - 1, code % 3 - 1
        src = vt4.at[1:9, 1 if b < 0 else 8] if a == 0 else v_src(a, b)
        v_copies.append(
            pltpu.make_async_remote_copy(
                src_ref=src,
                dst_ref=landing(a, b, v_row, v_col, v_corner),
                send_sem=v_send.at[n],
                recv_sem=v_recv.at[n],
                device_id=neighbour(code),
                device_id_type=MESH,
            )
        )
    for n in sorted(range(8), key=lambda n: (CODES[n] // 3 == 1, CODES[n])):
        v_copies[n].start()

    for copy in inner_loads:
        copy.wait()

    def inner_rows(q, carry):
        for step in range(3):
            project(inner_pair(3 * q + step), True, True)
        return carry

    def rim_u(q, carry):
        project(rim_pair(2 * q), False, True)
        project(rim_pair(2 * q + 1), False, True)
        return carry

    lax.fori_loop(0, 6, inner_rows, 0)
    lax.fori_loop(0, 7, rim_u, 0)

    def where_is(p):
        ia, ja, ib, jb = any_pair(p)
        found = [ia * 8 + ja, ib * 8 + jb]
        for i, j in ((ia, ja), (ib, jb)):
            for n in range(6):
                c = codes[n, i, j]
                found.append(i * 10 + j + c + 7 * ((c * 11) >> 5))
        return tuple(found)

    zeros128 = jnp.zeros((128, 128), BF16)

    def scores(at, s):
        for which in DOTS:
            if which == 4:
                rows = [jnp.concatenate([qf[n], qf[m]], axis=1) for n, m in zip(at[2:8], at[8:14])]
                right = jnp.concatenate(
                    [
                        jnp.concatenate([rp[at[0]]] * 4 + [zeros128], axis=0),
                        jnp.concatenate([zeros128] + [rp[at[1]]] * 4, axis=0),
                    ],
                    axis=1,
                )
            else:
                x, half = which // 2, which % 2
                rows = [vt[n] for n in at[2 + 6 * x : 8 + 6 * x]]
                first = u[at[x], 256 * half : 256 * half + 128, :]
                second = u[at[x], 256 * half + 128 : 256 * half + 256, :]
                right = jnp.concatenate([first, second], axis=1)
            s[which] = mm(jnp.concatenate(rows, axis=0), right)
            yield

    def couples(at, s):
        for x in range(2):
            t, found = at[x], at[2 + 6 * x : 8 + 6 * x]
            total = None
            for two in range(3):
                couple = []
                for n in (2 * two, 2 * two + 1):
                    rows = slice(n * 128, (n + 1) * 128)
                    t0 = s[4, rows, x * 128 : (x + 1) * 128]
                    mixed = None
                    for k in range(4):
                        score = s[2 * x + k // 2, rows, (k % 2) * 128 : (k % 2 + 1) * 128]
                        term = jnp.exp2(t0 if k == 0 else t0 * ratio[k]) * score
                        mixed = term if mixed is None else mixed + term
                    inside = jnp.maximum(t0 + four_lead, 0.0)
                    couple.append((mixed * (inside * inside)).astype(BF16))
                    yield
                left = jnp.concatenate([qm[found[2 * two]], qm[found[2 * two + 1]]], axis=1)
                got = mm(left, jnp.concatenate(couple, axis=0))
                total = got if total is None else total + got
            raw[pl.ds(pl.multiple_of(t * 8, 8), 8), :] = total[0:8]

    def run(steps):
        for _ in steps:
            pass

    def mixed_run(first, second):
        for which in MIX:
            next(first if which == "D" else second)
        run(first)
        run(second)

    def finish_halo():
        for copy in pos_copies:
            copy.wait_recv()
        for copy in v_copies:
            copy.wait_recv()

        def rows(side, carry):
            edge = place(9 * side - 1)
            at = [90 * side + 1 + m for m in range(8)]
            for m in range(8):
                vt[at[m]] = v_row[side, m]
            partner_tables([pos_row[side, c] for c in range(3)], edge, steps8, at)
            return carry

        def cols(side, carry):
            edge = place(9 * side - 1)
            at = [(m + 1) * 10 + 9 * side for m in range(8)]
            for m in range(8):
                vt[at[m]] = v_col[side, m]
            partner_tables([pos_col[side, c] for c in range(3)], steps8, edge, at)
            return carry

        lax.fori_loop(0, 2, rows, 0)
        lax.fori_loop(0, 2, cols, 0)
        k = lax.broadcasted_iota(jnp.int32, (8, 128), 0)
        gi = jnp.where(k < 2, -4.5, 4.5)
        gj = jnp.where(k % 2 == 0, -4.5, 4.5)
        at = [0, 9, 90, 99]
        for m in range(4):
            vt[at[m]] = v_corner[m]
        partner_tables([pos_corner[c] for c in range(3)], gi, gj, at)

    def force_terms():
        def row(i, carry):
            def strided(c):
                return raw[pl.ds(64 * i + c, 8, stride=8), :]

            weight = strided(3)
            px, py, pz = pos32[i, 0] + place(i), pos32[i, 1] + steps8, pos32[i, 2]
            lx, ly, lz = lever[i, 0], lever[i, 1], lever[i, 2]
            fx = (px * weight - (strided(0) + strided(4))) * final_scale
            fy = (py * weight - (strided(1) + strided(5))) * final_scale
            fz = (pz * weight - strided(2)) * final_scale
            rows = [fx, fy, fz, ly * fz - lz * fy, lz * fx - lx * fz, lx * fy - ly * fx]
            put = rows + [zero8] * 2
            for c, value in enumerate(put):
                high = value.astype(BF16).astype(F32)
                terms[pl.ds(128 * i + c, 8, stride=16), :] = high
                terms[pl.ds(128 * i + 8 + c, 8, stride=16), :] = value - high
            return carry

        lax.fori_loop(0, 8, row, 0)

    def part_terms(t):
        return terms[pl.ds(pl.multiple_of(t * 16, 16), 16), :]

    def masked_sums(places, start, count):
        left, right = [], []
        for i, j in places:
            t = i * 8 + j
            value = part_terms(t)
            whose = owner[i, pl.ds(j, 1), :]
            masks = [jnp.where(whose == start + c, value, 0.0) for c in range(count)]
            left.append(jnp.concatenate(masks, axis=0).astype(BF16))
            right.append(oh[t])
        got = mm_nt(jnp.concatenate(left, axis=1), jnp.concatenate(right, axis=1))
        where = pl.ds(pl.multiple_of(start * 16, 16), count * 16)
        acc[where, :] = acc[where, :] + got

    part_copies = []
    for n, code in enumerate(CODES):
        part_copies.append(
            pltpu.make_async_remote_copy(
                src_ref=part_out.at[code],
                dst_ref=part_in.at[code],
                send_sem=part_send.at[n],
                recv_sem=part_recv.at[n],
                device_id=neighbour(code),
                device_id_type=MESH,
            )
        )

    def send_parts():
        force_terms()

        def rows(side, carry):
            masked_sums([(7 * side, m) for m in range(8)], 3 * side, 6)
            return carry

        def cols(side, carry):
            masked_sums([(m, 7 * side) for m in range(1, 7)], 3 + side, 2)
            return carry

        lax.fori_loop(0, 2, rows, 0)
        lax.fori_loop(0, 2, cols, 0)
        for code in CODES:
            part_out[code] = acc[16 * code : 16 * code + 8, :] + acc[16 * code + 8 : 16 * code + 16, :]
        for copy in part_copies:
            copy.start()

    first = where_is(jnp.int32(0))
    run(scores(first, s_even))

    def two_pairs(q, carry):
        now, after = carry[:14], carry[14:]
        pl.when(q == INNER_FIRST // 2 - 1)(finish_halo)
        pl.when(q == INNER_FIRST // 2 + 7)(send_parts)
        later = where_is(2 * q + 2)
        last = where_is(2 * q + 3)
        mixed_run(scores(after, s_odd), couples(now, s_even))
        mixed_run(scores(later, s_even), couples(after, s_odd))
        return later + last

    carry = lax.fori_loop(0, 15, two_pairs, first + where_is(jnp.int32(1)))
    now, after = carry[:14], carry[14:]
    mixed_run(scores(after, s_odd), couples(now, s_even))
    run(couples(after, s_odd))

    force_terms()

    def inner_sums(q, total):
        left, right = [], []
        for i in (2 * q + 1, 2 * q + 2):
            for j in range(1, 7):
                left.append(part_terms(i * 8 + j).astype(BF16))
                right.append(oh[i * 8 + j])
        return total + mm_nt(jnp.concatenate(left, axis=1), jnp.concatenate(right, axis=1))

    own = lax.fori_loop(0, 3, inner_sums, acc[64:80, :])
    total = own[0:8] + own[8:16]
    for copy in part_copies:
        copy.wait_recv()
    for code in CODES:
        total = total + part_in[code]

    inv = inverse[0, 0]
    centre = [pose[0, c] for c in range(3)]
    quat = [pose[0, c] for c in range(3, 7)]
    vel = [motion[0, c] + STEP_DT * inv[0:1] * total[c : c + 1] for c in range(3)]
    ang = [motion[0, c] + STEP_DT * total[c : c + 1] for c in range(3, 6)]
    shift = [STEP_DT * v for v in vel]
    rot = rotation_rows(*quat)
    frame = [
        (rot[0][c] * ang[0] + rot[1][c] * ang[1] + rot[2][c] * ang[2]) * inv[c + 1 : c + 2]
        for c in range(3)
    ]
    omega = [rot[r][0] * frame[0] + rot[r][1] * frame[1] + rot[r][2] * frame[2] for r in range(3)]
    qw, qv = quat[0], quat[1:4]
    change = [
        -(omega[0] * qv[0] + omega[1] * qv[1] + omega[2] * qv[2]),
        qw * omega[0] + (omega[1] * qv[2] - omega[2] * qv[1]),
        qw * omega[1] + (omega[2] * qv[0] - omega[0] * qv[2]),
        qw * omega[2] + (omega[0] * qv[1] - omega[1] * qv[0]),
    ]
    stepped = [q + 0.5 * STEP_DT * d for q, d in zip(quat, change)]
    norm = jnp.sqrt(sum(s * s for s in stepped[1:]) + stepped[0] * stepped[0])
    turned = [s / norm for s in stepped]
    rot_new = rotation_rows(*turned)
    for c in range(3):
        table_f32[c : c + 1, :] = shift[c]
        for r in range(3):
            entry = sum(rot_new[r][k] * rot[c][k] for k in range(3))
            table_f32[3 * (c + 1) + r : 3 * (c + 1) + r + 1, :] = entry
    whole = table_f32[...]
    high = whole.astype(BF16)
    table[128:144, :] = high
    table[144:160, :] = (whole - high.astype(F32)).astype(BF16)
    table_copies = []
    for n, code in enumerate(CODES):
        table_copies.append(
            pltpu.make_async_remote_copy(
                src_ref=table.at[pl.ds(128, 32)],
                dst_ref=table.at[pl.ds((8 - code) * 32, 32)],
                send_sem=table_send.at[n],
                recv_sem=table_recv.at[n],
                device_id=neighbour(code),
                device_id_type=MESH,
            )
        )
    for copy in table_copies:
        copy.start()
    next_rows = [c + s for c, s in zip(centre, shift)] + turned + vel + ang
    for c, value in enumerate(next_rows):
        body_next[0, c] = value

    def look_up(places, start, count):
        if count == 1:
            rows = table[128:160, :]
        else:
            rows = table[pl.ds(pl.multiple_of(start * 32, 32), count * 32), :]
        tiles = [i * 8 + j for i, j in places]
        got = mm(rows, jnp.concatenate([oh[t] for t in tiles], axis=1))
        for n, (i, j) in enumerate(places):
            lanes = slice(128 * n, 128 * n + 128)
            found = None
            for c in range(count):
                one = got[32 * c : 32 * c + 16, lanes] + got[32 * c + 16 : 32 * c + 32, lanes]
                if c:
                    whose = owner[i, pl.ds(j, 1), :]
                    found = jnp.where(whose == start + c, one, found)
                else:
                    found = one
            picked[pl.ds(pl.multiple_of(tiles[n] * 16, 16), 16), :] = found

    def look_inner(i, carry):
        look_up([(i, j) for j in range(1, 7)], 4, 1)
        return carry

    lax.fori_loop(1, 7, look_inner, 0)
    for copy in table_copies:
        copy.wait_recv()

    def look_rows(q, carry):
        i, start = 7 * (q // 2), 3 * (q // 2)
        look_up([(i, 4 * (q % 2) + m) for m in range(4)], start, 6)
        return carry

    def look_cols(side, carry):
        look_up([(i, 7 * side) for i in range(1, 7)], 3 + side, 2)
        return carry

    lax.fori_loop(0, 4, look_rows, 0)
    lax.fori_loop(0, 2, look_cols, 0)

    def move(i, carry):
        def strided(c):
            return picked[pl.ds(128 * i + c, 8, stride=16), :]

        levers = [lever[i, c] for c in range(3)]
        for r in range(3):
            value = pos32[i, r] + strided(r)
            for c in range(3):
                value = value + strided(3 + 3 * c + r) * levers[c]
            moved[i, r] = value - levers[r]
        return carry

    lax.fori_loop(0, 8, move, 0)
    for copy in pos_copies + v_copies + part_copies + table_copies:
        copy.wait_send()


def local(
    positions,
    features,
    lever,
    partner,
    body_slot,
    owner_dir,
    body_pose,
    body_motion,
    body_inverse,
    weight_u,
    weight_v,
    radial_rate,
):
    hbm = pl.BlockSpec(memory_space=pl.ANY)
    smem = pl.BlockSpec(memory_space=pltpu.SMEM)
    vmem = pl.BlockSpec(memory_space=pltpu.VMEM)
    dma = pltpu.SemaphoreType.DMA
    like = lambda x: pltpu.VMEM(x.shape, x.dtype)
    inside = lambda x: jnp.transpose(x, (0, 2, 1, 3))
    positions, lever = inside(positions), inside(lever)
    body_pose, body_motion = inside(body_pose), inside(body_motion)
    partner = jnp.transpose(partner, (2, 0, 1))
    moved, body_next = pl.pallas_call(
        kernel,
        out_shape=(
            jax.ShapeDtypeStruct((8, 3, 8, 128), F32),
            jax.ShapeDtypeStruct((1, 13, 1, 128), F32),
        ),
        in_specs=[smem, smem] + [hbm] * 10,
        out_specs=(vmem, vmem),
        scratch_shapes=[
            like(positions),
            like(features),
            like(lever),
            like(body_slot),
            like(owner_dir),
            like(body_pose),
            like(body_motion),
            like(body_inverse),
            like(weight_u),
            like(weight_v),
            pltpu.VMEM((100, 128, 128), BF16),
            pltpu.VMEM((100, 128, 128), BF16),
            pltpu.VMEM((100, 16, 128), BF16),
            pltpu.VMEM((64, 32, 128), BF16),
            pltpu.VMEM((64, 512, 128), BF16),
            pltpu.VMEM((64, 128, 128), BF16),
            pltpu.VMEM((512, 128), F32),
            pltpu.VMEM((1024, 128), F32),
            pltpu.VMEM((1024, 128), F32),
            pltpu.VMEM((144, 128), F32),
            pltpu.VMEM((9, 8, 128), F32),
            pltpu.VMEM((9, 8, 128), F32),
            pltpu.VMEM((288, 128), BF16),
            pltpu.VMEM((16, 128), F32),
            pltpu.VMEM((8, 3, 8, 128), F32),
            pltpu.VMEM((256, 128), F32),
            pltpu.VMEM((256, 128), F32),
            pltpu.VMEM((64, 128), F32),
            pltpu.VMEM((2, 3, 8, 128), F32),
            pltpu.VMEM((2, 3, 8, 128), F32),
            pltpu.VMEM((3, 8, 128), F32),
            pltpu.VMEM((2, 8, 128, 128), BF16),
            pltpu.VMEM((2, 8, 128, 128), BF16),
            pltpu.VMEM((4, 128, 128), BF16),
            pltpu.VMEM((5, 768, 256), F32),
            pltpu.VMEM((5, 768, 256), F32),
            dma((24,)),
            dma((12,)),
            dma((12,)),
            dma((8,)),
            dma((8,)),
            dma((8,)),
            dma((8,)),
            dma((8,)),
            dma((8,)),
        ],
        compiler_params=pltpu.CompilerParams(
            collective_id=0, has_side_effects=True, vmem_limit_bytes=60 * 1024 * 1024
        ),
        name="step",
    )(
        partner,
        radial_rate,
        positions,
        features,
        lever,
        body_slot,
        owner_dir,
        body_pose,
        body_motion,
        body_inverse,
        weight_u,
        weight_v,
    )
    return inside(moved), inside(body_next)


def solution(mesh):
    tiles = P("gx", "gy", None, None)
    flat = P("gx", "gy", None)
    return jax.shard_map(
        local,
        mesh=mesh,
        in_specs=(tiles, tiles, tiles, flat, flat, flat, tiles, tiles, tiles, P(), P(), P()),
        out_specs=(tiles, tiles),
        check_vma=False,
    )
```

```python
import jax
import jax.numpy as jnp
from jax import lax
from jax.experimental import pallas as pl
from jax.experimental.pallas import tpu as pltpu
from jax.sharding import PartitionSpec as P

STEP_DT = 0.25
LOG2E = 1.4426950408889634
MESH = pl.DeviceIdType.MESH
F32 = jnp.float32
BF16 = jnp.bfloat16
INNER_FIRST = 14
CODES = [c for c in range(9) if c != 4]
MIX = "DUUDUUDUUDUUDUU"
DOTS = (0, 1, 4, 2, 3)


def mm(a, b):
    return jnp.dot(a, b, preferred_element_type=F32)


def mm_nt(a, b):
    return lax.dot_general(a, b, (((1,), (1,)), ((), ())), preferred_element_type=F32)


def split3(value):
    high = value.astype(BF16).astype(F32)
    rest = value - high
    mid = rest.astype(BF16).astype(F32)
    return high, mid, rest - mid


def inner_pair(q):
    i = 1 + q // 3
    j = 1 + 2 * (q % 3)
    return i, j, i, j + 1


def rim_pair(q):
    in_rows = q < 8
    c = q - 8
    i = jnp.where(in_rows, 7 * (q // 4), 1 + 2 * (c % 3))
    j = jnp.where(in_rows, 2 * (q % 4), 7 * (c // 3))
    return i, j, jnp.where(in_rows, i, i + 1), jnp.where(in_rows, j + 1, j)


def row_pair(q):
    i = 7 * (q // 4)
    j = 2 * (q % 4)
    return i, j, i, j + 1


def col_pair(q):
    i = 1 + 2 * (q % 3)
    j = 7 * (q // 3)
    return i, j, i + 1, j


def rim_then_inner(p):
    rim = rim_pair(jnp.clip(p, 0, 13))
    inner = inner_pair(jnp.clip(p - 14, 0, 17))
    return tuple(jnp.where(p < 14, r, n) for r, n in zip(rim, inner))


def any_pair(p):
    rim = rim_pair(jnp.clip(p - INNER_FIRST, 0, 13))
    inner = inner_pair(jnp.clip(jnp.where(p < INNER_FIRST, p, p - 14), 0, 17))
    is_rim = (p >= INNER_FIRST) & (p < INNER_FIRST + 14)
    return tuple(jnp.where(is_rim, r, n) for r, n in zip(rim, inner))


def rotation_rows(qw, qa, qb, qc):
    return [
        [1 - 2 * (qb * qb + qc * qc), 2 * (qa * qb - qw * qc), 2 * (qa * qc + qw * qb)],
        [2 * (qa * qb + qw * qc), 1 - 2 * (qa * qa + qc * qc), 2 * (qb * qc - qw * qa)],
        [2 * (qa * qc - qw * qb), 2 * (qb * qc + qw * qa), 1 - 2 * (qa * qa + qb * qb)],
    ]


def kernel(
    codes,
    rates,
    positions,
    features,
    lever_in,
    slot_in,
    owner_in,
    pose_in,
    motion_in,
    inverse_in,
    wu_in,
    wv_in,
    moved,
    body_next,
    pos,
    feat,
    lever,
    slot,
    owner,
    pose,
    motion,
    inverse,
    weights,
    vt,
    qf,
    qm,
    rp,
    u,
    oh,
    raw,
    terms,
    picked,
    acc,
    part_out,
    part_in,
    table,
    table_f32,
    pos32,
    stage_q,
    stage_r,
    stage_m,
    pos_row,
    pos_col,
    pos_corner,
    v_row,
    v_col,
    v_corner,
    s_even,
    s_odd,
    in_sem,
    pos_send,
    pos_recv,
    v_send,
    v_recv,
    part_send,
    part_recv,
    table_send,
    table_recv,
):
    gx, gy = lax.axis_index("gx"), lax.axis_index("gy")
    nx, ny = lax.axis_size("gx"), lax.axis_size("gy")

    def neighbour(code):
        a, b = code // 3 - 1, code % 3 - 1
        return (lax.rem(gx + a + nx, nx), lax.rem(gy + b + ny, ny))

    loads = []

    def load(src, dst):
        copy = pltpu.make_async_copy(src, dst, in_sem.at[len(loads)])
        copy.start()
        loads.append(copy)
        return copy

    got_pos = load(positions, pos)
    got_weights = [load(wu_in, weights.at[0:512]), load(wv_in, weights.at[512:640])]
    rim_loads = [
        load(features.at[0], feat.at[0]),
        load(features.at[7], feat.at[7]),
        load(features.at[1:7, 0], feat.at[1:7, 0]),
        load(features.at[1:7, 7], feat.at[1:7, 7]),
    ]
    small_loads = [
        load(slot_in, slot),
        load(owner_in, owner),
        load(lever_in, lever),
        load(pose_in, pose),
        load(motion_in, motion),
        load(inverse_in, inverse),
    ]
    inner_loads = [load(features.at[i, 1:7], feat.at[i, 1:7]) for i in range(1, 7)]

    barrier = pltpu.get_barrier_semaphore()
    for code in CODES:
        pl.semaphore_signal(barrier, inc=1, device_id=neighbour(code), device_id_type=MESH)

    rate_scale = [rates[k] * (-LOG2E) for k in range(4)]
    lead = rate_scale[0]
    ratio = [None] + [rate_scale[k] / lead for k in range(1, 4)]
    four_lead = -4.0 * lead
    final_scale = 1.0 / (2048.0 * lead * lead)
    raw[...] = jnp.zeros_like(raw)
    acc[...] = jnp.zeros_like(acc)
    stage_q[...] = jnp.zeros_like(stage_q)
    stage_r[...] = jnp.zeros_like(stage_r)
    stage_m[...] = jnp.zeros_like(stage_m)
    table_f32[...] = jnp.zeros_like(table_f32)

    got_pos.wait()
    pos32[...] = pos[...].astype(F32)

    def v_src(a, b):
        if b == 0:
            return vt.at[pl.ds(11 if a < 0 else 81, 8)]
        if a == 0:
            return None
        return vt.at[(10 if a < 0 else 80) + (1 if b < 0 else 8)]

    def landing(a, b, row_ref, col_ref, corner_ref):
        if b == 0:
            return row_ref.at[1 if a < 0 else 0]
        if a == 0:
            return col_ref.at[1 if b < 0 else 0]
        return corner_ref.at[(2 if a < 0 else 0) + (1 if b < 0 else 0)]

    lane = lax.broadcasted_iota(jnp.int32, (128, 128), 1)
    own_lanes = [jnp.where(lane // 32 == m, 1.0, 0.0).astype(BF16) for m in range(4)]
    zero8 = jnp.zeros((8, 128), F32)
    one8 = jnp.ones((8, 128), F32)
    steps8 = lax.broadcasted_iota(jnp.int32, (8, 128), 0).astype(F32) - 3.5

    def place(i):
        return jnp.full((8, 128), i.astype(F32) - 3.5)

    def put_rows(ref, stride, values):
        for r, value in enumerate(values):
            ref[pl.ds(r, 8, stride=stride), :] = value

    def partner_tables(q, gi, gj, indices):
        ax, ay = q[0] + gi, q[1] + gj
        square = split3(lead * (ax * ax + ay * ay + q[2] * q[2]))
        values = [q[0]] * 3 + [q[1]] * 3 + [q[2]] * 3 + [gi] * 3 + [gj] * 3
        put_rows(stage_q, 32, values + list(square) + [one8] * 3)
        put_rows(stage_m, 8, [q[0], q[1], q[2], one8, gi, gj])
        for half in range((len(indices) + 3) // 4):
            turned = stage_q[128 * half : 128 * half + 128, :].T.astype(BF16)
            for m, index in enumerate(indices[4 * half : 4 * half + 4]):
                qf[index] = turned * own_lanes[m]
        for m, index in enumerate(indices):
            rows = stage_m[8 * m : 8 * m + 8, :]
            qm[index] = jnp.concatenate([rows, zero8], axis=0).astype(BF16)

    slots = lax.broadcasted_iota(jnp.int32, (128, 128), 0)
    for copy in small_loads:
        copy.wait()

    def prepare(i, carry):
        q = [pos32[i, c] for c in range(3)]
        gi = place(i)
        partner_tables(q, gi, steps8, [(i + 1) * 10 + 1 + m for m in range(8)])
        ax, ay, az = q[0] + gi, q[1] + steps8, q[2]
        xs = list(split3(-2.0 * lead * ax))
        ys = list(split3(-2.0 * lead * ay))
        zs = list(split3(-2.0 * lead * az))
        sq = list(split3(lead * (ax * ax + ay * ay + az * az)))
        put_rows(stage_r, 32, xs + ys + zs + xs + ys + [one8] * 3 + sq)
        for m in range(8):
            rp[i * 8 + m] = stage_r[32 * m : 32 * m + 32, :].astype(BF16)
            here = slot[i, m : m + 1, :]
            oh[i * 8 + m] = jnp.where(slots == here, 1.0, 0.0).astype(BF16)
        return carry

    lax.fori_loop(0, 8, prepare, 0)

    pos_copies, v_copies = [], []

    def project(pair, s):
        ia, ja, ib, jb = pair
        both = jnp.concatenate([feat[ia, ja], feat[ib, jb]], axis=1)
        s[0, 0:640, :] = mm(weights[...], both)

    def settle(pair, s):
        ia, ja, ib, jb = pair
        for i, j, lanes in ((ia, ja, slice(0, 128)), (ib, jb, slice(128, 256))):
            u[i * 8 + j] = s[0, 0:512, lanes].astype(BF16)
            vt[(i + 1) * 10 + j + 1] = s[0, 512:640, lanes].astype(BF16).T

    for copy in got_weights + rim_loads + inner_loads:
        copy.wait()
    start = [rim_then_inner(jnp.int32(p)) for p in range(3)]
    project(start[0], s_even)

    def project_two(q, carry):
        now, after, later = carry
        project(after, s_odd)
        settle(now, s_even)
        project(later, s_even)
        settle(after, s_odd)
        return later, rim_then_inner(2 * q + 3), rim_then_inner(2 * q + 4)

    carry = lax.fori_loop(0, 7, project_two, tuple(start))
    pl.semaphore_wait(barrier, 8)

    def send_pos(src, dst, code):
        n = len(pos_copies)
        copy = pltpu.make_async_remote_copy(
            src_ref=src,
            dst_ref=dst,
            send_sem=pos_send.at[n],
            recv_sem=pos_recv.at[n],
            device_id=neighbour(code),
            device_id_type=MESH,
        )
        copy.start()
        pos_copies.append(copy)

    for code in CODES:
        a, b = code // 3 - 1, code % 3 - 1
        i, j = (0 if a < 0 else 7), (0 if b < 0 else 7)
        if b == 0:
            send_pos(pos32.at[i], pos_row.at[1 if a < 0 else 0], code)
        elif a == 0:
            for c in range(3):
                send_pos(pos32.at[:, c, j], pos_col.at[1 if b < 0 else 0, c], code)
        else:
            k = (2 if a < 0 else 0) + (1 if b < 0 else 0)
            send_pos(pos32.at[i, :, j], pos_corner.at[:, k], code)

    vt4 = vt.reshape(10, 10, 128, 128)
    for n, code in enumerate(CODES):
        a, b = code // 3 - 1, code % 3 - 1
        src = vt4.at[1:9, 1 if b < 0 else 8] if a == 0 else v_src(a, b)
        v_copies.append(
            pltpu.make_async_remote_copy(
                src_ref=src,
                dst_ref=landing(a, b, v_row, v_col, v_corner),
                send_sem=v_send.at[n],
                recv_sem=v_recv.at[n],
                device_id=neighbour(code),
                device_id_type=MESH,
            )
        )
    for n in sorted(range(8), key=lambda n: (CODES[n] // 3 == 1, CODES[n])):
        v_copies[n].start()

    lax.fori_loop(7, 16, project_two, carry)

    def where_is(p):
        ia, ja, ib, jb = any_pair(p)
        found = [ia * 8 + ja, ib * 8 + jb]
        for i, j in ((ia, ja), (ib, jb)):
            for n in range(6):
                c = codes[n, i, j]
                found.append(i * 10 + j + c + 7 * ((c * 11) >> 5))
        return tuple(found)

    zeros128 = jnp.zeros((128, 128), BF16)

    def scores(at, s):
        for which in DOTS:
            if which == 4:
                rows = [jnp.concatenate([qf[n], qf[m]], axis=1) for n, m in zip(at[2:8], at[8:14])]
                right = jnp.concatenate(
                    [
                        jnp.concatenate([rp[at[0]]] * 4 + [zeros128], axis=0),
                        jnp.concatenate([zeros128] + [rp[at[1]]] * 4, axis=0),
                    ],
                    axis=1,
                )
            else:
                x, half = which // 2, which % 2
                rows = [vt[n] for n in at[2 + 6 * x : 8 + 6 * x]]
                first = u[at[x], 256 * half : 256 * half + 128, :]
                second = u[at[x], 256 * half + 128 : 256 * half + 256, :]
                right = jnp.concatenate([first, second], axis=1)
            s[which] = mm(jnp.concatenate(rows, axis=0), right)
            yield

    def couples(at, s):
        for x in range(2):
            t, found = at[x], at[2 + 6 * x : 8 + 6 * x]
            total = None
            for two in range(3):
                couple = []
                for n in (2 * two, 2 * two + 1):
                    rows = slice(n * 128, (n + 1) * 128)
                    t0 = s[4, rows, x * 128 : (x + 1) * 128]
                    mixed = None
                    for k in range(4):
                        score = s[2 * x + k // 2, rows, (k % 2) * 128 : (k % 2 + 1) * 128]
                        term = jnp.exp2(t0 if k == 0 else t0 * ratio[k]) * score
                        mixed = term if mixed is None else mixed + term
                    inside = jnp.maximum(t0 + four_lead, 0.0)
                    couple.append((mixed * (inside * inside)).astype(BF16))
                    yield
                left = jnp.concatenate([qm[found[2 * two]], qm[found[2 * two + 1]]], axis=1)
                got = mm(left, jnp.concatenate(couple, axis=0))
                total = got if total is None else total + got
            raw[pl.ds(pl.multiple_of(t * 8, 8), 8), :] = total[0:8]

    def run(steps):
        for _ in steps:
            pass

    def mixed_run(first, second):
        for which in MIX:
            next(first if which == "D" else second)
        run(first)
        run(second)

    def finish_halo():
        for copy in pos_copies:
            copy.wait_recv()
        for copy in v_copies:
            copy.wait_recv()

        def rows(side, carry):
            edge = place(9 * side - 1)
            at = [90 * side + 1 + m for m in range(8)]
            for m in range(8):
                vt[at[m]] = v_row[side, m]
            partner_tables([pos_row[side, c] for c in range(3)], edge, steps8, at)
            return carry

        def cols(side, carry):
            edge = place(9 * side - 1)
            at = [(m + 1) * 10 + 9 * side for m in range(8)]
            for m in range(8):
                vt[at[m]] = v_col[side, m]
            partner_tables([pos_col[side, c] for c in range(3)], steps8, edge, at)
            return carry

        lax.fori_loop(0, 2, rows, 0)
        lax.fori_loop(0, 2, cols, 0)
        k = lax.broadcasted_iota(jnp.int32, (8, 128), 0)
        gi = jnp.where(k < 2, -4.5, 4.5)
        gj = jnp.where(k % 2 == 0, -4.5, 4.5)
        at = [0, 9, 90, 99]
        for m in range(4):
            vt[at[m]] = v_corner[m]
        partner_tables([pos_corner[c] for c in range(3)], gi, gj, at)

    def force_terms():
        def row(i, carry):
            def strided(c):
                return raw[pl.ds(64 * i + c, 8, stride=8), :]

            weight = strided(3)
            px, py, pz = pos32[i, 0] + place(i), pos32[i, 1] + steps8, pos32[i, 2]
            lx, ly, lz = lever[i, 0], lever[i, 1], lever[i, 2]
            fx = (px * weight - (strided(0) + strided(4))) * final_scale
            fy = (py * weight - (strided(1) + strided(5))) * final_scale
            fz = (pz * weight - strided(2)) * final_scale
            rows = [fx, fy, fz, ly * fz - lz * fy, lz * fx - lx * fz, lx * fy - ly * fx]
            put = rows + [zero8] * 2
            for c, value in enumerate(put):
                high = value.astype(BF16).astype(F32)
                terms[pl.ds(128 * i + c, 8, stride=16), :] = high
                terms[pl.ds(128 * i + 8 + c, 8, stride=16), :] = value - high
            return carry

        lax.fori_loop(0, 8, row, 0)

    def part_terms(t):
        return terms[pl.ds(pl.multiple_of(t * 16, 16), 16), :]

    def masked_sums(places, start, count):
        left, right = [], []
        for i, j in places:
            t = i * 8 + j
            value = part_terms(t)
            whose = owner[i, pl.ds(j, 1), :]
            masks = [jnp.where(whose == start + c, value, 0.0) for c in range(count)]
            left.append(jnp.concatenate(masks, axis=0).astype(BF16))
            right.append(oh[t])
        got = mm_nt(jnp.concatenate(left, axis=1), jnp.concatenate(right, axis=1))
        where = pl.ds(pl.multiple_of(start * 16, 16), count * 16)
        acc[where, :] = acc[where, :] + got

    part_copies = []
    for n, code in enumerate(CODES):
        part_copies.append(
            pltpu.make_async_remote_copy(
                src_ref=part_out.at[code],
                dst_ref=part_in.at[code],
                send_sem=part_send.at[n],
                recv_sem=part_recv.at[n],
                device_id=neighbour(code),
                device_id_type=MESH,
            )
        )

    def send_parts():
        force_terms()

        def rows(side, carry):
            masked_sums([(7 * side, m) for m in range(8)], 3 * side, 6)
            return carry

        def cols(side, carry):
            masked_sums([(m, 7 * side) for m in range(1, 7)], 3 + side, 2)
            return carry

        lax.fori_loop(0, 2, rows, 0)
        lax.fori_loop(0, 2, cols, 0)
        for code in CODES:
            part_out[code] = acc[16 * code : 16 * code + 8, :] + acc[16 * code + 8 : 16 * code + 16, :]
        for copy in part_copies:
            copy.start()

    first = where_is(jnp.int32(0))
    run(scores(first, s_even))

    def two_pairs(q, carry):
        now, after = carry[:14], carry[14:]
        pl.when(q == INNER_FIRST // 2 - 1)(finish_halo)
        pl.when(q == INNER_FIRST // 2 + 7)(send_parts)
        later = where_is(2 * q + 2)
        last = where_is(2 * q + 3)
        mixed_run(scores(after, s_odd), couples(now, s_even))
        mixed_run(scores(later, s_even), couples(after, s_odd))
        return later + last

    carry = lax.fori_loop(0, 15, two_pairs, first + where_is(jnp.int32(1)))
    now, after = carry[:14], carry[14:]
    mixed_run(scores(after, s_odd), couples(now, s_even))
    run(couples(after, s_odd))

    force_terms()

    def inner_sums(q, total):
        left, right = [], []
        for i in (2 * q + 1, 2 * q + 2):
            for j in range(1, 7):
                left.append(part_terms(i * 8 + j).astype(BF16))
                right.append(oh[i * 8 + j])
        return total + mm_nt(jnp.concatenate(left, axis=1), jnp.concatenate(right, axis=1))

    own = lax.fori_loop(0, 3, inner_sums, acc[64:80, :])
    total = own[0:8] + own[8:16]
    for copy in part_copies:
        copy.wait_recv()
    for code in CODES:
        total = total + part_in[code]

    inv = inverse[0, 0]
    centre = [pose[0, c] for c in range(3)]
    quat = [pose[0, c] for c in range(3, 7)]
    vel = [motion[0, c] + STEP_DT * inv[0:1] * total[c : c + 1] for c in range(3)]
    ang = [motion[0, c] + STEP_DT * total[c : c + 1] for c in range(3, 6)]
    shift = [STEP_DT * v for v in vel]
    rot = rotation_rows(*quat)
    frame = [
        (rot[0][c] * ang[0] + rot[1][c] * ang[1] + rot[2][c] * ang[2]) * inv[c + 1 : c + 2]
        for c in range(3)
    ]
    omega = [rot[r][0] * frame[0] + rot[r][1] * frame[1] + rot[r][2] * frame[2] for r in range(3)]
    qw, qv = quat[0], quat[1:4]
    change = [
        -(omega[0] * qv[0] + omega[1] * qv[1] + omega[2] * qv[2]),
        qw * omega[0] + (omega[1] * qv[2] - omega[2] * qv[1]),
        qw * omega[1] + (omega[2] * qv[0] - omega[0] * qv[2]),
        qw * omega[2] + (omega[0] * qv[1] - omega[1] * qv[0]),
    ]
    stepped = [q + 0.5 * STEP_DT * d for q, d in zip(quat, change)]
    norm = jnp.sqrt(sum(s * s for s in stepped[1:]) + stepped[0] * stepped[0])
    turned = [s / norm for s in stepped]
    rot_new = rotation_rows(*turned)
    for c in range(3):
        table_f32[c : c + 1, :] = shift[c]
        for r in range(3):
            entry = sum(rot_new[r][k] * rot[c][k] for k in range(3))
            table_f32[3 * (c + 1) + r : 3 * (c + 1) + r + 1, :] = entry
    whole = table_f32[...]
    high = whole.astype(BF16)
    table[128:144, :] = high
    table[144:160, :] = (whole - high.astype(F32)).astype(BF16)
    table_copies = []
    for n, code in enumerate(CODES):
        table_copies.append(
            pltpu.make_async_remote_copy(
                src_ref=table.at[pl.ds(128, 32)],
                dst_ref=table.at[pl.ds((8 - code) * 32, 32)],
                send_sem=table_send.at[n],
                recv_sem=table_recv.at[n],
                device_id=neighbour(code),
                device_id_type=MESH,
            )
        )
    for copy in table_copies:
        copy.start()
    next_rows = [c + s for c, s in zip(centre, shift)] + turned + vel + ang
    for c, value in enumerate(next_rows):
        body_next[0, c] = value

    def look_up(places, start, count):
        if count == 1:
            rows = table[128:160, :]
        else:
            rows = table[pl.ds(pl.multiple_of(start * 32, 32), count * 32), :]
        tiles = [i * 8 + j for i, j in places]
        got = mm(rows, jnp.concatenate([oh[t] for t in tiles], axis=1))
        for n, (i, j) in enumerate(places):
            lanes = slice(128 * n, 128 * n + 128)
            found = None
            for c in range(count):
                one = got[32 * c : 32 * c + 16, lanes] + got[32 * c + 16 : 32 * c + 32, lanes]
                if c:
                    whose = owner[i, pl.ds(j, 1), :]
                    found = jnp.where(whose == start + c, one, found)
                else:
                    found = one
            picked[pl.ds(pl.multiple_of(tiles[n] * 16, 16), 16), :] = found

    def look_inner(i, carry):
        look_up([(i, j) for j in range(1, 7)], 4, 1)
        return carry

    lax.fori_loop(1, 7, look_inner, 0)
    for copy in table_copies:
        copy.wait_recv()

    def look_rows(q, carry):
        i, start = 7 * (q // 2), 3 * (q // 2)
        look_up([(i, 4 * (q % 2) + m) for m in range(4)], start, 6)
        return carry

    def look_cols(side, carry):
        look_up([(i, 7 * side) for i in range(1, 7)], 3 + side, 2)
        return carry

    lax.fori_loop(0, 4, look_rows, 0)
    lax.fori_loop(0, 2, look_cols, 0)

    def move(i, carry):
        def strided(c):
            return picked[pl.ds(128 * i + c, 8, stride=16), :]

        levers = [lever[i, c] for c in range(3)]
        for r in range(3):
            value = pos32[i, r] + strided(r)
            for c in range(3):
                value = value + strided(3 + 3 * c + r) * levers[c]
            moved[i, r] = value - levers[r]
        return carry

    lax.fori_loop(0, 8, move, 0)
    for copy in pos_copies + v_copies + part_copies + table_copies:
        copy.wait_send()


def hand_over(moved, body_next, moved_out, body_out, sem):
    copies = [
        pltpu.make_async_copy(moved, moved_out, sem.at[0]),
        pltpu.make_async_copy(body_next, body_out, sem.at[1]),
    ]
    for copy in copies:
        copy.start()
    for copy in copies:
        copy.wait()


def local(
    positions,
    features,
    lever,
    partner,
    body_slot,
    owner_dir,
    body_pose,
    body_motion,
    body_inverse,
    weight_u,
    weight_v,
    radial_rate,
):
    hbm = pl.BlockSpec(memory_space=pl.ANY)
    smem = pl.BlockSpec(memory_space=pltpu.SMEM)
    vmem = pl.BlockSpec(memory_space=pltpu.VMEM)
    dma = pltpu.SemaphoreType.DMA
    like = lambda x: pltpu.VMEM(x.shape, x.dtype)
    inside = lambda x: jnp.transpose(x, (0, 2, 1, 3))
    positions, lever = inside(positions), inside(lever)
    body_pose, body_motion = inside(body_pose), inside(body_motion)
    partner = jnp.transpose(partner, (2, 0, 1))
    moved, body_next = pl.pallas_call(
        kernel,
        out_shape=(
            pltpu.VMEM((8, 3, 8, 128), F32),
            pltpu.VMEM((1, 13, 1, 128), F32),
        ),
        in_specs=[smem, smem] + [hbm] * 10,
        out_specs=(vmem, vmem),
        scratch_shapes=[
            like(positions),
            like(features),
            like(lever),
            like(body_slot),
            like(owner_dir),
            like(body_pose),
            like(body_motion),
            like(body_inverse),
            pltpu.VMEM((640, 256), BF16),
            pltpu.VMEM((100, 128, 128), BF16),
            pltpu.VMEM((100, 128, 128), BF16),
            pltpu.VMEM((100, 16, 128), BF16),
            pltpu.VMEM((64, 32, 128), BF16),
            pltpu.VMEM((64, 512, 128), BF16),
            pltpu.VMEM((64, 128, 128), BF16),
            pltpu.VMEM((512, 128), F32),
            pltpu.VMEM((1024, 128), F32),
            pltpu.VMEM((1024, 128), F32),
            pltpu.VMEM((144, 128), F32),
            pltpu.VMEM((9, 8, 128), F32),
            pltpu.VMEM((9, 8, 128), F32),
            pltpu.VMEM((288, 128), BF16),
            pltpu.VMEM((16, 128), F32),
            pltpu.VMEM((8, 3, 8, 128), F32),
            pltpu.VMEM((256, 128), F32),
            pltpu.VMEM((256, 128), F32),
            pltpu.VMEM((64, 128), F32),
            pltpu.VMEM((2, 3, 8, 128), F32),
            pltpu.VMEM((2, 3, 8, 128), F32),
            pltpu.VMEM((3, 8, 128), F32),
            pltpu.VMEM((2, 8, 128, 128), BF16),
            pltpu.VMEM((2, 8, 128, 128), BF16),
            pltpu.VMEM((4, 128, 128), BF16),
            pltpu.VMEM((5, 768, 256), F32),
            pltpu.VMEM((5, 768, 256), F32),
            dma((24,)),
            dma((12,)),
            dma((12,)),
            dma((8,)),
            dma((8,)),
            dma((8,)),
            dma((8,)),
            dma((8,)),
            dma((8,)),
        ],
        compiler_params=pltpu.CompilerParams(
            collective_id=0, has_side_effects=True, vmem_limit_bytes=60 * 1024 * 1024
        ),
        name="step",
    )(
        partner,
        radial_rate,
        positions,
        features,
        lever,
        body_slot,
        owner_dir,
        body_pose,
        body_motion,
        body_inverse,
        weight_u,
        weight_v,
    )
    moved, body_next = pl.pallas_call(
        hand_over,
        out_shape=(
            jax.ShapeDtypeStruct((8, 3, 8, 128), F32),
            jax.ShapeDtypeStruct((1, 13, 1, 128), F32),
        ),
        in_specs=[vmem, vmem],
        out_specs=(hbm, hbm),
        scratch_shapes=[dma((2,))],
        name="out",
    )(
        pltpu.with_memory_space_constraint(moved, pltpu.VMEM),
        pltpu.with_memory_space_constraint(body_next, pltpu.VMEM),
    )
    return inside(moved), inside(body_next)


def solution(mesh):
    tiles = P("gx", "gy", None, None)
    flat = P("gx", "gy", None)
    return jax.shard_map(
        local,
        mesh=mesh,
        in_specs=(tiles, tiles, tiles, flat, flat, flat, tiles, tiles, tiles, P(), P(), P()),
        out_specs=(tiles, tiles),
        check_vma=False,
    )
```

```python
import functools

import jax
import jax.numpy as jnp
from jax import lax
from jax.experimental import pallas as pl
from jax.experimental.pallas import tpu as pltpu
from jax.sharding import PartitionSpec as P

STEP_DT = 0.25
LOG2E = 1.4426950408889634
MESH = pl.DeviceIdType.MESH
F32 = jnp.float32
BF16 = jnp.bfloat16
INNER_FIRST = 14
CODES = [c for c in range(9) if c != 4]
MIX = "DUUDUUDUUDUUDUU"
DOTS = (0, 1, 4, 2, 3)


def mm(a, b):
    return jnp.dot(a, b, preferred_element_type=F32)


def mm_nt(a, b):
    return lax.dot_general(a, b, (((1,), (1,)), ((), ())), preferred_element_type=F32)


def split3(value):
    high = value.astype(BF16).astype(F32)
    rest = value - high
    mid = rest.astype(BF16).astype(F32)
    return high, mid, rest - mid


def inner_pair(q):
    i = 1 + q // 3
    j = 1 + 2 * (q % 3)
    return i, j, i, j + 1


def rim_pair(q):
    in_rows = q < 8
    c = q - 8
    i = jnp.where(in_rows, 7 * (q // 4), 1 + 2 * (c % 3))
    j = jnp.where(in_rows, 2 * (q % 4), 7 * (c // 3))
    return i, j, jnp.where(in_rows, i, i + 1), jnp.where(in_rows, j + 1, j)


def row_pair(q):
    i = 7 * (q // 4)
    j = 2 * (q % 4)
    return i, j, i, j + 1


def col_pair(q):
    i = 1 + 2 * (q % 3)
    j = 7 * (q // 3)
    return i, j, i + 1, j


def rim_then_inner(p):
    rim = rim_pair(jnp.clip(p, 0, 13))
    inner = inner_pair(jnp.clip(p - 14, 0, 17))
    return tuple(jnp.where(p < 14, r, n) for r, n in zip(rim, inner))


def any_pair(p):
    rim = rim_pair(jnp.clip(p - INNER_FIRST, 0, 13))
    inner = inner_pair(jnp.clip(jnp.where(p < INNER_FIRST, p, p - 14), 0, 17))
    is_rim = (p >= INNER_FIRST) & (p < INNER_FIRST + 14)
    return tuple(jnp.where(is_rim, r, n) for r, n in zip(rim, inner))


def rotation_rows(qw, qa, qb, qc):
    return [
        [1 - 2 * (qb * qb + qc * qc), 2 * (qa * qb - qw * qc), 2 * (qa * qc + qw * qb)],
        [2 * (qa * qb + qw * qc), 1 - 2 * (qa * qa + qc * qc), 2 * (qb * qc - qw * qa)],
        [2 * (qa * qc - qw * qb), 2 * (qb * qc + qw * qa), 1 - 2 * (qa * qa + qb * qb)],
    ]


def kernel(
    codes,
    rates,
    positions,
    features,
    lever_in,
    slot_in,
    owner_in,
    pose_in,
    motion_in,
    inverse_in,
    wu_in,
    wv_in,
    moved,
    body_next,
    pos,
    feat,
    lever,
    slot,
    owner,
    pose,
    motion,
    inverse,
    weights,
    vt,
    qf,
    qm,
    rp,
    u,
    oh,
    raw,
    terms,
    picked,
    acc,
    part_out,
    part_in,
    table,
    table_f32,
    pos32,
    stage_q,
    stage_r,
    stage_m,
    pos_row,
    pos_col,
    pos_corner,
    v_row,
    v_col,
    v_corner,
    s_even,
    s_odd,
    in_sem,
    pos_send,
    pos_recv,
    v_send,
    v_recv,
    part_send,
    part_recv,
    table_send,
    table_recv,
):
    gx, gy = lax.axis_index("gx"), lax.axis_index("gy")
    nx, ny = lax.axis_size("gx"), lax.axis_size("gy")

    def neighbour(code):
        a, b = code // 3 - 1, code % 3 - 1
        return (lax.rem(gx + a + nx, nx), lax.rem(gy + b + ny, ny))

    loads = []

    def load(src, dst):
        copy = pltpu.make_async_copy(src, dst, in_sem.at[len(loads)])
        copy.start()
        loads.append(copy)
        return copy

    got_pos = load(positions, pos)
    got_weights = [load(wu_in, weights.at[0:512]), load(wv_in, weights.at[512:640])]
    rim_loads = [
        load(features.at[0], feat.at[0]),
        load(features.at[7], feat.at[7]),
        load(features.at[1:7, 0], feat.at[1:7, 0]),
        load(features.at[1:7, 7], feat.at[1:7, 7]),
    ]
    small_loads = [
        load(slot_in, slot),
        load(owner_in, owner),
        load(lever_in, lever),
        load(pose_in, pose),
        load(motion_in, motion),
        load(inverse_in, inverse),
    ]
    inner_loads = [load(features.at[i, 1:7], feat.at[i, 1:7]) for i in range(1, 7)]

    barrier = pltpu.get_barrier_semaphore()
    for code in CODES:
        pl.semaphore_signal(barrier, inc=1, device_id=neighbour(code), device_id_type=MESH)

    rate_scale = [rates[k] * (-LOG2E) for k in range(4)]
    lead = rate_scale[0]
    ratio = [None] + [rate_scale[k] / lead for k in range(1, 4)]
    four_lead = -4.0 * lead
    final_scale = 1.0 / (2048.0 * lead * lead)
    raw[...] = jnp.zeros_like(raw)
    acc[...] = jnp.zeros_like(acc)
    stage_q[...] = jnp.zeros_like(stage_q)
    stage_r[...] = jnp.zeros_like(stage_r)
    stage_m[...] = jnp.zeros_like(stage_m)
    table_f32[...] = jnp.zeros_like(table_f32)

    got_pos.wait()
    pos32[...] = pos[...].astype(F32)

    def v_src(a, b):
        if b == 0:
            return vt.at[pl.ds(11 if a < 0 else 81, 8)]
        if a == 0:
            return None
        return vt.at[(10 if a < 0 else 80) + (1 if b < 0 else 8)]

    def landing(a, b, row_ref, col_ref, corner_ref):
        if b == 0:
            return row_ref.at[1 if a < 0 else 0]
        if a == 0:
            return col_ref.at[1 if b < 0 else 0]
        return corner_ref.at[(2 if a < 0 else 0) + (1 if b < 0 else 0)]

    lane = lax.broadcasted_iota(jnp.int32, (128, 128), 1)
    own_lanes = [jnp.where(lane // 32 == m, 1.0, 0.0).astype(BF16) for m in range(4)]
    zero8 = jnp.zeros((8, 128), F32)
    one8 = jnp.ones((8, 128), F32)
    steps8 = lax.broadcasted_iota(jnp.int32, (8, 128), 0).astype(F32) - 3.5

    def place(i):
        return jnp.full((8, 128), i.astype(F32) - 3.5)

    def put_rows(ref, stride, values):
        for r, value in enumerate(values):
            ref[pl.ds(r, 8, stride=stride), :] = value

    def partner_tables(q, gi, gj, indices):
        ax, ay = q[0] + gi, q[1] + gj
        square = split3(lead * (ax * ax + ay * ay + q[2] * q[2]))
        values = [q[0]] * 3 + [q[1]] * 3 + [q[2]] * 3 + [gi] * 3 + [gj] * 3
        put_rows(stage_q, 32, values + list(square) + [one8] * 3)
        put_rows(stage_m, 8, [q[0], q[1], q[2], one8, gi, gj])
        for half in range((len(indices) + 3) // 4):
            turned = stage_q[128 * half : 128 * half + 128, :].T.astype(BF16)
            for m, index in enumerate(indices[4 * half : 4 * half + 4]):
                qf[index] = turned * own_lanes[m]
        for m, index in enumerate(indices):
            rows = stage_m[8 * m : 8 * m + 8, :]
            qm[index] = jnp.concatenate([rows, zero8], axis=0).astype(BF16)

    slots = lax.broadcasted_iota(jnp.int32, (128, 128), 0)
    for copy in small_loads:
        copy.wait()

    def prepare(i):
        q = [pos32[i, c] for c in range(3)]
        gi = place(i)
        partner_tables(q, gi, steps8, [(i + 1) * 10 + 1 + m for m in range(8)])
        ax, ay, az = q[0] + gi, q[1] + steps8, q[2]
        xs = list(split3(-2.0 * lead * ax))
        ys = list(split3(-2.0 * lead * ay))
        zs = list(split3(-2.0 * lead * az))
        sq = list(split3(lead * (ax * ax + ay * ay + az * az)))
        put_rows(stage_r, 32, xs + ys + zs + xs + ys + [one8] * 3 + sq)
        for m in range(8):
            rp[i * 8 + m] = stage_r[32 * m : 32 * m + 32, :].astype(BF16)
            here = slot[i, m : m + 1, :]
            oh[i * 8 + m] = jnp.where(slots == here, 1.0, 0.0).astype(BF16)


    pos_copies, v_copies = [], []

    buffers = [s_even.at[0], s_odd.at[0], s_even.at[1], s_odd.at[1]]

    def project(pair, s):
        ia, ja, ib, jb = pair
        both = jnp.concatenate([feat[ia, ja], feat[ib, jb]], axis=1)
        s[0:640, :] = mm(weights[...], both)

    def settle(pair, s):
        ia, ja, ib, jb = pair
        for i, j, lanes in ((ia, ja, slice(0, 128)), (ib, jb, slice(128, 256))):
            u[i * 8 + j] = s[0:512, lanes].astype(BF16)
            vt[(i + 1) * 10 + j + 1] = s[512:640, lanes].astype(BF16).T

    for copy in got_weights + rim_loads + inner_loads:
        copy.wait()
    start = [rim_then_inner(jnp.int32(p)) for p in range(5)]
    project(start[0], buffers[0])

    def project_four(q, carry, tables):
        for step in range(4):
            project(carry[step + 1], buffers[(step + 1) % 4])
            settle(carry[step], buffers[step])
            if tables and step % 2 == 0:
                prepare(2 * (q - 4) + step // 2)
        return carry[4:] + tuple(rim_then_inner(4 * q + p) for p in range(5, 9))

    rim_part = functools.partial(project_four, tables=False)
    carry = lax.fori_loop(0, 4, rim_part, tuple(start))
    pl.semaphore_wait(barrier, 8)

    def send_pos(src, dst, code):
        n = len(pos_copies)
        copy = pltpu.make_async_remote_copy(
            src_ref=src,
            dst_ref=dst,
            send_sem=pos_send.at[n],
            recv_sem=pos_recv.at[n],
            device_id=neighbour(code),
            device_id_type=MESH,
        )
        copy.start()
        pos_copies.append(copy)

    for code in CODES:
        a, b = code // 3 - 1, code % 3 - 1
        i, j = (0 if a < 0 else 7), (0 if b < 0 else 7)
        if b == 0:
            send_pos(pos32.at[i], pos_row.at[1 if a < 0 else 0], code)
        elif a == 0:
            for c in range(3):
                send_pos(pos32.at[:, c, j], pos_col.at[1 if b < 0 else 0, c], code)
        else:
            k = (2 if a < 0 else 0) + (1 if b < 0 else 0)
            send_pos(pos32.at[i, :, j], pos_corner.at[:, k], code)

    vt4 = vt.reshape(10, 10, 128, 128)
    for n, code in enumerate(CODES):
        a, b = code // 3 - 1, code % 3 - 1
        src = vt4.at[1:9, 1 if b < 0 else 8] if a == 0 else v_src(a, b)
        v_copies.append(
            pltpu.make_async_remote_copy(
                src_ref=src,
                dst_ref=landing(a, b, v_row, v_col, v_corner),
                send_sem=v_send.at[n],
                recv_sem=v_recv.at[n],
                device_id=neighbour(code),
                device_id_type=MESH,
            )
        )
    for n in sorted(range(8), key=lambda n: (CODES[n] // 3 == 1, CODES[n])):
        v_copies[n].start()

    lax.fori_loop(4, 8, functools.partial(project_four, tables=True), carry)

    def where_is(p):
        ia, ja, ib, jb = any_pair(p)
        found = [ia * 8 + ja, ib * 8 + jb]
        for i, j in ((ia, ja), (ib, jb)):
            for n in range(6):
                c = codes[n, i, j]
                found.append(i * 10 + j + c + 7 * ((c * 11) >> 5))
        return tuple(found)

    zeros128 = jnp.zeros((128, 128), BF16)

    def scores(at, s):
        for which in DOTS:
            if which == 4:
                rows = [jnp.concatenate([qf[n], qf[m]], axis=1) for n, m in zip(at[2:8], at[8:14])]
                right = jnp.concatenate(
                    [
                        jnp.concatenate([rp[at[0]]] * 4 + [zeros128], axis=0),
                        jnp.concatenate([zeros128] + [rp[at[1]]] * 4, axis=0),
                    ],
                    axis=1,
                )
            else:
                x, half = which // 2, which % 2
                rows = [vt[n] for n in at[2 + 6 * x : 8 + 6 * x]]
                first = u[at[x], 256 * half : 256 * half + 128, :]
                second = u[at[x], 256 * half + 128 : 256 * half + 256, :]
                right = jnp.concatenate([first, second], axis=1)
            s[which] = mm(jnp.concatenate(rows, axis=0), right)
            yield

    def couples(at, s):
        for x in range(2):
            t, found = at[x], at[2 + 6 * x : 8 + 6 * x]
            total = None
            for two in range(3):
                couple = []
                for n in (2 * two, 2 * two + 1):
                    rows = slice(n * 128, (n + 1) * 128)
                    t0 = s[4, rows, x * 128 : (x + 1) * 128]
                    mixed = None
                    for k in range(4):
                        score = s[2 * x + k // 2, rows, (k % 2) * 128 : (k % 2 + 1) * 128]
                        term = jnp.exp2(t0 if k == 0 else t0 * ratio[k]) * score
                        mixed = term if mixed is None else mixed + term
                    inside = jnp.maximum(t0 + four_lead, 0.0)
                    couple.append((mixed * (inside * inside)).astype(BF16))
                    yield
                left = jnp.concatenate([qm[found[2 * two]], qm[found[2 * two + 1]]], axis=1)
                got = mm(left, jnp.concatenate(couple, axis=0))
                total = got if total is None else total + got
            raw[pl.ds(pl.multiple_of(t * 8, 8), 8), :] = total[0:8]

    def run(steps):
        for _ in steps:
            pass

    def mixed_run(first, second):
        for which in MIX:
            next(first if which == "D" else second)
        run(first)
        run(second)

    def finish_halo():
        for copy in pos_copies:
            copy.wait_recv()
        for copy in v_copies:
            copy.wait_recv()

        def rows(side, carry):
            edge = place(9 * side - 1)
            at = [90 * side + 1 + m for m in range(8)]
            for m in range(8):
                vt[at[m]] = v_row[side, m]
            partner_tables([pos_row[side, c] for c in range(3)], edge, steps8, at)
            return carry

        def cols(side, carry):
            edge = place(9 * side - 1)
            at = [(m + 1) * 10 + 9 * side for m in range(8)]
            for m in range(8):
                vt[at[m]] = v_col[side, m]
            partner_tables([pos_col[side, c] for c in range(3)], steps8, edge, at)
            return carry

        lax.fori_loop(0, 2, rows, 0)
        lax.fori_loop(0, 2, cols, 0)
        k = lax.broadcasted_iota(jnp.int32, (8, 128), 0)
        gi = jnp.where(k < 2, -4.5, 4.5)
        gj = jnp.where(k % 2 == 0, -4.5, 4.5)
        at = [0, 9, 90, 99]
        for m in range(4):
            vt[at[m]] = v_corner[m]
        partner_tables([pos_corner[c] for c in range(3)], gi, gj, at)

    def force_terms():
        def row(i, carry):
            def strided(c):
                return raw[pl.ds(64 * i + c, 8, stride=8), :]

            weight = strided(3)
            px, py, pz = pos32[i, 0] + place(i), pos32[i, 1] + steps8, pos32[i, 2]
            lx, ly, lz = lever[i, 0], lever[i, 1], lever[i, 2]
            fx = (px * weight - (strided(0) + strided(4))) * final_scale
            fy = (py * weight - (strided(1) + strided(5))) * final_scale
            fz = (pz * weight - strided(2)) * final_scale
            rows = [fx, fy, fz, ly * fz - lz * fy, lz * fx - lx * fz, lx * fy - ly * fx]
            put = rows + [zero8] * 2
            for c, value in enumerate(put):
                high = value.astype(BF16).astype(F32)
                terms[pl.ds(128 * i + c, 8, stride=16), :] = high
                terms[pl.ds(128 * i + 8 + c, 8, stride=16), :] = value - high
            return carry

        lax.fori_loop(0, 8, row, 0)

    def part_terms(t):
        return terms[pl.ds(pl.multiple_of(t * 16, 16), 16), :]

    def masked_sums(places, start, count):
        left, right = [], []
        for i, j in places:
            t = i * 8 + j
            value = part_terms(t)
            whose = owner[i, pl.ds(j, 1), :]
            masks = [jnp.where(whose == start + c, value, 0.0) for c in range(count)]
            left.append(jnp.concatenate(masks, axis=0).astype(BF16))
            right.append(oh[t])
        got = mm_nt(jnp.concatenate(left, axis=1), jnp.concatenate(right, axis=1))
        where = pl.ds(pl.multiple_of(start * 16, 16), count * 16)
        acc[where, :] = acc[where, :] + got

    part_copies = []
    for n, code in enumerate(CODES):
        part_copies.append(
            pltpu.make_async_remote_copy(
                src_ref=part_out.at[code],
                dst_ref=part_in.at[code],
                send_sem=part_send.at[n],
                recv_sem=part_recv.at[n],
                device_id=neighbour(code),
                device_id_type=MESH,
            )
        )

    def send_parts():
        force_terms()

        def rows(side, carry):
            masked_sums([(7 * side, m) for m in range(8)], 3 * side, 6)
            return carry

        def cols(side, carry):
            masked_sums([(m, 7 * side) for m in range(1, 7)], 3 + side, 2)
            return carry

        lax.fori_loop(0, 2, rows, 0)
        lax.fori_loop(0, 2, cols, 0)
        for code in CODES:
            part_out[code] = acc[16 * code : 16 * code + 8, :] + acc[16 * code + 8 : 16 * code + 16, :]
        for copy in part_copies:
            copy.start()

    first = where_is(jnp.int32(0))
    run(scores(first, s_even))

    def two_pairs(q, carry):
        now, after = carry[:14], carry[14:]
        pl.when(q == INNER_FIRST // 2 - 1)(finish_halo)
        pl.when(q == INNER_FIRST // 2 + 7)(send_parts)
        later = where_is(2 * q + 2)
        last = where_is(2 * q + 3)
        mixed_run(scores(after, s_odd), couples(now, s_even))
        mixed_run(scores(later, s_even), couples(after, s_odd))
        return later + last

    carry = lax.fori_loop(0, 15, two_pairs, first + where_is(jnp.int32(1)))
    now, after = carry[:14], carry[14:]
    mixed_run(scores(after, s_odd), couples(now, s_even))
    run(couples(after, s_odd))

    force_terms()

    def inner_sums(q, total):
        left, right = [], []
        for i in (2 * q + 1, 2 * q + 2):
            for j in range(1, 7):
                left.append(part_terms(i * 8 + j).astype(BF16))
                right.append(oh[i * 8 + j])
        return total + mm_nt(jnp.concatenate(left, axis=1), jnp.concatenate(right, axis=1))

    own = lax.fori_loop(0, 3, inner_sums, acc[64:80, :])
    total = own[0:8] + own[8:16]
    for copy in part_copies:
        copy.wait_recv()
    for code in CODES:
        total = total + part_in[code]

    inv = inverse[0, 0]
    centre = [pose[0, c] for c in range(3)]
    quat = [pose[0, c] for c in range(3, 7)]
    vel = [motion[0, c] + STEP_DT * inv[0:1] * total[c : c + 1] for c in range(3)]
    ang = [motion[0, c] + STEP_DT * total[c : c + 1] for c in range(3, 6)]
    shift = [STEP_DT * v for v in vel]
    rot = rotation_rows(*quat)
    frame = [
        (rot[0][c] * ang[0] + rot[1][c] * ang[1] + rot[2][c] * ang[2]) * inv[c + 1 : c + 2]
        for c in range(3)
    ]
    omega = [rot[r][0] * frame[0] + rot[r][1] * frame[1] + rot[r][2] * frame[2] for r in range(3)]
    qw, qv = quat[0], quat[1:4]
    change = [
        -(omega[0] * qv[0] + omega[1] * qv[1] + omega[2] * qv[2]),
        qw * omega[0] + (omega[1] * qv[2] - omega[2] * qv[1]),
        qw * omega[1] + (omega[2] * qv[0] - omega[0] * qv[2]),
        qw * omega[2] + (omega[0] * qv[1] - omega[1] * qv[0]),
    ]
    stepped = [q + 0.5 * STEP_DT * d for q, d in zip(quat, change)]
    norm = jnp.sqrt(sum(s * s for s in stepped[1:]) + stepped[0] * stepped[0])
    turned = [s / norm for s in stepped]
    rot_new = rotation_rows(*turned)
    for c in range(3):
        table_f32[c : c + 1, :] = shift[c]
        for r in range(3):
            entry = sum(rot_new[r][k] * rot[c][k] for k in range(3))
            table_f32[3 * (c + 1) + r : 3 * (c + 1) + r + 1, :] = entry
    whole = table_f32[...]
    high = whole.astype(BF16)
    table[128:144, :] = high
    table[144:160, :] = (whole - high.astype(F32)).astype(BF16)
    table_copies = []
    for n, code in enumerate(CODES):
        table_copies.append(
            pltpu.make_async_remote_copy(
                src_ref=table.at[pl.ds(128, 32)],
                dst_ref=table.at[pl.ds((8 - code) * 32, 32)],
                send_sem=table_send.at[n],
                recv_sem=table_recv.at[n],
                device_id=neighbour(code),
                device_id_type=MESH,
            )
        )
    for copy in table_copies:
        copy.start()
    next_rows = [c + s for c, s in zip(centre, shift)] + turned + vel + ang
    for c, value in enumerate(next_rows):
        body_next[0, c] = value

    def look_up(places, start, count):
        if count == 1:
            rows = table[128:160, :]
        else:
            rows = table[pl.ds(pl.multiple_of(start * 32, 32), count * 32), :]
        tiles = [i * 8 + j for i, j in places]
        got = mm(rows, jnp.concatenate([oh[t] for t in tiles], axis=1))
        for n, (i, j) in enumerate(places):
            lanes = slice(128 * n, 128 * n + 128)
            found = None
            for c in range(count):
                one = got[32 * c : 32 * c + 16, lanes] + got[32 * c + 16 : 32 * c + 32, lanes]
                if c:
                    whose = owner[i, pl.ds(j, 1), :]
                    found = jnp.where(whose == start + c, one, found)
                else:
                    found = one
            picked[pl.ds(pl.multiple_of(tiles[n] * 16, 16), 16), :] = found

    def look_inner(i, carry):
        look_up([(i, j) for j in range(1, 7)], 4, 1)
        return carry

    lax.fori_loop(1, 7, look_inner, 0)
    for copy in table_copies:
        copy.wait_recv()

    def look_rows(q, carry):
        i, start = 7 * (q // 2), 3 * (q // 2)
        look_up([(i, 4 * (q % 2) + m) for m in range(4)], start, 6)
        return carry

    def look_cols(side, carry):
        look_up([(i, 7 * side) for i in range(1, 7)], 3 + side, 2)
        return carry

    lax.fori_loop(0, 4, look_rows, 0)
    lax.fori_loop(0, 2, look_cols, 0)

    def move(i, carry):
        def strided(c):
            return picked[pl.ds(128 * i + c, 8, stride=16), :]

        levers = [lever[i, c] for c in range(3)]
        for r in range(3):
            value = pos32[i, r] + strided(r)
            for c in range(3):
                value = value + strided(3 + 3 * c + r) * levers[c]
            moved[i, r] = value - levers[r]
        return carry

    lax.fori_loop(0, 8, move, 0)
    for copy in pos_copies + v_copies + part_copies + table_copies:
        copy.wait_send()


def hand_over(moved, body_next, moved_out, body_out, sem):
    copies = [
        pltpu.make_async_copy(moved, moved_out, sem.at[0]),
        pltpu.make_async_copy(body_next, body_out, sem.at[1]),
    ]
    for copy in copies:
        copy.start()
    for copy in copies:
        copy.wait()


def local(
    positions,
    features,
    lever,
    partner,
    body_slot,
    owner_dir,
    body_pose,
    body_motion,
    body_inverse,
    weight_u,
    weight_v,
    radial_rate,
):
    hbm = pl.BlockSpec(memory_space=pl.ANY)
    smem = pl.BlockSpec(memory_space=pltpu.SMEM)
    vmem = pl.BlockSpec(memory_space=pltpu.VMEM)
    dma = pltpu.SemaphoreType.DMA
    like = lambda x: pltpu.VMEM(x.shape, x.dtype)
    inside = lambda x: jnp.transpose(x, (0, 2, 1, 3))
    positions, lever = inside(positions), inside(lever)
    body_pose, body_motion = inside(body_pose), inside(body_motion)
    partner = jnp.transpose(partner, (2, 0, 1))
    moved, body_next = pl.pallas_call(
        kernel,
        out_shape=(
            pltpu.VMEM((8, 3, 8, 128), F32),
            pltpu.VMEM((1, 13, 1, 128), F32),
        ),
        in_specs=[smem, smem] + [hbm] * 10,
        out_specs=(vmem, vmem),
        scratch_shapes=[
            like(positions),
            like(features),
            like(lever),
            like(body_slot),
            like(owner_dir),
            like(body_pose),
            like(body_motion),
            like(body_inverse),
            pltpu.VMEM((640, 256), BF16),
            pltpu.VMEM((100, 128, 128), BF16),
            pltpu.VMEM((100, 128, 128), BF16),
            pltpu.VMEM((100, 16, 128), BF16),
            pltpu.VMEM((64, 32, 128), BF16),
            pltpu.VMEM((64, 512, 128), BF16),
            pltpu.VMEM((64, 128, 128), BF16),
            pltpu.VMEM((512, 128), F32),
            pltpu.VMEM((1024, 128), F32),
            pltpu.VMEM((1024, 128), F32),
            pltpu.VMEM((144, 128), F32),
            pltpu.VMEM((9, 8, 128), F32),
            pltpu.VMEM((9, 8, 128), F32),
            pltpu.VMEM((288, 128), BF16),
            pltpu.VMEM((16, 128), F32),
            pltpu.VMEM((8, 3, 8, 128), F32),
            pltpu.VMEM((256, 128), F32),
            pltpu.VMEM((256, 128), F32),
            pltpu.VMEM((64, 128), F32),
            pltpu.VMEM((2, 3, 8, 128), F32),
            pltpu.VMEM((2, 3, 8, 128), F32),
            pltpu.VMEM((3, 8, 128), F32),
            pltpu.VMEM((2, 8, 128, 128), BF16),
            pltpu.VMEM((2, 8, 128, 128), BF16),
            pltpu.VMEM((4, 128, 128), BF16),
            pltpu.VMEM((5, 768, 256), F32),
            pltpu.VMEM((5, 768, 256), F32),
            dma((24,)),
            dma((12,)),
            dma((12,)),
            dma((8,)),
            dma((8,)),
            dma((8,)),
            dma((8,)),
            dma((8,)),
            dma((8,)),
        ],
        compiler_params=pltpu.CompilerParams(
            collective_id=0, has_side_effects=True, vmem_limit_bytes=60 * 1024 * 1024
        ),
        name="step",
    )(
        partner,
        radial_rate,
        positions,
        features,
        lever,
        body_slot,
        owner_dir,
        body_pose,
        body_motion,
        body_inverse,
        weight_u,
        weight_v,
    )
    moved, body_next = pl.pallas_call(
        hand_over,
        out_shape=(
            jax.ShapeDtypeStruct((8, 3, 8, 128), F32),
            jax.ShapeDtypeStruct((1, 13, 1, 128), F32),
        ),
        in_specs=[vmem, vmem],
        out_specs=(hbm, hbm),
        scratch_shapes=[dma((2,))],
        name="out",
    )(
        pltpu.with_memory_space_constraint(moved, pltpu.VMEM),
        pltpu.with_memory_space_constraint(body_next, pltpu.VMEM),
    )
    return inside(moved), inside(body_next)


def solution(mesh):
    tiles = P("gx", "gy", None, None)
    flat = P("gx", "gy", None)
    return jax.shard_map(
        local,
        mesh=mesh,
        in_specs=(tiles, tiles, tiles, flat, flat, flat, tiles, tiles, tiles, P(), P(), P()),
        out_specs=(tiles, tiles),
        check_vma=False,
    )
```

```python
import functools

import jax
import jax.numpy as jnp
from jax import lax
from jax.experimental import pallas as pl
from jax.experimental.pallas import tpu as pltpu
from jax.sharding import PartitionSpec as P

STEP_DT = 0.25
LOG2E = 1.4426950408889634
MESH = pl.DeviceIdType.MESH
F32 = jnp.float32
BF16 = jnp.bfloat16
INNER_FIRST = 14
CODES = [c for c in range(9) if c != 4]
MIX = "DUUDUUDUUDUUDUU"
DOTS = (0, 1, 2, 3, 4)


def mm(a, b):
    return jnp.dot(a, b, preferred_element_type=F32)


def mm_nt(a, b):
    return lax.dot_general(a, b, (((1,), (1,)), ((), ())), preferred_element_type=F32)


def split3(value):
    high = value.astype(BF16).astype(F32)
    rest = value - high
    mid = rest.astype(BF16).astype(F32)
    return high, mid, rest - mid


def inner_pair(q):
    i = 1 + q // 3
    j = 1 + 2 * (q % 3)
    return i, j, i, j + 1


def rim_pair(q):
    in_rows = q < 8
    c = q - 8
    i = jnp.where(in_rows, 7 * (q // 4), 1 + 2 * (c % 3))
    j = jnp.where(in_rows, 2 * (q % 4), 7 * (c // 3))
    return i, j, jnp.where(in_rows, i, i + 1), jnp.where(in_rows, j + 1, j)


def row_pair(q):
    i = 7 * (q // 4)
    j = 2 * (q % 4)
    return i, j, i, j + 1


def col_pair(q):
    i = 1 + 2 * (q % 3)
    j = 7 * (q // 3)
    return i, j, i + 1, j


def rim_then_inner(p):
    rim = rim_pair(jnp.clip(p, 0, 13))
    inner = inner_pair(jnp.clip(p - 14, 0, 17))
    return tuple(jnp.where(p < 14, r, n) for r, n in zip(rim, inner))


def any_pair(p):
    rim = rim_pair(jnp.clip(p - INNER_FIRST, 0, 13))
    inner = inner_pair(jnp.clip(jnp.where(p < INNER_FIRST, p, p - 14), 0, 17))
    is_rim = (p >= INNER_FIRST) & (p < INNER_FIRST + 14)
    return tuple(jnp.where(is_rim, r, n) for r, n in zip(rim, inner))


def rotation_rows(qw, qa, qb, qc):
    return [
        [1 - 2 * (qb * qb + qc * qc), 2 * (qa * qb - qw * qc), 2 * (qa * qc + qw * qb)],
        [2 * (qa * qb + qw * qc), 1 - 2 * (qa * qa + qc * qc), 2 * (qb * qc - qw * qa)],
        [2 * (qa * qc - qw * qb), 2 * (qb * qc + qw * qa), 1 - 2 * (qa * qa + qb * qb)],
    ]


def kernel(
    codes,
    rates,
    positions,
    features,
    lever_in,
    slot_in,
    owner_in,
    pose_in,
    motion_in,
    inverse_in,
    wu_in,
    wv_in,
    moved,
    body_next,
    pos,
    feat,
    lever,
    slot,
    owner,
    pose,
    motion,
    inverse,
    weights,
    vt,
    qf,
    qm,
    rp,
    u,
    oh,
    raw,
    terms,
    picked,
    acc,
    part_out,
    part_in,
    table,
    table_f32,
    pos32,
    stage_q,
    stage_r,
    stage_m,
    stage_n,
    pos_row,
    pos_col,
    pos_corner,
    v_row,
    v_col,
    v_corner,
    s_even,
    s_odd,
    in_sem,
    pos_send,
    pos_recv,
    v_send,
    v_recv,
    part_send,
    part_recv,
    table_send,
    table_recv,
):
    gx, gy = lax.axis_index("gx"), lax.axis_index("gy")
    nx, ny = lax.axis_size("gx"), lax.axis_size("gy")

    def neighbour(code):
        a, b = code // 3 - 1, code % 3 - 1
        return (lax.rem(gx + a + nx, nx), lax.rem(gy + b + ny, ny))

    loads = []

    def load(src, dst):
        copy = pltpu.make_async_copy(src, dst, in_sem.at[len(loads)])
        copy.start()
        loads.append(copy)
        return copy

    got_pos = load(positions, pos)
    got_weights = [load(wu_in, weights.at[0:512]), load(wv_in, weights.at[512:640])]
    rim_loads = [
        load(features.at[0], feat.at[0]),
        load(features.at[7], feat.at[7]),
        load(features.at[1:7, 0], feat.at[1:7, 0]),
        load(features.at[1:7, 7], feat.at[1:7, 7]),
    ]
    small_loads = [
        load(slot_in, slot),
        load(owner_in, owner),
        load(lever_in, lever),
        load(pose_in, pose),
        load(motion_in, motion),
        load(inverse_in, inverse),
    ]
    inner_loads = [load(features.at[i, 1:7], feat.at[i, 1:7]) for i in range(1, 7)]

    barrier = pltpu.get_barrier_semaphore()
    for code in CODES:
        pl.semaphore_signal(barrier, inc=1, device_id=neighbour(code), device_id_type=MESH)

    rate_scale = [rates[k] * (-LOG2E) for k in range(4)]
    lead = rate_scale[0]
    ratio = [None] + [rate_scale[k] / lead for k in range(1, 4)]
    four_lead = -4.0 * lead
    final_scale = 1.0 / (2048.0 * lead * lead)
    raw[...] = jnp.zeros_like(raw)
    acc[...] = jnp.zeros_like(acc)
    stage_q[...] = jnp.zeros_like(stage_q)
    stage_r[...] = jnp.zeros_like(stage_r)
    stage_m[...] = jnp.zeros_like(stage_m)
    stage_n[...] = jnp.zeros_like(stage_n)
    table_f32[...] = jnp.zeros_like(table_f32)

    got_pos.wait()
    pos32[...] = pos[...].astype(F32)

    def v_src(a, b):
        if b == 0:
            return vt.at[pl.ds(11 if a < 0 else 81, 8)]
        if a == 0:
            return None
        return vt.at[(10 if a < 0 else 80) + (1 if b < 0 else 8)]

    def landing(a, b, row_ref, col_ref, corner_ref):
        if b == 0:
            return row_ref.at[1 if a < 0 else 0]
        if a == 0:
            return col_ref.at[1 if b < 0 else 0]
        return corner_ref.at[(2 if a < 0 else 0) + (1 if b < 0 else 0)]

    lane = lax.broadcasted_iota(jnp.int32, (128, 128), 1)
    own_lanes = [jnp.where(lane // 32 == m, 1.0, 0.0).astype(BF16) for m in range(4)]
    zero8 = jnp.zeros((8, 128), F32)
    one8 = jnp.ones((8, 128), F32)
    steps8 = lax.broadcasted_iota(jnp.int32, (8, 128), 0).astype(F32) - 3.5

    def place(i):
        return jnp.full((8, 128), i.astype(F32) - 3.5)

    def put_rows(ref, stride, values):
        for r, value in enumerate(values):
            ref[pl.ds(r, 8, stride=stride), :] = value

    def partner_tables(q, gi, gj, indices, wide=stage_q, narrow=stage_m):
        ax, ay = q[0] + gi, q[1] + gj
        square = split3(lead * (ax * ax + ay * ay + q[2] * q[2]))
        values = [q[0]] * 3 + [q[1]] * 3 + [q[2]] * 3 + [gi] * 3 + [gj] * 3
        put_rows(wide, 32, values + list(square) + [one8] * 3)
        put_rows(narrow, 8, [q[0], q[1], q[2], one8, gi, gj])
        for half in range((len(indices) + 3) // 4):
            turned = wide[128 * half : 128 * half + 128, :].T.astype(BF16)
            for m, index in enumerate(indices[4 * half : 4 * half + 4]):
                qf[index] = turned * own_lanes[m]
        for m, index in enumerate(indices):
            rows = narrow[8 * m : 8 * m + 8, :]
            qm[index] = jnp.concatenate([rows, zero8], axis=0).astype(BF16)

    slots = lax.broadcasted_iota(jnp.int32, (128, 128), 0)
    for copy in small_loads:
        copy.wait()

    def prepare(i):
        q = [pos32[i, c] for c in range(3)]
        gi = place(i)
        partner_tables(q, gi, steps8, [(i + 1) * 10 + 1 + m for m in range(8)])
        ax, ay, az = q[0] + gi, q[1] + steps8, q[2]
        xs = list(split3(-2.0 * lead * ax))
        ys = list(split3(-2.0 * lead * ay))
        zs = list(split3(-2.0 * lead * az))
        sq = list(split3(lead * (ax * ax + ay * ay + az * az)))
        put_rows(stage_r, 32, xs + ys + zs + xs + ys + [one8] * 3 + sq)
        for m in range(8):
            rp[i * 8 + m] = stage_r[32 * m : 32 * m + 32, :].astype(BF16)
            here = slot[i, m : m + 1, :]
            oh[i * 8 + m] = jnp.where(slots == here, 1.0, 0.0).astype(BF16)


    pos_copies, v_copies = [], []

    buffers = [s_even.at[0], s_odd.at[0], s_even.at[1], s_odd.at[1]]

    def project(pair, s):
        ia, ja, ib, jb = pair
        both = jnp.concatenate([feat[ia, ja], feat[ib, jb]], axis=1)
        s[0:640, :] = mm(weights[...], both)

    def settle(pair, s):
        ia, ja, ib, jb = pair
        for i, j, lanes in ((ia, ja, slice(0, 128)), (ib, jb, slice(128, 256))):
            u[i * 8 + j] = s[0:512, lanes].astype(BF16)
            vt[(i + 1) * 10 + j + 1] = s[512:640, lanes].astype(BF16).T

    for copy in got_weights + rim_loads + inner_loads[:1]:
        copy.wait()
    start = [rim_then_inner(jnp.int32(p)) for p in range(5)]
    project(start[0], buffers[0])

    def project_four(q, carry, tables):
        for step in range(4):
            project(carry[step + 1], buffers[(step + 1) % 4])
            settle(carry[step], buffers[step])
            if tables and step % 2 == 0:
                prepare(2 * (q - 4) + step // 2)
        return carry[4:] + tuple(rim_then_inner(4 * q + p) for p in range(5, 9))

    rim_part = functools.partial(project_four, tables=False)
    carry = lax.fori_loop(0, 4, rim_part, tuple(start))
    pl.semaphore_wait(barrier, 8)

    def send_pos(src, dst, code):
        n = len(pos_copies)
        copy = pltpu.make_async_remote_copy(
            src_ref=src,
            dst_ref=dst,
            send_sem=pos_send.at[n],
            recv_sem=pos_recv.at[n],
            device_id=neighbour(code),
            device_id_type=MESH,
        )
        copy.start()
        pos_copies.append(copy)

    for code in CODES:
        a, b = code // 3 - 1, code % 3 - 1
        i, j = (0 if a < 0 else 7), (0 if b < 0 else 7)
        if b == 0:
            send_pos(pos32.at[i], pos_row.at[1 if a < 0 else 0], code)
        elif a == 0:
            for c in range(3):
                send_pos(pos32.at[:, c, j], pos_col.at[1 if b < 0 else 0, c], code)
        else:
            k = (2 if a < 0 else 0) + (1 if b < 0 else 0)
            send_pos(pos32.at[i, :, j], pos_corner.at[:, k], code)

    vt4 = vt.reshape(10, 10, 128, 128)
    for n, code in enumerate(CODES):
        a, b = code // 3 - 1, code % 3 - 1
        src = vt4.at[1:9, 1 if b < 0 else 8] if a == 0 else v_src(a, b)
        v_copies.append(
            pltpu.make_async_remote_copy(
                src_ref=src,
                dst_ref=landing(a, b, v_row, v_col, v_corner),
                send_sem=v_send.at[n],
                recv_sem=v_recv.at[n],
                device_id=neighbour(code),
                device_id_type=MESH,
            )
        )
    for n in sorted(range(8), key=lambda n: (CODES[n] // 3 == 1, CODES[n])):
        v_copies[n].start()

    for copy in inner_loads[1:]:
        copy.wait()
    lax.fori_loop(4, 8, functools.partial(project_four, tables=True), carry)

    def where_is(p):
        ia, ja, ib, jb = any_pair(p)
        found = [ia * 8 + ja, ib * 8 + jb]
        for i, j in ((ia, ja), (ib, jb)):
            for n in range(6):
                c = codes[n, i, j]
                found.append(i * 10 + j + c + 7 * ((c * 11) >> 5))
        return tuple(found)

    zeros128 = jnp.zeros((128, 128), BF16)

    def scores(at, s):
        for which in DOTS:
            if which == 4:
                rows = [jnp.concatenate([qf[n], qf[m]], axis=1) for n, m in zip(at[2:8], at[8:14])]
                right = jnp.concatenate(
                    [
                        jnp.concatenate([rp[at[0]]] * 4 + [zeros128], axis=0),
                        jnp.concatenate([zeros128] + [rp[at[1]]] * 4, axis=0),
                    ],
                    axis=1,
                )
            else:
                x, half = which // 2, which % 2
                rows = [vt[n] for n in at[2 + 6 * x : 8 + 6 * x]]
                first = u[at[x], 256 * half : 256 * half + 128, :]
                second = u[at[x], 256 * half + 128 : 256 * half + 256, :]
                right = jnp.concatenate([first, second], axis=1)
            s[which] = mm(jnp.concatenate(rows, axis=0), right)
            yield

    def couples(at, s):
        for x in range(2):
            t, found = at[x], at[2 + 6 * x : 8 + 6 * x]
            total = None
            for two in range(3):
                couple = []
                for n in (2 * two, 2 * two + 1):
                    rows = slice(n * 128, (n + 1) * 128)
                    t0 = s[4, rows, x * 128 : (x + 1) * 128]
                    mixed = None
                    for k in range(4):
                        score = s[2 * x + k // 2, rows, (k % 2) * 128 : (k % 2 + 1) * 128]
                        term = jnp.exp2(t0 if k == 0 else t0 * ratio[k]) * score
                        mixed = term if mixed is None else mixed + term
                    inside = jnp.maximum(t0 + four_lead, 0.0)
                    couple.append((mixed * (inside * inside)).astype(BF16))
                    yield
                left = jnp.concatenate([qm[found[2 * two]], qm[found[2 * two + 1]]], axis=1)
                got = mm(left, jnp.concatenate(couple, axis=0))
                total = got if total is None else total + got
            raw[pl.ds(pl.multiple_of(t * 8, 8), 8), :] = total[0:8]

    def run(steps):
        for _ in steps:
            pass

    def mixed_run(first, second):
        for which in MIX:
            next(first if which == "D" else second)
        run(first)
        run(second)

    def finish_halo():
        for copy in pos_copies:
            copy.wait_recv()
        for copy in v_copies:
            copy.wait_recv()

        def sides(side, carry):
            edge = place(9 * side - 1)
            in_row = [90 * side + 1 + m for m in range(8)]
            in_col = [(m + 1) * 10 + 9 * side for m in range(8)]
            along = [pos_row[side, c] for c in range(3)]
            across = [pos_col[side, c] for c in range(3)]
            partner_tables(along, edge, steps8, in_row)
            partner_tables(across, steps8, edge, in_col, stage_r, stage_n)
            for m in range(8):
                vt[in_row[m]] = v_row[side, m]
                vt[in_col[m]] = v_col[side, m]
            return carry

        lax.fori_loop(0, 2, sides, 0)
        k = lax.broadcasted_iota(jnp.int32, (8, 128), 0)
        gi = jnp.where(k < 2, -4.5, 4.5)
        gj = jnp.where(k % 2 == 0, -4.5, 4.5)
        at = [0, 9, 90, 99]
        for m in range(4):
            vt[at[m]] = v_corner[m]
        partner_tables([pos_corner[c] for c in range(3)], gi, gj, at)

    def force_terms():
        def row(i, carry):
            def strided(c):
                return raw[pl.ds(64 * i + c, 8, stride=8), :]

            weight = strided(3)
            px, py, pz = pos32[i, 0] + place(i), pos32[i, 1] + steps8, pos32[i, 2]
            lx, ly, lz = lever[i, 0], lever[i, 1], lever[i, 2]
            fx = (px * weight - (strided(0) + strided(4))) * final_scale
            fy = (py * weight - (strided(1) + strided(5))) * final_scale
            fz = (pz * weight - strided(2)) * final_scale
            rows = [fx, fy, fz, ly * fz - lz * fy, lz * fx - lx * fz, lx * fy - ly * fx]
            put = rows + [zero8] * 2
            for c, value in enumerate(put):
                high = value.astype(BF16).astype(F32)
                terms[pl.ds(128 * i + c, 8, stride=16), :] = high
                terms[pl.ds(128 * i + 8 + c, 8, stride=16), :] = value - high
            return carry

        lax.fori_loop(0, 8, row, 0)

    def part_terms(t):
        return terms[pl.ds(pl.multiple_of(t * 16, 16), 16), :]

    def masked_sums(places, start, count):
        left, right = [], []
        for i, j in places:
            t = i * 8 + j
            value = part_terms(t)
            whose = owner[i, pl.ds(j, 1), :]
            masks = [jnp.where(whose == start + c, value, 0.0) for c in range(count)]
            left.append(jnp.concatenate(masks, axis=0).astype(BF16))
            right.append(oh[t])
        got = mm_nt(jnp.concatenate(left, axis=1), jnp.concatenate(right, axis=1))
        where = pl.ds(pl.multiple_of(start * 16, 16), count * 16)
        acc[where, :] = acc[where, :] + got

    part_copies = []
    for n, code in enumerate(CODES):
        part_copies.append(
            pltpu.make_async_remote_copy(
                src_ref=part_out.at[code],
                dst_ref=part_in.at[code],
                send_sem=part_send.at[n],
                recv_sem=part_recv.at[n],
                device_id=neighbour(code),
                device_id_type=MESH,
            )
        )

    def send_parts():
        force_terms()

        def rows(side, carry):
            masked_sums([(7 * side, m) for m in range(8)], 3 * side, 6)
            return carry

        def cols(side, carry):
            masked_sums([(m, 7 * side) for m in range(1, 7)], 3 + side, 2)
            return carry

        lax.fori_loop(0, 2, rows, 0)
        lax.fori_loop(0, 2, cols, 0)
        for code in CODES:
            part_out[code] = acc[16 * code : 16 * code + 8, :] + acc[16 * code + 8 : 16 * code + 16, :]
        for copy in part_copies:
            copy.start()

    first = where_is(jnp.int32(0))
    run(scores(first, s_even))

    def two_pairs(q, carry):
        now, after = carry[:14], carry[14:]
        pl.when(q == INNER_FIRST // 2 - 1)(finish_halo)
        pl.when(q == INNER_FIRST // 2 + 7)(send_parts)
        later = where_is(2 * q + 2)
        last = where_is(2 * q + 3)
        mixed_run(scores(after, s_odd), couples(now, s_even))
        mixed_run(scores(later, s_even), couples(after, s_odd))
        return later + last

    carry = lax.fori_loop(0, 15, two_pairs, first + where_is(jnp.int32(1)))
    now, after = carry[:14], carry[14:]
    mixed_run(scores(after, s_odd), couples(now, s_even))
    run(couples(after, s_odd))

    force_terms()

    def inner_sums(q, total):
        left, right = [], []
        for i in (2 * q + 1, 2 * q + 2):
            for j in range(1, 7):
                left.append(part_terms(i * 8 + j).astype(BF16))
                right.append(oh[i * 8 + j])
        return total + mm_nt(jnp.concatenate(left, axis=1), jnp.concatenate(right, axis=1))

    own = lax.fori_loop(0, 3, inner_sums, acc[64:80, :])
    total = own[0:8] + own[8:16]
    for copy in part_copies:
        copy.wait_recv()
    for code in CODES:
        total = total + part_in[code]

    inv = inverse[0, 0]
    centre = [pose[0, c] for c in range(3)]
    quat = [pose[0, c] for c in range(3, 7)]
    vel = [motion[0, c] + STEP_DT * inv[0:1] * total[c : c + 1] for c in range(3)]
    ang = [motion[0, c] + STEP_DT * total[c : c + 1] for c in range(3, 6)]
    shift = [STEP_DT * v for v in vel]
    rot = rotation_rows(*quat)
    frame = [
        (rot[0][c] * ang[0] + rot[1][c] * ang[1] + rot[2][c] * ang[2]) * inv[c + 1 : c + 2]
        for c in range(3)
    ]
    omega = [rot[r][0] * frame[0] + rot[r][1] * frame[1] + rot[r][2] * frame[2] for r in range(3)]
    qw, qv = quat[0], quat[1:4]
    change = [
        -(omega[0] * qv[0] + omega[1] * qv[1] + omega[2] * qv[2]),
        qw * omega[0] + (omega[1] * qv[2] - omega[2] * qv[1]),
        qw * omega[1] + (omega[2] * qv[0] - omega[0] * qv[2]),
        qw * omega[2] + (omega[0] * qv[1] - omega[1] * qv[0]),
    ]
    stepped = [q + 0.5 * STEP_DT * d for q, d in zip(quat, change)]
    norm = jnp.sqrt(sum(s * s for s in stepped[1:]) + stepped[0] * stepped[0])
    turned = [s / norm for s in stepped]
    rot_new = rotation_rows(*turned)
    for c in range(3):
        table_f32[c : c + 1, :] = shift[c]
        for r in range(3):
            entry = sum(rot_new[r][k] * rot[c][k] for k in range(3))
            table_f32[3 * (c + 1) + r : 3 * (c + 1) + r + 1, :] = entry
    whole = table_f32[...]
    high = whole.astype(BF16)
    table[128:144, :] = high
    table[144:160, :] = (whole - high.astype(F32)).astype(BF16)
    table_copies = []
    for n, code in enumerate(CODES):
        table_copies.append(
            pltpu.make_async_remote_copy(
                src_ref=table.at[pl.ds(128, 32)],
                dst_ref=table.at[pl.ds((8 - code) * 32, 32)],
                send_sem=table_send.at[n],
                recv_sem=table_recv.at[n],
                device_id=neighbour(code),
                device_id_type=MESH,
            )
        )
    for copy in table_copies:
        copy.start()
    next_rows = [c + s for c, s in zip(centre, shift)] + turned + vel + ang
    for c, value in enumerate(next_rows):
        body_next[0, c] = value

    def look_up(places, start, count):
        if count == 1:
            rows = table[128:160, :]
        else:
            rows = table[pl.ds(pl.multiple_of(start * 32, 32), count * 32), :]
        tiles = [i * 8 + j for i, j in places]
        got = mm(rows, jnp.concatenate([oh[t] for t in tiles], axis=1))
        for n, (i, j) in enumerate(places):
            lanes = slice(128 * n, 128 * n + 128)
            found = None
            for c in range(count):
                one = got[32 * c : 32 * c + 16, lanes] + got[32 * c + 16 : 32 * c + 32, lanes]
                if c:
                    whose = owner[i, pl.ds(j, 1), :]
                    found = jnp.where(whose == start + c, one, found)
                else:
                    found = one
            picked[pl.ds(pl.multiple_of(tiles[n] * 16, 16), 16), :] = found

    def look_inner(i, carry):
        look_up([(i, j) for j in range(1, 7)], 4, 1)
        return carry

    lax.fori_loop(1, 7, look_inner, 0)
    for copy in table_copies:
        copy.wait_recv()

    def look_rows(q, carry):
        i, start = 7 * (q // 2), 3 * (q // 2)
        look_up([(i, 4 * (q % 2) + m) for m in range(4)], start, 6)
        return carry

    def look_cols(side, carry):
        look_up([(i, 7 * side) for i in range(1, 7)], 3 + side, 2)
        return carry

    lax.fori_loop(0, 4, look_rows, 0)
    lax.fori_loop(0, 2, look_cols, 0)

    def move(i, carry):
        def strided(c):
            return picked[pl.ds(128 * i + c, 8, stride=16), :]

        levers = [lever[i, c] for c in range(3)]
        for r in range(3):
            value = pos32[i, r] + strided(r)
            for c in range(3):
                value = value + strided(3 + 3 * c + r) * levers[c]
            moved[i, r] = value - levers[r]
        return carry

    lax.fori_loop(0, 8, move, 0)
    for copy in pos_copies + v_copies + part_copies + table_copies:
        copy.wait_send()


def hand_over(moved, body_next, moved_out, body_out, sem):
    copies = [
        pltpu.make_async_copy(moved, moved_out, sem.at[0]),
        pltpu.make_async_copy(body_next, body_out, sem.at[1]),
    ]
    for copy in copies:
        copy.start()
    for copy in copies:
        copy.wait()


def local(
    positions,
    features,
    lever,
    partner,
    body_slot,
    owner_dir,
    body_pose,
    body_motion,
    body_inverse,
    weight_u,
    weight_v,
    radial_rate,
):
    hbm = pl.BlockSpec(memory_space=pl.ANY)
    smem = pl.BlockSpec(memory_space=pltpu.SMEM)
    vmem = pl.BlockSpec(memory_space=pltpu.VMEM)
    dma = pltpu.SemaphoreType.DMA
    like = lambda x: pltpu.VMEM(x.shape, x.dtype)
    inside = lambda x: jnp.transpose(x, (0, 2, 1, 3))
    positions, lever = inside(positions), inside(lever)
    body_pose, body_motion = inside(body_pose), inside(body_motion)
    partner = jnp.transpose(partner, (2, 0, 1))
    moved, body_next = pl.pallas_call(
        kernel,
        out_shape=(
            pltpu.VMEM((8, 3, 8, 128), F32),
            pltpu.VMEM((1, 13, 1, 128), F32),
        ),
        in_specs=[smem, smem] + [hbm] * 10,
        out_specs=(vmem, vmem),
        scratch_shapes=[
            like(positions),
            like(features),
            like(lever),
            like(body_slot),
            like(owner_dir),
            like(body_pose),
            like(body_motion),
            like(body_inverse),
            pltpu.VMEM((640, 256), BF16),
            pltpu.VMEM((100, 128, 128), BF16),
            pltpu.VMEM((100, 128, 128), BF16),
            pltpu.VMEM((100, 16, 128), BF16),
            pltpu.VMEM((64, 32, 128), BF16),
            pltpu.VMEM((64, 512, 128), BF16),
            pltpu.VMEM((64, 128, 128), BF16),
            pltpu.VMEM((512, 128), F32),
            pltpu.VMEM((1024, 128), F32),
            pltpu.VMEM((1024, 128), F32),
            pltpu.VMEM((144, 128), F32),
            pltpu.VMEM((9, 8, 128), F32),
            pltpu.VMEM((9, 8, 128), F32),
            pltpu.VMEM((288, 128), BF16),
            pltpu.VMEM((16, 128), F32),
            pltpu.VMEM((8, 3, 8, 128), F32),
            pltpu.VMEM((256, 128), F32),
            pltpu.VMEM((256, 128), F32),
            pltpu.VMEM((64, 128), F32),
            pltpu.VMEM((64, 128), F32),
            pltpu.VMEM((2, 3, 8, 128), F32),
            pltpu.VMEM((2, 3, 8, 128), F32),
            pltpu.VMEM((3, 8, 128), F32),
            pltpu.VMEM((2, 8, 128, 128), BF16),
            pltpu.VMEM((2, 8, 128, 128), BF16),
            pltpu.VMEM((4, 128, 128), BF16),
            pltpu.VMEM((5, 768, 256), F32),
            pltpu.VMEM((5, 768, 256), F32),
            dma((24,)),
            dma((12,)),
            dma((12,)),
            dma((8,)),
            dma((8,)),
            dma((8,)),
            dma((8,)),
            dma((8,)),
            dma((8,)),
        ],
        compiler_params=pltpu.CompilerParams(
            collective_id=0, has_side_effects=True, vmem_limit_bytes=60 * 1024 * 1024
        ),
        name="step",
    )(
        partner,
        radial_rate,
        positions,
        features,
        lever,
        body_slot,
        owner_dir,
        body_pose,
        body_motion,
        body_inverse,
        weight_u,
        weight_v,
    )
    moved, body_next = pl.pallas_call(
        hand_over,
        out_shape=(
            jax.ShapeDtypeStruct((8, 3, 8, 128), F32),
            jax.ShapeDtypeStruct((1, 13, 1, 128), F32),
        ),
        in_specs=[vmem, vmem],
        out_specs=(hbm, hbm),
        scratch_shapes=[dma((2,))],
        name="out",
    )(
        pltpu.with_memory_space_constraint(moved, pltpu.VMEM),
        pltpu.with_memory_space_constraint(body_next, pltpu.VMEM),
    )
    return inside(moved), inside(body_next)


def solution(mesh):
    tiles = P("gx", "gy", None, None)
    flat = P("gx", "gy", None)
    return jax.shard_map(
        local,
        mesh=mesh,
        in_specs=(tiles, tiles, tiles, flat, flat, flat, tiles, tiles, tiles, P(), P(), P()),
        out_specs=(tiles, tiles),
        check_vma=False,
    )
```

```python
import functools

import jax
import jax.numpy as jnp
from jax import lax
from jax.experimental import pallas as pl
from jax.experimental.pallas import tpu as pltpu
from jax.sharding import PartitionSpec as P

STEP_DT = 0.25
LOG2E = 1.4426950408889634
MESH = pl.DeviceIdType.MESH
F32 = jnp.float32
BF16 = jnp.bfloat16
INNER_FIRST = 13
CODES = [c for c in range(9) if c != 4]
MIX = "DUUDUUDUUDUUDUU"
DOTS = (0, 1, 2, 3, 4)


def mm(a, b):
    return jnp.dot(a, b, preferred_element_type=F32)


def mm_nt(a, b):
    return lax.dot_general(a, b, (((1,), (1,)), ((), ())), preferred_element_type=F32)


def split3(value):
    high = value.astype(BF16).astype(F32)
    rest = value - high
    mid = rest.astype(BF16).astype(F32)
    return high, mid, rest - mid


def inner_pair(q):
    i = 1 + q // 3
    j = 1 + 2 * (q % 3)
    return i, j, i, j + 1


def rim_pair(q):
    in_rows = q < 8
    c = q - 8
    i = jnp.where(in_rows, 7 * (q // 4), 1 + 2 * (c % 3))
    j = jnp.where(in_rows, 2 * (q % 4), 7 * (c // 3))
    return i, j, jnp.where(in_rows, i, i + 1), jnp.where(in_rows, j + 1, j)


def row_pair(q):
    i = 7 * (q // 4)
    j = 2 * (q % 4)
    return i, j, i, j + 1


def col_pair(q):
    i = 1 + 2 * (q % 3)
    j = 7 * (q // 3)
    return i, j, i + 1, j


def rim_then_inner(p):
    rim = rim_pair(jnp.clip(p, 0, 13))
    inner = inner_pair(jnp.clip(p - 14, 0, 17))
    return tuple(jnp.where(p < 14, r, n) for r, n in zip(rim, inner))


def any_pair(p):
    rim = rim_pair(jnp.clip(p - INNER_FIRST, 0, 13))
    inner = inner_pair(jnp.clip(jnp.where(p < INNER_FIRST, p, p - 14), 0, 17))
    is_rim = (p >= INNER_FIRST) & (p < INNER_FIRST + 14)
    return tuple(jnp.where(is_rim, r, n) for r, n in zip(rim, inner))


def rotation_rows(qw, qa, qb, qc):
    return [
        [1 - 2 * (qb * qb + qc * qc), 2 * (qa * qb - qw * qc), 2 * (qa * qc + qw * qb)],
        [2 * (qa * qb + qw * qc), 1 - 2 * (qa * qa + qc * qc), 2 * (qb * qc - qw * qa)],
        [2 * (qa * qc - qw * qb), 2 * (qb * qc + qw * qa), 1 - 2 * (qa * qa + qb * qb)],
    ]


def kernel(
    codes,
    rates,
    positions,
    features,
    lever_in,
    slot_in,
    owner_in,
    pose_in,
    motion_in,
    inverse_in,
    wu_in,
    wv_in,
    moved,
    body_next,
    pos,
    feat,
    lever,
    slot,
    owner,
    pose,
    motion,
    inverse,
    weights,
    vt,
    qf,
    qm,
    rp,
    u,
    oh,
    raw,
    terms,
    picked,
    acc,
    part_out,
    part_in,
    table,
    table_f32,
    pos32,
    stage_q,
    stage_r,
    stage_m,
    stage_n,
    pos_row,
    pos_col,
    pos_corner,
    v_row,
    v_col,
    v_corner,
    s_even,
    s_odd,
    in_sem,
    pos_send,
    pos_recv,
    v_send,
    v_recv,
    part_send,
    part_recv,
    table_send,
    table_recv,
):
    gx, gy = lax.axis_index("gx"), lax.axis_index("gy")
    nx, ny = lax.axis_size("gx"), lax.axis_size("gy")

    def neighbour(code):
        a, b = code // 3 - 1, code % 3 - 1
        return (lax.rem(gx + a + nx, nx), lax.rem(gy + b + ny, ny))

    loads = []

    def load(src, dst):
        copy = pltpu.make_async_copy(src, dst, in_sem.at[len(loads)])
        copy.start()
        loads.append(copy)
        return copy

    got_pos = load(positions, pos)
    got_weights = [load(wu_in, weights.at[0:512]), load(wv_in, weights.at[512:640])]
    rim_loads = [
        load(features.at[0], feat.at[0]),
        load(features.at[7], feat.at[7]),
        load(features.at[1:7, 0], feat.at[1:7, 0]),
        load(features.at[1:7, 7], feat.at[1:7, 7]),
    ]
    small_loads = [
        load(slot_in, slot),
        load(owner_in, owner),
        load(lever_in, lever),
        load(pose_in, pose),
        load(motion_in, motion),
        load(inverse_in, inverse),
    ]
    inner_loads = [load(features.at[i, 1:7], feat.at[i, 1:7]) for i in range(1, 7)]

    barrier = pltpu.get_barrier_semaphore()
    for code in CODES:
        pl.semaphore_signal(barrier, inc=1, device_id=neighbour(code), device_id_type=MESH)

    rate_scale = [rates[k] * (-LOG2E) for k in range(4)]
    lead = rate_scale[0]
    ratio = [None] + [rate_scale[k] / lead for k in range(1, 4)]
    four_lead = -4.0 * lead
    final_scale = 1.0 / (2048.0 * lead * lead)
    raw[...] = jnp.zeros_like(raw)
    acc[...] = jnp.zeros_like(acc)
    stage_q[...] = jnp.zeros_like(stage_q)
    stage_r[...] = jnp.zeros_like(stage_r)
    stage_m[...] = jnp.zeros_like(stage_m)
    stage_n[...] = jnp.zeros_like(stage_n)
    table_f32[...] = jnp.zeros_like(table_f32)

    got_pos.wait()
    pos32[...] = pos[...].astype(F32)

    def v_src(a, b):
        if b == 0:
            return vt.at[pl.ds(11 if a < 0 else 81, 8)]
        if a == 0:
            return None
        return vt.at[(10 if a < 0 else 80) + (1 if b < 0 else 8)]

    def landing(a, b, row_ref, col_ref, corner_ref):
        if b == 0:
            return row_ref.at[1 if a < 0 else 0]
        if a == 0:
            return col_ref.at[1 if b < 0 else 0]
        return corner_ref.at[(2 if a < 0 else 0) + (1 if b < 0 else 0)]

    lane = lax.broadcasted_iota(jnp.int32, (128, 128), 1)
    own_lanes = [jnp.where(lane // 32 == m, 1.0, 0.0).astype(BF16) for m in range(4)]
    zero8 = jnp.zeros((8, 128), F32)
    one8 = jnp.ones((8, 128), F32)
    steps8 = lax.broadcasted_iota(jnp.int32, (8, 128), 0).astype(F32) - 3.5

    def place(i):
        return jnp.full((8, 128), i.astype(F32) - 3.5)

    def put_rows(ref, stride, values):
        for r, value in enumerate(values):
            ref[pl.ds(r, 8, stride=stride), :] = value

    def partner_tables(q, gi, gj, indices, wide=stage_q, narrow=stage_m):
        ax, ay = q[0] + gi, q[1] + gj
        square = split3(lead * (ax * ax + ay * ay + q[2] * q[2]))
        values = [q[0]] * 3 + [q[1]] * 3 + [q[2]] * 3 + [gi] * 3 + [gj] * 3
        put_rows(wide, 32, values + list(square) + [one8] * 3)
        put_rows(narrow, 8, [q[0], q[1], q[2], one8, gi, gj])
        for half in range((len(indices) + 3) // 4):
            turned = wide[128 * half : 128 * half + 128, :].T.astype(BF16)
            for m, index in enumerate(indices[4 * half : 4 * half + 4]):
                qf[index] = turned * own_lanes[m]
        for m, index in enumerate(indices):
            rows = narrow[8 * m : 8 * m + 8, :]
            qm[index] = jnp.concatenate([rows, zero8], axis=0).astype(BF16)

    slots = lax.broadcasted_iota(jnp.int32, (128, 128), 0)
    for copy in small_loads:
        copy.wait()

    def prepare(i):
        q = [pos32[i, c] for c in range(3)]
        gi = place(i)
        partner_tables(q, gi, steps8, [(i + 1) * 10 + 1 + m for m in range(8)])
        ax, ay, az = q[0] + gi, q[1] + steps8, q[2]
        xs = list(split3(-2.0 * lead * ax))
        ys = list(split3(-2.0 * lead * ay))
        zs = list(split3(-2.0 * lead * az))
        sq = list(split3(lead * (ax * ax + ay * ay + az * az)))
        put_rows(stage_r, 32, xs + ys + zs + xs + ys + [one8] * 3 + sq)
        for m in range(8):
            rp[i * 8 + m] = stage_r[32 * m : 32 * m + 32, :].astype(BF16)
            here = slot[i, m : m + 1, :]
            oh[i * 8 + m] = jnp.where(slots == here, 1.0, 0.0).astype(BF16)


    pos_copies, v_copies = [], []

    buffers = [s_even.at[0], s_odd.at[0], s_even.at[1], s_odd.at[1]]

    def project(pair, s):
        ia, ja, ib, jb = pair
        both = jnp.concatenate([feat[ia, ja], feat[ib, jb]], axis=1)
        s[0:640, :] = mm(weights[...], both)

    def settle(pair, s):
        ia, ja, ib, jb = pair
        for i, j, lanes in ((ia, ja, slice(0, 128)), (ib, jb, slice(128, 256))):
            u[i * 8 + j] = s[0:512, lanes].astype(BF16)
            vt[(i + 1) * 10 + j + 1] = s[512:640, lanes].astype(BF16).T

    for copy in got_weights + rim_loads + inner_loads[:1]:
        copy.wait()
    start = [rim_then_inner(jnp.int32(p)) for p in range(5)]
    project(start[0], buffers[0])

    def project_four(q, carry, tables):
        for step in range(4):
            project(carry[step + 1], buffers[(step + 1) % 4])
            settle(carry[step], buffers[step])
            if tables and step % 2 == 0:
                prepare(2 * (q - 4) + step // 2)
        return carry[4:] + tuple(rim_then_inner(4 * q + p) for p in range(5, 9))

    rim_part = functools.partial(project_four, tables=False)
    carry = lax.fori_loop(0, 4, rim_part, tuple(start))
    pl.semaphore_wait(barrier, 8)

    def send_pos(src, dst, code):
        n = len(pos_copies)
        copy = pltpu.make_async_remote_copy(
            src_ref=src,
            dst_ref=dst,
            send_sem=pos_send.at[n],
            recv_sem=pos_recv.at[n],
            device_id=neighbour(code),
            device_id_type=MESH,
        )
        copy.start()
        pos_copies.append(copy)

    for code in CODES:
        a, b = code // 3 - 1, code % 3 - 1
        i, j = (0 if a < 0 else 7), (0 if b < 0 else 7)
        if b == 0:
            send_pos(pos32.at[i], pos_row.at[1 if a < 0 else 0], code)
        elif a == 0:
            for c in range(3):
                send_pos(pos32.at[:, c, j], pos_col.at[1 if b < 0 else 0, c], code)
        else:
            k = (2 if a < 0 else 0) + (1 if b < 0 else 0)
            send_pos(pos32.at[i, :, j], pos_corner.at[:, k], code)

    vt4 = vt.reshape(10, 10, 128, 128)
    for n, code in enumerate(CODES):
        a, b = code // 3 - 1, code % 3 - 1
        src = vt4.at[1:9, 1 if b < 0 else 8] if a == 0 else v_src(a, b)
        v_copies.append(
            pltpu.make_async_remote_copy(
                src_ref=src,
                dst_ref=landing(a, b, v_row, v_col, v_corner),
                send_sem=v_send.at[n],
                recv_sem=v_recv.at[n],
                device_id=neighbour(code),
                device_id_type=MESH,
            )
        )
    for n in sorted(range(8), key=lambda n: (CODES[n] // 3 == 1, CODES[n])):
        v_copies[n].start()

    for copy in inner_loads[1:]:
        copy.wait()
    lax.fori_loop(4, 8, functools.partial(project_four, tables=True), carry)

    def where_is(p):
        ia, ja, ib, jb = any_pair(p)
        found = [ia * 8 + ja, ib * 8 + jb]
        for i, j in ((ia, ja), (ib, jb)):
            for n in range(6):
                c = codes[n, i, j]
                found.append(i * 10 + j + c + 7 * ((c * 11) >> 5))
        return tuple(found)

    zeros128 = jnp.zeros((128, 128), BF16)

    def scores(at, s):
        for which in DOTS:
            if which == 4:
                rows = [jnp.concatenate([qf[n], qf[m]], axis=1) for n, m in zip(at[2:8], at[8:14])]
                right = jnp.concatenate(
                    [
                        jnp.concatenate([rp[at[0]]] * 4 + [zeros128], axis=0),
                        jnp.concatenate([zeros128] + [rp[at[1]]] * 4, axis=0),
                    ],
                    axis=1,
                )
            else:
                x, half = which // 2, which % 2
                rows = [vt[n] for n in at[2 + 6 * x : 8 + 6 * x]]
                first = u[at[x], 256 * half : 256 * half + 128, :]
                second = u[at[x], 256 * half + 128 : 256 * half + 256, :]
                right = jnp.concatenate([first, second], axis=1)
            s[which] = mm(jnp.concatenate(rows, axis=0), right)
            yield

    def couples(at, s):
        for x in range(2):
            t, found = at[x], at[2 + 6 * x : 8 + 6 * x]
            total = None
            for two in range(3):
                couple = []
                for n in (2 * two, 2 * two + 1):
                    rows = slice(n * 128, (n + 1) * 128)
                    t0 = s[4, rows, x * 128 : (x + 1) * 128]
                    mixed = None
                    for k in range(4):
                        score = s[2 * x + k // 2, rows, (k % 2) * 128 : (k % 2 + 1) * 128]
                        term = jnp.exp2(t0 if k == 0 else t0 * ratio[k]) * score
                        mixed = term if mixed is None else mixed + term
                    inside = jnp.maximum(t0 + four_lead, 0.0)
                    couple.append((mixed * (inside * inside)).astype(BF16))
                    yield
                left = jnp.concatenate([qm[found[2 * two]], qm[found[2 * two + 1]]], axis=1)
                got = mm(left, jnp.concatenate(couple, axis=0))
                total = got if total is None else total + got
            raw[pl.ds(pl.multiple_of(t * 8, 8), 8), :] = total[0:8]

    def run(steps):
        for _ in steps:
            pass

    def mixed_run(first, second):
        for which in MIX:
            next(first if which == "D" else second)
        run(first)
        run(second)

    def finish_halo():
        for copy in pos_copies:
            copy.wait_recv()
        for copy in v_copies:
            copy.wait_recv()

        def sides(side, carry):
            edge = place(9 * side - 1)
            in_row = [90 * side + 1 + m for m in range(8)]
            in_col = [(m + 1) * 10 + 9 * side for m in range(8)]
            along = [pos_row[side, c] for c in range(3)]
            across = [pos_col[side, c] for c in range(3)]
            partner_tables(along, edge, steps8, in_row)
            partner_tables(across, steps8, edge, in_col, stage_r, stage_n)
            for m in range(8):
                vt[in_row[m]] = v_row[side, m]
                vt[in_col[m]] = v_col[side, m]
            return carry

        lax.fori_loop(0, 2, sides, 0)
        k = lax.broadcasted_iota(jnp.int32, (8, 128), 0)
        gi = jnp.where(k < 2, -4.5, 4.5)
        gj = jnp.where(k % 2 == 0, -4.5, 4.5)
        at = [0, 9, 90, 99]
        for m in range(4):
            vt[at[m]] = v_corner[m]
        partner_tables([pos_corner[c] for c in range(3)], gi, gj, at)

    def force_terms():
        def row(i, carry):
            def strided(c):
                return raw[pl.ds(64 * i + c, 8, stride=8), :]

            weight = strided(3)
            px, py, pz = pos32[i, 0] + place(i), pos32[i, 1] + steps8, pos32[i, 2]
            lx, ly, lz = lever[i, 0], lever[i, 1], lever[i, 2]
            fx = (px * weight - (strided(0) + strided(4))) * final_scale
            fy = (py * weight - (strided(1) + strided(5))) * final_scale
            fz = (pz * weight - strided(2)) * final_scale
            rows = [fx, fy, fz, ly * fz - lz * fy, lz * fx - lx * fz, lx * fy - ly * fx]
            put = rows + [zero8] * 2
            for c, value in enumerate(put):
                high = value.astype(BF16).astype(F32)
                terms[pl.ds(128 * i + c, 8, stride=16), :] = high
                terms[pl.ds(128 * i + 8 + c, 8, stride=16), :] = value - high
            return carry

        lax.fori_loop(0, 8, row, 0)

    def part_terms(t):
        return terms[pl.ds(pl.multiple_of(t * 16, 16), 16), :]

    def masked_sums(places, start, count):
        left, right = [], []
        for i, j in places:
            t = i * 8 + j
            value = part_terms(t)
            whose = owner[i, pl.ds(j, 1), :]
            masks = [jnp.where(whose == start + c, value, 0.0) for c in range(count)]
            left.append(jnp.concatenate(masks, axis=0).astype(BF16))
            right.append(oh[t])
        got = mm_nt(jnp.concatenate(left, axis=1), jnp.concatenate(right, axis=1))
        where = pl.ds(pl.multiple_of(start * 16, 16), count * 16)
        acc[where, :] = acc[where, :] + got

    part_copies = []
    for n, code in enumerate(CODES):
        part_copies.append(
            pltpu.make_async_remote_copy(
                src_ref=part_out.at[code],
                dst_ref=part_in.at[code],
                send_sem=part_send.at[n],
                recv_sem=part_recv.at[n],
                device_id=neighbour(code),
                device_id_type=MESH,
            )
        )

    def send_parts():
        force_terms()

        def rows(side, carry):
            masked_sums([(7 * side, m) for m in range(8)], 3 * side, 6)
            return carry

        def cols(side, carry):
            masked_sums([(m, 7 * side) for m in range(1, 7)], 3 + side, 2)
            return carry

        lax.fori_loop(0, 2, rows, 0)
        lax.fori_loop(0, 2, cols, 0)
        for code in CODES:
            part_out[code] = acc[16 * code : 16 * code + 8, :] + acc[16 * code + 8 : 16 * code + 16, :]
        for copy in part_copies:
            copy.start()

    first = where_is(jnp.int32(0))
    run(scores(first, s_even))

    def four_pairs(q, carry):
        pl.when(q == 3)(finish_halo)
        at = [carry[14 * n : 14 * n + 14] for n in range(2)]
        at += [where_is(4 * q + n) for n in range(2, 6)]
        for n in range(4):
            filled, used = (s_odd, s_even) if n % 2 == 0 else (s_even, s_odd)
            mixed_run(scores(at[n + 1], filled), couples(at[n], used))
        return at[4] + at[5]

    carry = lax.fori_loop(0, 7, four_pairs, first + where_is(jnp.int32(1)))
    send_parts()

    def last_pairs(q, carry):
        now, after = carry[:14], carry[14:]
        later, last = where_is(30 + 2 * q), where_is(31 + 2 * q)
        mixed_run(scores(after, s_odd), couples(now, s_even))
        mixed_run(scores(later, s_even), couples(after, s_odd))
        return later + last

    carry = lax.fori_loop(0, 1, last_pairs, carry)
    now, after = carry[:14], carry[14:]
    mixed_run(scores(after, s_odd), couples(now, s_even))
    run(couples(after, s_odd))

    force_terms()

    def inner_sums(q, total):
        left, right = [], []
        for i in (2 * q + 1, 2 * q + 2):
            for j in range(1, 7):
                left.append(part_terms(i * 8 + j).astype(BF16))
                right.append(oh[i * 8 + j])
        return total + mm_nt(jnp.concatenate(left, axis=1), jnp.concatenate(right, axis=1))

    own = lax.fori_loop(0, 3, inner_sums, acc[64:80, :])
    total = own[0:8] + own[8:16]
    for copy in part_copies:
        copy.wait_recv()
    for code in CODES:
        total = total + part_in[code]

    inv = inverse[0, 0]
    centre = [pose[0, c] for c in range(3)]
    quat = [pose[0, c] for c in range(3, 7)]
    vel = [motion[0, c] + STEP_DT * inv[0:1] * total[c : c + 1] for c in range(3)]
    ang = [motion[0, c] + STEP_DT * total[c : c + 1] for c in range(3, 6)]
    shift = [STEP_DT * v for v in vel]
    rot = rotation_rows(*quat)
    frame = [
        (rot[0][c] * ang[0] + rot[1][c] * ang[1] + rot[2][c] * ang[2]) * inv[c + 1 : c + 2]
        for c in range(3)
    ]
    omega = [rot[r][0] * frame[0] + rot[r][1] * frame[1] + rot[r][2] * frame[2] for r in range(3)]
    qw, qv = quat[0], quat[1:4]
    change = [
        -(omega[0] * qv[0] + omega[1] * qv[1] + omega[2] * qv[2]),
        qw * omega[0] + (omega[1] * qv[2] - omega[2] * qv[1]),
        qw * omega[1] + (omega[2] * qv[0] - omega[0] * qv[2]),
        qw * omega[2] + (omega[0] * qv[1] - omega[1] * qv[0]),
    ]
    stepped = [q + 0.5 * STEP_DT * d for q, d in zip(quat, change)]
    norm = jnp.sqrt(sum(s * s for s in stepped[1:]) + stepped[0] * stepped[0])
    turned = [s / norm for s in stepped]
    rot_new = rotation_rows(*turned)
    for c in range(3):
        table_f32[c : c + 1, :] = shift[c]
        for r in range(3):
            entry = sum(rot_new[r][k] * rot[c][k] for k in range(3))
            table_f32[3 * (c + 1) + r : 3 * (c + 1) + r + 1, :] = entry
    whole = table_f32[...]
    high = whole.astype(BF16)
    table[128:144, :] = high
    table[144:160, :] = (whole - high.astype(F32)).astype(BF16)
    table_copies = []
    for n, code in enumerate(CODES):
        table_copies.append(
            pltpu.make_async_remote_copy(
                src_ref=table.at[pl.ds(128, 32)],
                dst_ref=table.at[pl.ds((8 - code) * 32, 32)],
                send_sem=table_send.at[n],
                recv_sem=table_recv.at[n],
                device_id=neighbour(code),
                device_id_type=MESH,
            )
        )
    for copy in table_copies:
        copy.start()
    next_rows = [c + s for c, s in zip(centre, shift)] + turned + vel + ang
    for c, value in enumerate(next_rows):
        body_next[0, c] = value

    def look_up(places, start, count):
        if count == 1:
            rows = table[128:160, :]
        else:
            rows = table[pl.ds(pl.multiple_of(start * 32, 32), count * 32), :]
        tiles = [i * 8 + j for i, j in places]
        got = mm(rows, jnp.concatenate([oh[t] for t in tiles], axis=1))
        for n, (i, j) in enumerate(places):
            lanes = slice(128 * n, 128 * n + 128)
            found = None
            for c in range(count):
                one = got[32 * c : 32 * c + 16, lanes] + got[32 * c + 16 : 32 * c + 32, lanes]
                if c:
                    whose = owner[i, pl.ds(j, 1), :]
                    found = jnp.where(whose == start + c, one, found)
                else:
                    found = one
            picked[pl.ds(pl.multiple_of(tiles[n] * 16, 16), 16), :] = found

    def look_inner(i, carry):
        look_up([(i, j) for j in range(1, 7)], 4, 1)
        return carry

    lax.fori_loop(1, 7, look_inner, 0)
    for copy in table_copies:
        copy.wait_recv()

    def look_rows(q, carry):
        i, start = 7 * (q // 2), 3 * (q // 2)
        look_up([(i, 4 * (q % 2) + m) for m in range(4)], start, 6)
        return carry

    def look_cols(side, carry):
        look_up([(i, 7 * side) for i in range(1, 7)], 3 + side, 2)
        return carry

    lax.fori_loop(0, 4, look_rows, 0)
    lax.fori_loop(0, 2, look_cols, 0)

    def move(i, carry):
        def strided(c):
            return picked[pl.ds(128 * i + c, 8, stride=16), :]

        levers = [lever[i, c] for c in range(3)]
        for r in range(3):
            value = pos32[i, r] + strided(r)
            for c in range(3):
                value = value + strided(3 + 3 * c + r) * levers[c]
            moved[i, r] = value - levers[r]
        return carry

    lax.fori_loop(0, 8, move, 0)
    for copy in pos_copies + v_copies + part_copies + table_copies:
        copy.wait_send()


def hand_over(moved, body_next, moved_out, body_out, sem):
    copies = [
        pltpu.make_async_copy(moved, moved_out, sem.at[0]),
        pltpu.make_async_copy(body_next, body_out, sem.at[1]),
    ]
    for copy in copies:
        copy.start()
    for copy in copies:
        copy.wait()


def local(
    positions,
    features,
    lever,
    partner,
    body_slot,
    owner_dir,
    body_pose,
    body_motion,
    body_inverse,
    weight_u,
    weight_v,
    radial_rate,
):
    hbm = pl.BlockSpec(memory_space=pl.ANY)
    smem = pl.BlockSpec(memory_space=pltpu.SMEM)
    vmem = pl.BlockSpec(memory_space=pltpu.VMEM)
    dma = pltpu.SemaphoreType.DMA
    like = lambda x: pltpu.VMEM(x.shape, x.dtype)
    inside = lambda x: jnp.transpose(x, (0, 2, 1, 3))
    positions, lever = inside(positions), inside(lever)
    body_pose, body_motion = inside(body_pose), inside(body_motion)
    partner = jnp.transpose(partner, (2, 0, 1))
    moved, body_next = pl.pallas_call(
        kernel,
        out_shape=(
            pltpu.VMEM((8, 3, 8, 128), F32),
            pltpu.VMEM((1, 13, 1, 128), F32),
        ),
        in_specs=[smem, smem] + [hbm] * 10,
        out_specs=(vmem, vmem),
        scratch_shapes=[
            like(positions),
            like(features),
            like(lever),
            like(body_slot),
            like(owner_dir),
            like(body_pose),
            like(body_motion),
            like(body_inverse),
            pltpu.VMEM((640, 256), BF16),
            pltpu.VMEM((100, 128, 128), BF16),
            pltpu.VMEM((100, 128, 128), BF16),
            pltpu.VMEM((100, 16, 128), BF16),
            pltpu.VMEM((64, 32, 128), BF16),
            pltpu.VMEM((64, 512, 128), BF16),
            pltpu.VMEM((64, 128, 128), BF16),
            pltpu.VMEM((512, 128), F32),
            pltpu.VMEM((1024, 128), F32),
            pltpu.VMEM((1024, 128), F32),
            pltpu.VMEM((144, 128), F32),
            pltpu.VMEM((9, 8, 128), F32),
            pltpu.VMEM((9, 8, 128), F32),
            pltpu.VMEM((288, 128), BF16),
            pltpu.VMEM((16, 128), F32),
            pltpu.VMEM((8, 3, 8, 128), F32),
            pltpu.VMEM((256, 128), F32),
            pltpu.VMEM((256, 128), F32),
            pltpu.VMEM((64, 128), F32),
            pltpu.VMEM((64, 128), F32),
            pltpu.VMEM((2, 3, 8, 128), F32),
            pltpu.VMEM((2, 3, 8, 128), F32),
            pltpu.VMEM((3, 8, 128), F32),
            pltpu.VMEM((2, 8, 128, 128), BF16),
            pltpu.VMEM((2, 8, 128, 128), BF16),
            pltpu.VMEM((4, 128, 128), BF16),
            pltpu.VMEM((5, 768, 256), F32),
            pltpu.VMEM((5, 768, 256), F32),
            dma((24,)),
            dma((12,)),
            dma((12,)),
            dma((8,)),
            dma((8,)),
            dma((8,)),
            dma((8,)),
            dma((8,)),
            dma((8,)),
        ],
        compiler_params=pltpu.CompilerParams(
            collective_id=0, has_side_effects=True, vmem_limit_bytes=60 * 1024 * 1024
        ),
        name="step",
    )(
        partner,
        radial_rate,
        positions,
        features,
        lever,
        body_slot,
        owner_dir,
        body_pose,
        body_motion,
        body_inverse,
        weight_u,
        weight_v,
    )
    moved, body_next = pl.pallas_call(
        hand_over,
        out_shape=(
            jax.ShapeDtypeStruct((8, 3, 8, 128), F32),
            jax.ShapeDtypeStruct((1, 13, 1, 128), F32),
        ),
        in_specs=[vmem, vmem],
        out_specs=(hbm, hbm),
        scratch_shapes=[dma((2,))],
        name="out",
    )(
        pltpu.with_memory_space_constraint(moved, pltpu.VMEM),
        pltpu.with_memory_space_constraint(body_next, pltpu.VMEM),
    )
    return inside(moved), inside(body_next)


def solution(mesh):
    tiles = P("gx", "gy", None, None)
    flat = P("gx", "gy", None)
    return jax.shard_map(
        local,
        mesh=mesh,
        in_specs=(tiles, tiles, tiles, flat, flat, flat, tiles, tiles, tiles, P(), P(), P()),
        out_specs=(tiles, tiles),
        check_vma=False,
    )
```

```python
import functools

import jax
import jax.numpy as jnp
from jax import lax
from jax.experimental import pallas as pl
from jax.experimental.pallas import tpu as pltpu
from jax.sharding import PartitionSpec as P

STEP_DT = 0.25
LOG2E = 1.4426950408889634
MESH = pl.DeviceIdType.MESH
F32 = jnp.float32
BF16 = jnp.bfloat16
INNER_FIRST = 13
CODES = [c for c in range(9) if c != 4]
MIX = "DUUDUUDUUDUUDUU"
DOTS = (0, 1, 2, 3, 4)


def mm(a, b):
    return jnp.dot(a, b, preferred_element_type=F32)


def mm_nt(a, b):
    return lax.dot_general(a, b, (((1,), (1,)), ((), ())), preferred_element_type=F32)


def split3(value):
    high = value.astype(BF16).astype(F32)
    rest = value - high
    mid = rest.astype(BF16).astype(F32)
    return high, mid, rest - mid


def inner_pair(q):
    i = 1 + q // 3
    j = 1 + 2 * (q % 3)
    return i, j, i, j + 1


def rim_pair(q):
    in_rows = q < 8
    c = q - 8
    i = jnp.where(in_rows, 7 * (q // 4), 1 + 2 * (c % 3))
    j = jnp.where(in_rows, 2 * (q % 4), 7 * (c // 3))
    return i, j, jnp.where(in_rows, i, i + 1), jnp.where(in_rows, j + 1, j)


def row_pair(q):
    i = 7 * (q // 4)
    j = 2 * (q % 4)
    return i, j, i, j + 1


def col_pair(q):
    i = 1 + 2 * (q % 3)
    j = 7 * (q // 3)
    return i, j, i + 1, j


def rim_then_inner(p):
    rim = rim_pair(jnp.clip(p, 0, 13))
    inner = inner_pair(jnp.clip(p - 14, 0, 17))
    return tuple(jnp.where(p < 14, r, n) for r, n in zip(rim, inner))


def any_pair(p):
    rim = rim_pair(jnp.clip(p - INNER_FIRST, 0, 13))
    inner = inner_pair(jnp.clip(jnp.where(p < INNER_FIRST, p, p - 14), 0, 17))
    is_rim = (p >= INNER_FIRST) & (p < INNER_FIRST + 14)
    return tuple(jnp.where(is_rim, r, n) for r, n in zip(rim, inner))


def rotation_rows(qw, qa, qb, qc):
    return [
        [1 - 2 * (qb * qb + qc * qc), 2 * (qa * qb - qw * qc), 2 * (qa * qc + qw * qb)],
        [2 * (qa * qb + qw * qc), 1 - 2 * (qa * qa + qc * qc), 2 * (qb * qc - qw * qa)],
        [2 * (qa * qc - qw * qb), 2 * (qb * qc + qw * qa), 1 - 2 * (qa * qa + qb * qb)],
    ]


def kernel(
    codes,
    rates,
    positions,
    features,
    lever_in,
    slot_in,
    owner_in,
    pose_in,
    motion_in,
    inverse_in,
    wu_in,
    wv_in,
    moved,
    body_next,
    pos,
    feat,
    lever,
    slot,
    owner,
    pose,
    motion,
    inverse,
    weights,
    vt,
    qf,
    qm,
    rp,
    u,
    oh,
    raw,
    terms,
    picked,
    acc,
    part_out,
    part_in,
    table,
    table_f32,
    pos32,
    stage_q,
    stage_r,
    stage_m,
    stage_n,
    pos_row,
    pos_col,
    pos_corner,
    v_row,
    v_col,
    v_corner,
    s_even,
    s_odd,
    in_sem,
    pos_send,
    pos_recv,
    v_send,
    v_recv,
    part_send,
    part_recv,
    table_send,
    table_recv,
):
    gx, gy = lax.axis_index("gx"), lax.axis_index("gy")
    nx, ny = lax.axis_size("gx"), lax.axis_size("gy")

    def neighbour(code):
        a, b = code // 3 - 1, code % 3 - 1
        return (lax.rem(gx + a + nx, nx), lax.rem(gy + b + ny, ny))

    loads = []

    def load(src, dst):
        copy = pltpu.make_async_copy(src, dst, in_sem.at[len(loads)])
        copy.start()
        loads.append(copy)
        return copy

    got_pos = load(positions, pos)
    got_weights = [load(wu_in, weights.at[0:512]), load(wv_in, weights.at[512:640])]
    rim_loads = [
        load(features.at[0], feat.at[0]),
        load(features.at[7], feat.at[7]),
        load(features.at[1:7, 0], feat.at[1:7, 0]),
        load(features.at[1:7, 7], feat.at[1:7, 7]),
    ]
    small_loads = [
        load(slot_in, slot),
        load(owner_in, owner),
        load(lever_in, lever),
        load(pose_in, pose),
        load(motion_in, motion),
        load(inverse_in, inverse),
    ]
    inner_loads = [load(features.at[i, 1:7], feat.at[i, 1:7]) for i in range(1, 7)]

    barrier = pltpu.get_barrier_semaphore()
    for code in CODES:
        pl.semaphore_signal(barrier, inc=1, device_id=neighbour(code), device_id_type=MESH)

    rate_scale = [rates[k] * (-LOG2E) for k in range(4)]
    lead = rate_scale[0]
    ratio = [None] + [rate_scale[k] / lead for k in range(1, 4)]
    four_lead = -4.0 * lead
    final_scale = 1.0 / (2048.0 * lead * lead)
    raw[...] = jnp.zeros_like(raw)
    acc[...] = jnp.zeros_like(acc)
    stage_q[...] = jnp.zeros_like(stage_q)
    stage_r[...] = jnp.zeros_like(stage_r)
    stage_m[...] = jnp.zeros_like(stage_m)
    stage_n[...] = jnp.zeros_like(stage_n)
    table_f32[...] = jnp.zeros_like(table_f32)

    got_pos.wait()
    pos32[...] = pos[...].astype(F32)

    def v_src(a, b):
        if b == 0:
            return vt.at[pl.ds(11 if a < 0 else 81, 8)]
        if a == 0:
            return None
        return vt.at[(10 if a < 0 else 80) + (1 if b < 0 else 8)]

    def landing(a, b, row_ref, col_ref, corner_ref):
        if b == 0:
            return row_ref.at[1 if a < 0 else 0]
        if a == 0:
            return col_ref.at[1 if b < 0 else 0]
        return corner_ref.at[(2 if a < 0 else 0) + (1 if b < 0 else 0)]

    lane = lax.broadcasted_iota(jnp.int32, (128, 128), 1)
    own_lanes = [jnp.where(lane // 32 == m, 1.0, 0.0).astype(BF16) for m in range(4)]
    zero8 = jnp.zeros((8, 128), F32)
    one8 = jnp.ones((8, 128), F32)
    steps8 = lax.broadcasted_iota(jnp.int32, (8, 128), 0).astype(F32) - 3.5

    def place(i):
        return jnp.full((8, 128), i.astype(F32) - 3.5)

    def put_rows(ref, stride, values):
        for r, value in enumerate(values):
            ref[pl.ds(r, 8, stride=stride), :] = value

    def partner_tables(q, gi, gj, indices, wide=stage_q, narrow=stage_m):
        ax, ay = q[0] + gi, q[1] + gj
        square = split3(lead * (ax * ax + ay * ay + q[2] * q[2]))
        values = [q[0]] * 3 + [q[1]] * 3 + [q[2]] * 3 + [gi] * 3 + [gj] * 3
        put_rows(wide, 32, values + list(square) + [one8] * 3)
        put_rows(narrow, 8, [q[0], q[1], q[2], one8, gi, gj])
        for half in range((len(indices) + 3) // 4):
            turned = wide[128 * half : 128 * half + 128, :].T.astype(BF16)
            for m, index in enumerate(indices[4 * half : 4 * half + 4]):
                qf[index] = turned * own_lanes[m]
        for m, index in enumerate(indices):
            rows = narrow[8 * m : 8 * m + 8, :]
            qm[index] = jnp.concatenate([rows, zero8], axis=0).astype(BF16)

    slots = lax.broadcasted_iota(jnp.int32, (128, 128), 0)
    for copy in small_loads:
        copy.wait()

    def prepare(i):
        q = [pos32[i, c] for c in range(3)]
        gi = place(i)
        partner_tables(q, gi, steps8, [(i + 1) * 10 + 1 + m for m in range(8)])
        ax, ay, az = q[0] + gi, q[1] + steps8, q[2]
        xs = list(split3(-2.0 * lead * ax))
        ys = list(split3(-2.0 * lead * ay))
        zs = list(split3(-2.0 * lead * az))
        sq = list(split3(lead * (ax * ax + ay * ay + az * az)))
        put_rows(stage_r, 32, xs + ys + zs + xs + ys + [one8] * 3 + sq)
        for m in range(8):
            rp[i * 8 + m] = stage_r[32 * m : 32 * m + 32, :].astype(BF16)
            here = slot[i, m : m + 1, :]
            oh[i * 8 + m] = jnp.where(slots == here, 1.0, 0.0).astype(BF16)


    pos_copies, v_copies = [], []

    buffers = [s_even.at[0], s_odd.at[0], s_even.at[1], s_odd.at[1]]

    def project(pair, s):
        ia, ja, ib, jb = pair
        both = jnp.concatenate([feat[ia, ja], feat[ib, jb]], axis=1)
        s[0:640, :] = mm(weights[...], both)

    def settle(pair, s):
        ia, ja, ib, jb = pair
        for i, j, lanes in ((ia, ja, slice(0, 128)), (ib, jb, slice(128, 256))):
            u[i * 8 + j] = s[0:512, lanes].astype(BF16)
            vt[(i + 1) * 10 + j + 1] = s[512:640, lanes].astype(BF16).T

    for copy in got_weights + rim_loads + inner_loads[:1]:
        copy.wait()
    start = [rim_then_inner(jnp.int32(p)) for p in range(5)]
    project(start[0], buffers[0])

    def project_four(q, carry, tables):
        for step in range(4):
            project(carry[step + 1], buffers[(step + 1) % 4])
            settle(carry[step], buffers[step])
            if tables and step % 2 == 0:
                prepare(2 * (q - 4) + step // 2)
        return carry[4:] + tuple(rim_then_inner(4 * q + p) for p in range(5, 9))

    rim_part = functools.partial(project_four, tables=False)
    carry = lax.fori_loop(0, 4, rim_part, tuple(start))
    pl.semaphore_wait(barrier, 8)

    def send_pos(src, dst, code):
        n = len(pos_copies)
        copy = pltpu.make_async_remote_copy(
            src_ref=src,
            dst_ref=dst,
            send_sem=pos_send.at[n],
            recv_sem=pos_recv.at[n],
            device_id=neighbour(code),
            device_id_type=MESH,
        )
        copy.start()
        pos_copies.append(copy)

    for code in CODES:
        a, b = code // 3 - 1, code % 3 - 1
        i, j = (0 if a < 0 else 7), (0 if b < 0 else 7)
        if b == 0:
            send_pos(pos32.at[i], pos_row.at[1 if a < 0 else 0], code)
        elif a == 0:
            for c in range(3):
                send_pos(pos32.at[:, c, j], pos_col.at[1 if b < 0 else 0, c], code)
        else:
            k = (2 if a < 0 else 0) + (1 if b < 0 else 0)
            send_pos(pos32.at[i, :, j], pos_corner.at[:, k], code)

    vt4 = vt.reshape(10, 10, 128, 128)
    for n, code in enumerate(CODES):
        a, b = code // 3 - 1, code % 3 - 1
        src = vt4.at[1:9, 1 if b < 0 else 8] if a == 0 else v_src(a, b)
        v_copies.append(
            pltpu.make_async_remote_copy(
                src_ref=src,
                dst_ref=landing(a, b, v_row, v_col, v_corner),
                send_sem=v_send.at[n],
                recv_sem=v_recv.at[n],
                device_id=neighbour(code),
                device_id_type=MESH,
            )
        )
    for n in sorted(range(8), key=lambda n: (CODES[n] // 3 == 1, CODES[n])):
        v_copies[n].start()

    for copy in inner_loads[1:]:
        copy.wait()
    lax.fori_loop(4, 8, functools.partial(project_four, tables=True), carry)

    def where_is(p):
        ia, ja, ib, jb = any_pair(p)
        found = [ia * 8 + ja, ib * 8 + jb]
        for i, j in ((ia, ja), (ib, jb)):
            for n in range(6):
                c = codes[n, i, j]
                found.append(i * 10 + j + c + 7 * ((c * 11) >> 5))
        return tuple(found)

    zeros128 = jnp.zeros((128, 128), BF16)

    def scores(at, s):
        for which in DOTS:
            if which == 4:
                rows = [jnp.concatenate([qf[n], qf[m]], axis=1) for n, m in zip(at[2:8], at[8:14])]
                right = jnp.concatenate(
                    [
                        jnp.concatenate([rp[at[0]]] * 4 + [zeros128], axis=0),
                        jnp.concatenate([zeros128] + [rp[at[1]]] * 4, axis=0),
                    ],
                    axis=1,
                )
            else:
                x, half = which // 2, which % 2
                rows = [vt[n] for n in at[2 + 6 * x : 8 + 6 * x]]
                first = u[at[x], 256 * half : 256 * half + 128, :]
                second = u[at[x], 256 * half + 128 : 256 * half + 256, :]
                right = jnp.concatenate([first, second], axis=1)
            s[which] = mm(jnp.concatenate(rows, axis=0), right)
            yield

    def couples(at, s):
        for x in range(2):
            t, found = at[x], at[2 + 6 * x : 8 + 6 * x]
            total = None
            for two in range(3):
                couple = []
                for n in (2 * two, 2 * two + 1):
                    rows = slice(n * 128, (n + 1) * 128)
                    t0 = s[4, rows, x * 128 : (x + 1) * 128]
                    mixed = None
                    for k in range(4):
                        score = s[2 * x + k // 2, rows, (k % 2) * 128 : (k % 2 + 1) * 128]
                        term = jnp.exp2(t0 if k == 0 else t0 * ratio[k]) * score
                        mixed = term if mixed is None else mixed + term
                    inside = jnp.maximum(t0 + four_lead, 0.0)
                    couple.append((mixed * (inside * inside)).astype(BF16))
                    yield
                left = jnp.concatenate([qm[found[2 * two]], qm[found[2 * two + 1]]], axis=1)
                got = mm(left, jnp.concatenate(couple, axis=0))
                total = got if total is None else total + got
            raw[pl.ds(pl.multiple_of(t * 8, 8), 8), :] = total[0:8]

    def run(steps):
        for _ in steps:
            pass

    def mixed_run(first, second):
        for which in MIX:
            next(first if which == "D" else second)
        run(first)
        run(second)

    def finish_halo():
        for copy in pos_copies:
            copy.wait_recv()
        for copy in v_copies:
            copy.wait_recv()

        def sides(side, carry):
            edge = place(9 * side - 1)
            in_row = [90 * side + 1 + m for m in range(8)]
            in_col = [(m + 1) * 10 + 9 * side for m in range(8)]
            along = [pos_row[side, c] for c in range(3)]
            across = [pos_col[side, c] for c in range(3)]
            partner_tables(along, edge, steps8, in_row)
            partner_tables(across, steps8, edge, in_col, stage_r, stage_n)
            for m in range(8):
                vt[in_row[m]] = v_row[side, m]
                vt[in_col[m]] = v_col[side, m]
            return carry

        lax.fori_loop(0, 2, sides, 0)
        k = lax.broadcasted_iota(jnp.int32, (8, 128), 0)
        gi = jnp.where(k < 2, -4.5, 4.5)
        gj = jnp.where(k % 2 == 0, -4.5, 4.5)
        at = [0, 9, 90, 99]
        for m in range(4):
            vt[at[m]] = v_corner[m]
        partner_tables([pos_corner[c] for c in range(3)], gi, gj, at)

    def force_terms():
        def row(i, carry):
            def strided(c):
                return raw[pl.ds(64 * i + c, 8, stride=8), :]

            weight = strided(3)
            px, py, pz = pos32[i, 0] + place(i), pos32[i, 1] + steps8, pos32[i, 2]
            lx, ly, lz = lever[i, 0], lever[i, 1], lever[i, 2]
            fx = (px * weight - (strided(0) + strided(4))) * final_scale
            fy = (py * weight - (strided(1) + strided(5))) * final_scale
            fz = (pz * weight - strided(2)) * final_scale
            rows = [fx, fy, fz, ly * fz - lz * fy, lz * fx - lx * fz, lx * fy - ly * fx]
            put = rows + [zero8] * 2
            for c, value in enumerate(put):
                high = value.astype(BF16).astype(F32)
                terms[pl.ds(128 * i + c, 8, stride=16), :] = high
                terms[pl.ds(128 * i + 8 + c, 8, stride=16), :] = value - high
            return carry

        lax.fori_loop(0, 8, row, 0)

    def part_terms(t):
        return terms[pl.ds(pl.multiple_of(t * 16, 16), 16), :]

    def masked_sums(places, start, count):
        left, right = [], []
        for i, j in places:
            t = i * 8 + j
            value = part_terms(t)
            whose = owner[i, pl.ds(j, 1), :]
            masks = [jnp.where(whose == start + c, value, 0.0) for c in range(count)]
            left.append(jnp.concatenate(masks, axis=0).astype(BF16))
            right.append(oh[t])
        got = mm_nt(jnp.concatenate(left, axis=1), jnp.concatenate(right, axis=1))
        where = pl.ds(pl.multiple_of(start * 16, 16), count * 16)
        acc[where, :] = acc[where, :] + got

    part_copies = []
    for n, code in enumerate(CODES):
        part_copies.append(
            pltpu.make_async_remote_copy(
                src_ref=part_out.at[code],
                dst_ref=part_in.at[code],
                send_sem=part_send.at[n],
                recv_sem=part_recv.at[n],
                device_id=neighbour(code),
                device_id_type=MESH,
            )
        )

    def send_parts():
        force_terms()

        def rows(side, carry):
            masked_sums([(7 * side, m) for m in range(8)], 3 * side, 6)
            return carry

        def cols(side, carry):
            masked_sums([(m, 7 * side) for m in range(1, 7)], 3 + side, 2)
            return carry

        lax.fori_loop(0, 2, rows, 0)
        lax.fori_loop(0, 2, cols, 0)
        for code in CODES:
            part_out[code] = acc[16 * code : 16 * code + 8, :] + acc[16 * code + 8 : 16 * code + 16, :]
        for copy in part_copies:
            copy.start()

    first = where_is(jnp.int32(0))
    run(scores(first, s_even))

    def four_pairs(q, carry):
        pl.when(q == 3)(finish_halo)
        at = [carry[14 * n : 14 * n + 14] for n in range(2)]
        at += [where_is(4 * q + n) for n in range(2, 6)]
        for n in range(4):
            filled, used = (s_odd, s_even) if n % 2 == 0 else (s_even, s_odd)
            mixed_run(scores(at[n + 1], filled), couples(at[n], used))
        return at[4] + at[5]

    carry = lax.fori_loop(0, 7, four_pairs, first + where_is(jnp.int32(1)))
    send_parts()

    def last_pairs(q, carry):
        now, after = carry[:14], carry[14:]
        later, last = where_is(30 + 2 * q), where_is(31 + 2 * q)
        mixed_run(scores(after, s_odd), couples(now, s_even))
        mixed_run(scores(later, s_even), couples(after, s_odd))
        return later + last

    carry = lax.fori_loop(0, 1, last_pairs, carry)
    now, after = carry[:14], carry[14:]
    mixed_run(scores(after, s_odd), couples(now, s_even))
    run(couples(after, s_odd))

    force_terms()

    def inner_sums(q, total):
        left, right = [], []
        for i in (2 * q + 1, 2 * q + 2):
            for j in range(1, 7):
                left.append(part_terms(i * 8 + j).astype(BF16))
                right.append(oh[i * 8 + j])
        return total + mm_nt(jnp.concatenate(left, axis=1), jnp.concatenate(right, axis=1))

    own = lax.fori_loop(0, 3, inner_sums, acc[64:80, :])
    total = own[0:8] + own[8:16]
    rot = rotation_rows(*[pose[0, c] for c in range(3, 7)])
    for copy in part_copies:
        copy.wait_recv()
    for code in CODES:
        total = total + part_in[code]

    inv = inverse[0, 0]
    centre = [pose[0, c] for c in range(3)]
    quat = [pose[0, c] for c in range(3, 7)]
    vel = [motion[0, c] + STEP_DT * inv[0:1] * total[c : c + 1] for c in range(3)]
    ang = [motion[0, c] + STEP_DT * total[c : c + 1] for c in range(3, 6)]
    shift = [STEP_DT * v for v in vel]
    frame = [
        (rot[0][c] * ang[0] + rot[1][c] * ang[1] + rot[2][c] * ang[2]) * inv[c + 1 : c + 2]
        for c in range(3)
    ]
    omega = [rot[r][0] * frame[0] + rot[r][1] * frame[1] + rot[r][2] * frame[2] for r in range(3)]
    qw, qv = quat[0], quat[1:4]
    change = [
        -(omega[0] * qv[0] + omega[1] * qv[1] + omega[2] * qv[2]),
        qw * omega[0] + (omega[1] * qv[2] - omega[2] * qv[1]),
        qw * omega[1] + (omega[2] * qv[0] - omega[0] * qv[2]),
        qw * omega[2] + (omega[0] * qv[1] - omega[1] * qv[0]),
    ]
    stepped = [q + 0.5 * STEP_DT * d for q, d in zip(quat, change)]
    norm = jnp.sqrt(sum(s * s for s in stepped[1:]) + stepped[0] * stepped[0])
    turned = [s / norm for s in stepped]
    rot_new = rotation_rows(*turned)
    for c in range(3):
        table_f32[c : c + 1, :] = shift[c]
        for r in range(3):
            entry = sum(rot_new[r][k] * rot[c][k] for k in range(3))
            table_f32[3 * (c + 1) + r : 3 * (c + 1) + r + 1, :] = entry
    whole = table_f32[...]
    high = whole.astype(BF16)
    table[128:144, :] = high
    table[144:160, :] = (whole - high.astype(F32)).astype(BF16)
    table_copies = []
    for n, code in enumerate(CODES):
        table_copies.append(
            pltpu.make_async_remote_copy(
                src_ref=table.at[pl.ds(128, 32)],
                dst_ref=table.at[pl.ds((8 - code) * 32, 32)],
                send_sem=table_send.at[n],
                recv_sem=table_recv.at[n],
                device_id=neighbour(code),
                device_id_type=MESH,
            )
        )
    for copy in table_copies:
        copy.start()
    next_rows = [c + s for c, s in zip(centre, shift)] + turned + vel + ang
    for c, value in enumerate(next_rows):
        body_next[0, c] = value

    def look_up(places, start, count):
        if count == 1:
            rows = table[128:160, :]
        else:
            rows = table[pl.ds(pl.multiple_of(start * 32, 32), count * 32), :]
        tiles = [i * 8 + j for i, j in places]
        got = mm(rows, jnp.concatenate([oh[t] for t in tiles], axis=1))
        for n, (i, j) in enumerate(places):
            lanes = slice(128 * n, 128 * n + 128)
            found = None
            for c in range(count):
                one = got[32 * c : 32 * c + 16, lanes] + got[32 * c + 16 : 32 * c + 32, lanes]
                if c:
                    whose = owner[i, pl.ds(j, 1), :]
                    found = jnp.where(whose == start + c, one, found)
                else:
                    found = one
            picked[pl.ds(pl.multiple_of(tiles[n] * 16, 16), 16), :] = found

    def look_inner(i, carry):
        look_up([(i, j) for j in range(1, 7)], 4, 1)
        return carry

    lax.fori_loop(1, 7, look_inner, 0)
    for copy in table_copies:
        copy.wait_recv()

    def look_rows(q, carry):
        look_up([(7 * q, m) for m in range(8)], 3 * q, 6)
        return carry

    def look_cols(side, carry):
        look_up([(i, 7 * side) for i in range(1, 7)], 3 + side, 2)
        return carry

    lax.fori_loop(0, 2, look_rows, 0)
    lax.fori_loop(0, 2, look_cols, 0)

    def move(i, carry):
        def strided(c):
            return picked[pl.ds(128 * i + c, 8, stride=16), :]

        levers = [lever[i, c] for c in range(3)]
        for r in range(3):
            value = pos32[i, r] + strided(r)
            for c in range(3):
                value = value + strided(3 + 3 * c + r) * levers[c]
            moved[i, r] = value - levers[r]
        return carry

    lax.fori_loop(0, 8, move, 0)
    for copy in pos_copies + v_copies + part_copies + table_copies:
        copy.wait_send()


def hand_over(moved, body_next, moved_out, body_out, sem):
    copies = [
        pltpu.make_async_copy(moved, moved_out, sem.at[0]),
        pltpu.make_async_copy(body_next, body_out, sem.at[1]),
    ]
    for copy in copies:
        copy.start()
    for copy in copies:
        copy.wait()


def local(
    positions,
    features,
    lever,
    partner,
    body_slot,
    owner_dir,
    body_pose,
    body_motion,
    body_inverse,
    weight_u,
    weight_v,
    radial_rate,
):
    hbm = pl.BlockSpec(memory_space=pl.ANY)
    smem = pl.BlockSpec(memory_space=pltpu.SMEM)
    vmem = pl.BlockSpec(memory_space=pltpu.VMEM)
    dma = pltpu.SemaphoreType.DMA
    like = lambda x: pltpu.VMEM(x.shape, x.dtype)
    inside = lambda x: jnp.transpose(x, (0, 2, 1, 3))
    positions, lever = inside(positions), inside(lever)
    body_pose, body_motion = inside(body_pose), inside(body_motion)
    partner = jnp.transpose(partner, (2, 0, 1))
    moved, body_next = pl.pallas_call(
        kernel,
        out_shape=(
            pltpu.VMEM((8, 3, 8, 128), F32),
            pltpu.VMEM((1, 13, 1, 128), F32),
        ),
        in_specs=[smem, smem] + [hbm] * 10,
        out_specs=(vmem, vmem),
        scratch_shapes=[
            like(positions),
            like(features),
            like(lever),
            like(body_slot),
            like(owner_dir),
            like(body_pose),
            like(body_motion),
            like(body_inverse),
            pltpu.VMEM((640, 256), BF16),
            pltpu.VMEM((100, 128, 128), BF16),
            pltpu.VMEM((100, 128, 128), BF16),
            pltpu.VMEM((100, 16, 128), BF16),
            pltpu.VMEM((64, 32, 128), BF16),
            pltpu.VMEM((64, 512, 128), BF16),
            pltpu.VMEM((64, 128, 128), BF16),
            pltpu.VMEM((512, 128), F32),
            pltpu.VMEM((1024, 128), F32),
            pltpu.VMEM((1024, 128), F32),
            pltpu.VMEM((144, 128), F32),
            pltpu.VMEM((9, 8, 128), F32),
            pltpu.VMEM((9, 8, 128), F32),
            pltpu.VMEM((288, 128), BF16),
            pltpu.VMEM((16, 128), F32),
            pltpu.VMEM((8, 3, 8, 128), F32),
            pltpu.VMEM((256, 128), F32),
            pltpu.VMEM((256, 128), F32),
            pltpu.VMEM((64, 128), F32),
            pltpu.VMEM((64, 128), F32),
            pltpu.VMEM((2, 3, 8, 128), F32),
            pltpu.VMEM((2, 3, 8, 128), F32),
            pltpu.VMEM((3, 8, 128), F32),
            pltpu.VMEM((2, 8, 128, 128), BF16),
            pltpu.VMEM((2, 8, 128, 128), BF16),
            pltpu.VMEM((4, 128, 128), BF16),
            pltpu.VMEM((5, 768, 256), F32),
            pltpu.VMEM((5, 768, 256), F32),
            dma((24,)),
            dma((12,)),
            dma((12,)),
            dma((8,)),
            dma((8,)),
            dma((8,)),
            dma((8,)),
            dma((8,)),
            dma((8,)),
        ],
        compiler_params=pltpu.CompilerParams(
            collective_id=0, has_side_effects=True, vmem_limit_bytes=60 * 1024 * 1024
        ),
        name="step",
    )(
        partner,
        radial_rate,
        positions,
        features,
        lever,
        body_slot,
        owner_dir,
        body_pose,
        body_motion,
        body_inverse,
        weight_u,
        weight_v,
    )
    moved, body_next = pl.pallas_call(
        hand_over,
        out_shape=(
            jax.ShapeDtypeStruct((8, 3, 8, 128), F32),
            jax.ShapeDtypeStruct((1, 13, 1, 128), F32),
        ),
        in_specs=[vmem, vmem],
        out_specs=(hbm, hbm),
        scratch_shapes=[dma((2,))],
        name="out",
    )(
        pltpu.with_memory_space_constraint(moved, pltpu.VMEM),
        pltpu.with_memory_space_constraint(body_next, pltpu.VMEM),
    )
    return inside(moved), inside(body_next)


def solution(mesh):
    tiles = P("gx", "gy", None, None)
    flat = P("gx", "gy", None)
    return jax.shard_map(
        local,
        mesh=mesh,
        in_specs=(tiles, tiles, tiles, flat, flat, flat, tiles, tiles, tiles, P(), P(), P()),
        out_specs=(tiles, tiles),
        check_vma=False,
    )
```
